32 devices in a mesh: block: 8 (over y, x, core), sub: 4 (over z).
Axes of the slice: x: 2, y: 2, z: 4, core: 2. Of those that a mesh axis runs over, the one named last changes fastest.
Arguments:
- source: float32 [8, 16, 128, 128], P('block', 'sub'), may hold values from -48 to 48
- trans_x: float32 [8, 16, 128, 128], P('block', 'sub'), may hold values from 0.1 to 10
- trans_y: float32 [8, 16, 128, 128], P('block', 'sub'), may hold values from 0.1 to 10
- trans_z: float32 [8, 16, 128, 128], P('block', 'sub'), may hold values from 0.1 to 10
- mortar_bot: float32 [8, 16, 128, 256], P('block', 'sub'), may hold values from -0.375 to 0.375
- mortar_top: float32 [8, 16, 128, 256], P('block', 'sub'), may hold values from -0.375 to 0.375
Outputs:
- pressure: float32 [8, 16, 128, 128], P('block', 'sub')
- mortar: float32 [8, 256], P('block', 'sub')
The draws below stay inside these ranges and needn't reach their ends.
All inputs are finite; a program needn't handle non-finite values.
Results may differ from the reference program's by a relative error of at most 0.0003.
Values sent between devices are 32-bit elements; how exact they have to be, the bound alone decides.
No kernel may reach another device: no remote copies, remote signals or barrier semaphores. Data moves between devices by JAX's collectives and lax.ppermute only.
A program may use at most 64 MiB of HBM per device.

```python
import math
import jax
import jax.numpy as jnp
from jax import lax

NY = 128
CZ = 128
M = 256
PASSES = 3
OUTER = 2
NX = 16
N_BLOCK = 8


def block_levels(rng, extent, split, low, largest):
    def one(dim, blocks):
        steps = jax.random.uniform(jax.random.fold_in(jax.random.fold_in(rng, 6), dim), (blocks,), jnp.float32, low / len(split), largest / len(split))
        return jnp.repeat(jnp.exp(steps), extent[dim] // blocks).reshape((-1,) + (1,) * (len(extent) - dim - 1))

    level = one(*split[0])
    for cut in split[1:]:
        level = level * one(*cut)
    return level


def normal_values(key, extent, spread, limit, cuts=(), held_as=jnp.bfloat16):
    entries = spread * jax.random.normal(key, extent, jnp.float32)
    if cuts:
        entries = entries * block_levels(key, extent, cuts, -0.22, 0.18)
    return jnp.clip(entries, -limit, limit).astype(held_as)


def setup_inputs(seed: int = 0) -> dict:
    seeds = jax.random.split(jax.random.key(seed), 7)
    return {
        "source": normal_values(seeds[0], (N_BLOCK, NX, NY, CZ), 8.0, 48.0, ((0, 8), (1, 4)), jnp.float32),
        "trans_x": jnp.clip(jnp.exp(math.log(10.0) - 4.6051702 * jax.random.uniform(seeds[1], (N_BLOCK, NX, NY, CZ), jnp.float32) ** block_levels(seeds[1], (N_BLOCK, NX, NY, CZ), ((0, 8), (1, 4)), -0.2, 0.2)), 0.1, 10.0),
        "trans_y": jnp.clip(jnp.exp(math.log(10.0) - 4.6051702 * jax.random.uniform(seeds[2], (N_BLOCK, NX, NY, CZ), jnp.float32) ** block_levels(seeds[2], (N_BLOCK, NX, NY, CZ), ((0, 8), (1, 4)), -0.2, 0.2)), 0.1, 10.0),
        "trans_z": jnp.clip(jnp.exp(math.log(10.0) - 4.6051702 * jax.random.uniform(seeds[3], (N_BLOCK, NX, NY, CZ), jnp.float32) ** block_levels(seeds[3], (N_BLOCK, NX, NY, CZ), ((0, 8), (1, 4)), -0.2, 0.2)), 0.1, 10.0),
        "mortar_bot": normal_values(seeds[4], (N_BLOCK, NX, NY, M), M ** -0.5, 0.375, ((0, 8), (1, 4)), jnp.float32),
        "mortar_top": normal_values(seeds[5], (N_BLOCK, NX, NY, M), M ** -0.5, 0.375, ((0, 8), (1, 4)), jnp.float32),
    }


RELAX = 0.8
MORTAR_STEP = 0.05
HIGHEST = lax.Precision.HIGHEST


def below_of(values, axis):
    widths = [(0, 0)] * values.ndim
    widths[axis] = (1, 0)
    return lax.slice_in_dim(jnp.pad(values, widths), 0, values.shape[axis], axis=axis)


def above_of(values, axis):
    widths = [(0, 0)] * values.ndim
    widths[axis] = (0, 1)
    return lax.slice_in_dim(jnp.pad(values, widths), 1, values.shape[axis] + 1, axis=axis)


def reference(source, trans_x, trans_y, trans_z, mortar_bot, mortar_top):
    shape = source.shape
    blocks = shape[0]
    index_b = lax.broadcasted_iota(jnp.int32, shape, 0)
    index_x = lax.broadcasted_iota(jnp.int32, shape, 1)
    index_y = lax.broadcasted_iota(jnp.int32, shape, 2)
    index_z = lax.broadcasted_iota(jnp.int32, shape, 3)
    coupling_x = jnp.where(index_x > 0, trans_x, 0.0)
    coupling_y = jnp.where(index_y > 0, trans_y, 0.0)
    coupling_z = jnp.where(index_z > 0, trans_z, 0.0)
    dirichlet_bot = jnp.where((index_z == 0) & (index_b > 0), trans_z, 0.0)
    dirichlet_top = jnp.where((index_z == CZ - 1) & (index_b < blocks - 1), trans_z, 0.0)
    diagonal = (coupling_x + above_of(coupling_x, 1) + coupling_y + above_of(coupling_y, 2)
                + coupling_z + above_of(coupling_z, 3) + dirichlet_bot + dirichlet_top)
    face_bot = mortar_bot.reshape(blocks, NX * NY, M)
    face_top = mortar_top.reshape(blocks, NX * NY, M)
    pressure = jnp.zeros_like(source)
    mortar = jnp.zeros((blocks, M), source.dtype)
    for outer_round in range(OUTER):
        bottom_data = jnp.einsum("sfm,sm->sf", face_bot, below_of(mortar, 0), precision=HIGHEST).reshape(blocks, NX, NY)
        top_data = jnp.einsum("sfm,sm->sf", face_top, mortar, precision=HIGHEST).reshape(blocks, NX, NY)
        rhs = source + dirichlet_bot * bottom_data[..., None] + dirichlet_top * top_data[..., None]
        for pass_round in range(PASSES):
            applied = (diagonal * pressure
                       - coupling_x * below_of(pressure, 1) - above_of(coupling_x, 1) * above_of(pressure, 1)
                       - coupling_y * below_of(pressure, 2) - above_of(coupling_y, 2) * above_of(pressure, 2)
                       - coupling_z * below_of(pressure, 3) - above_of(coupling_z, 3) * above_of(pressure, 3))
            pressure = pressure + RELAX * (rhs - applied) / diagonal
        flux_bot = dirichlet_bot[..., 0] * (pressure[..., 0] - bottom_data)
        flux_top = dirichlet_top[..., CZ - 1] * (pressure[..., CZ - 1] - top_data)
        traces_bot = jnp.einsum("sfm,sf->sm", face_bot, flux_bot.reshape(blocks, NX * NY), precision=HIGHEST)
        traces_top = jnp.einsum("sfm,sf->sm", face_top, flux_top.reshape(blocks, NX * NY), precision=HIGHEST)
        mortar = mortar + MORTAR_STEP * (traces_top + above_of(traces_bot, 0))
    return pressure, mortar
```

```python
import jax
import jax.numpy as jnp
from jax import lax
from jax.experimental import pallas as pl
from jax.experimental.pallas import tpu as pltpu
from jax.sharding import PartitionSpec as P

RELAX = 0.8
KEEP = 1.0 - RELAX
MORTAR_STEP = 0.05
F32 = jnp.float32
EDGE = 5
REST = 8
HALO = 2
VMEM = pl.BlockSpec(memory_space=pltpu.VMEM)


def prev(v, axis):
    return pltpu.roll(v, 1, axis)


def following(v, axis):
    return pltpu.roll(v, v.shape[axis] - 1, axis)


class Layer:
    def __init__(self, trans_y, trans_z, has_bot, has_top):
        rows = lax.broadcasted_iota(jnp.int32, trans_y.shape, 0)
        cols = lax.broadcasted_iota(jnp.int32, trans_y.shape, 1)
        self.first = cols == 0
        self.last = cols == trans_y.shape[1] - 1
        self.cy = jnp.where(rows > 0, trans_y, 0.0)
        self.cz = jnp.where(self.first, 0.0, trans_z)
        self.dbot = jnp.where(self.first, trans_z, 0.0) * has_bot
        self.dtop = jnp.where(self.last, trans_z, 0.0) * has_top
        self.diag = (
            self.cy
            + following(self.cy, 0)
            + self.cz
            + following(self.cz, 1)
            + self.dbot
            + self.dtop
        )

    def around(self, p):
        return (
            self.cy * prev(p, 0)
            + following(self.cy * p, 0)
            + self.cz * prev(p, 1)
            + following(self.cz * p, 1)
        )


def flags():
    block = lax.axis_index("block")
    sub = lax.axis_index("sub")
    has_bot = (block > 0).astype(F32)
    has_top = (block < lax.axis_size("block") - 1).astype(F32)
    has_below = (sub > 0).astype(F32)
    has_above = (sub < lax.axis_size("sub") - 1).astype(F32)
    return has_bot, has_top, has_below, has_above


def by_parity(axis, first, second, upward, downward):
    even = lax.rem(lax.axis_index(axis), 2) == 0

    @pl.when(even)
    def _():
        upward(first)
        downward(second)

    @pl.when(jnp.logical_not(even))
    def _():
        upward(second)
        downward(first)


def edge_kernel(src, tx, ty, tz, out_a, out_b):
    count = src.shape[1]
    has_bot, has_top, has_below, _ = flags()

    def layer(x):
        return Layer(ty[0, x], tz[0, x], has_bot, has_top)

    low = layer(0)
    w_low = RELAX / (low.diag + tx[0, 0] * has_below + tx[0, 1])
    p_low = w_low * src[0, 0]
    p_next = RELAX * src[0, 1] / (layer(1).diag + tx[0, 1] + tx[0, 2])
    q_low = KEEP * p_low + w_low * (src[0, 0] + tx[0, 1] * p_next + low.around(p_low))
    top = count - 1
    p_top = RELAX * src[0, top - 1] / (layer(top - 1).diag + tx[0, top - 1] + tx[0, top])

    def upward(ref):
        ref[0] = src[0, top]
        ref[1] = tx[0, top]
        ref[2] = ty[0, top]
        ref[3] = tz[0, top]
        ref[4] = p_top

    def downward(ref):
        ref[0] = tx[0, 0]
        ref[1] = p_low
        ref[2] = q_low
        ref[3] = w_low
        ref[4] = src[0, 0]

    by_parity("sub", out_a, out_b, upward, downward)


def rest_kernel(src, tx, ty, tz, bot, top, out_a, out_b, rows_a, rows_b):
    count = src.shape[1]

    def upward(ref):
        for i, part in enumerate((src, tx, ty, tz)):
            ref[i] = part[0, count - 2]
            ref[i + 4] = part[0, count - 2]

    def downward(ref):
        for i, part in enumerate((ty, tz)):
            ref[i] = part[0, 0]
        for i, part in enumerate((src, tx, ty, tz)):
            ref[i + 2] = part[0, 1]
        ref[6] = tx[0, 2]
        ref[7] = tx[0, 2]

    by_parity("sub", out_a, out_b, upward, downward)

    def rows_up(ref):
        ref[0:HALO] = bot[0, count - HALO : count]
        ref[HALO : 2 * HALO] = top[0, count - HALO : count]

    def rows_down(ref):
        ref[0:HALO] = bot[0, 0:HALO]
        ref[HALO : 2 * HALO] = top[0, 0:HALO]

    by_parity("sub", rows_a, rows_b, rows_up, rows_down)


def traces(flux, basis):
    return sum(
        jnp.sum(f * basis[0, x], axis=0, keepdims=True) for x, f in enumerate(flux)
    )


def place_shares(cbot, ctop, out_a, out_b):
    def upward(ref):
        ref[...] = ctop

    def downward(ref):
        ref[...] = cbot

    by_parity("block", out_a, out_b, upward, downward)


def first_kernel(src, tx, ty, tz, bot, top, got_a, got_b, p_out, halo_a, halo_b, sh_a, sh_b, above, below):
    count = src.shape[1]
    has_bot, has_top, has_below, has_above = flags()

    def take_above(ref):
        above[...] = ref[...]

    def take_below(ref):
        below[...] = ref[...]

    by_parity("sub", got_a, got_b, take_above, take_below)
    source = {x: src[0, x] for x in range(count)}
    source[-1] = below[0]
    cx = {x: tx[0, x] for x in range(1, count)}
    cx[-1] = below[1]
    cx[0] = tx[0, 0] * has_below
    cx[count] = above[0] * has_above
    layers = {x: Layer(ty[0, x], tz[0, x], has_bot, has_top) for x in range(count)}
    layers[-1] = Layer(below[2], below[3], has_bot, has_top)
    w = {x: RELAX / (layers[x].diag + cx[x] + cx[x + 1]) for x in range(-1, count)}
    p1 = {x: w[x] * source[x] for x in range(-1, count)}
    p1[-2] = below[4]
    p1[count] = above[1]

    def step(p, x):
        return KEEP * p[x] + w[x] * (
            source[x] + cx[x] * p[x - 1] + cx[x + 1] * p[x + 1] + layers[x].around(p[x])
        )

    p2 = {x: step(p1, x) for x in range(-1, count)}
    p2[count] = above[2] + above[3] * cx[count] * p1[count - 1]
    p3 = {x: step(p2, x) for x in range(count)}
    for x in range(count):
        p_out[x] = p3[x]
    width = halo_a.shape[0]

    def upward(ref):
        for i in range(width):
            ref[i] = p3[count - width + i]

    def downward(ref):
        for i in range(width):
            ref[i] = p3[i]

    by_parity("sub", halo_a, halo_b, upward, downward)
    end = src.shape[3] - 1
    flux_bot = [layers[x].dbot[:, 0:1] * p3[x][:, 0:1] for x in range(count)]
    flux_top = [layers[x].dtop[:, end:] * p3[x][:, end:] for x in range(count)]
    place_shares(traces(flux_bot, bot), traces(flux_top, top), sh_a, sh_b)


def second_kernel(
    src, tx, ty, tz, bot, top, got_a, got_b, rest_a, rest_b, rows_a, rows_b,
    p_in, halo_a, halo_b, *rest,
):
    parts = rest[:-12]
    p_out, cbot_out, ctop_out, mortar_out = rest[-12:-8]
    above, below, more_above, more_below, rows_above, rows_below, p_above, p_below = rest[-8:]
    count = src.shape[1]
    has_bot, has_top, has_below, has_above = flags()
    for pair, (up, down) in (
        ((got_a, got_b), (above, below)),
        ((rest_a, rest_b), (more_above, more_below)),
        ((rows_a, rows_b), (rows_above, rows_below)),
        ((halo_a, halo_b), (p_above, p_below)),
    ):
        def take_above(ref, to=up):
            to[...] = ref[...]

        def take_below(ref, to=down):
            to[...] = ref[...]

        by_parity("sub", *pair, take_above, take_below)

    jumps = MORTAR_STEP * sum(part[...] for part in parts)
    even = lax.rem(lax.axis_index("block"), 2) == 0
    own = jnp.where(even, jumps[0:1], jumps[1:2])
    under = jnp.where(even, jumps[1:2], jumps[0:1])
    mortar_out[...] = own

    source = {x: src[0, x] for x in range(count)}
    source[-1] = below[0]
    source[-2] = more_below[0]
    source[count] = above[4]
    source[count + 1] = more_above[2]
    cx = {x: tx[0, x] for x in range(1, count)}
    cx[-2] = more_below[1]
    cx[-1] = below[1]
    cx[0] = tx[0, 0] * has_below
    cx[count] = above[0] * has_above
    cx[count + 1] = more_above[3]
    cx[count + 2] = more_above[6]
    ty_of = {x: ty[0, x] for x in range(count)}
    tz_of = {x: tz[0, x] for x in range(count)}
    ty_of[-1], tz_of[-1] = below[2], below[3]
    ty_of[-2], tz_of[-2] = more_below[2], more_below[3]
    ty_of[count], tz_of[count] = more_above[0], more_above[1]
    ty_of[count + 1], tz_of[count + 1] = more_above[4], more_above[5]
    reach = range(-HALO, count + HALO)
    layers = {x: Layer(ty_of[x], tz_of[x], has_bot, has_top) for x in reach}
    w = {x: RELAX / (layers[x].diag + cx[x] + cx[x + 1]) for x in reach}

    def basis(ref, rows, face, x):
        if x < 0:
            return rows[1][face * HALO + x + HALO]
        if x >= count:
            return rows[0][face * HALO + x - count]
        return ref[0, x]

    halves = (rows_above, rows_below)
    gbot = {x: jnp.sum(basis(bot, halves, 0, x) * under, axis=1, keepdims=True) for x in reach}
    gtop = {x: jnp.sum(basis(top, halves, 1, x) * own, axis=1, keepdims=True) for x in reach}
    rhs = {
        x: source[x] + layers[x].dbot * gbot[x] + layers[x].dtop * gtop[x] for x in reach
    }
    width = p_above.shape[0]
    p = {x: p_in[x] for x in range(count)}
    for i in range(width):
        p[count + i] = p_above[i]
        p[i - width] = p_below[i]
    for margin in range(HALO, -1, -1):
        old = p
        p = {
            x: KEEP * old[x]
            + w[x] * (rhs[x] + cx[x] * old[x - 1] + cx[x + 1] * old[x + 1] + layers[x].around(old[x]))
            for x in range(-margin, count + margin)
        }
    for x in range(count):
        p_out[0, x] = p[x]
    end = src.shape[3] - 1
    flux_bot = [layers[x].dbot[:, 0:1] * (p[x][:, 0:1] - gbot[x]) for x in range(count)]
    flux_top = [layers[x].dtop[:, end:] * (p[x][:, end:] - gtop[x]) for x in range(count)]
    cbot_out[...] = traces(flux_bot, bot)
    ctop_out[...] = traces(flux_top, top)


def call(kernel, outs, args, scratch=()):
    return pl.pallas_call(
        kernel,
        out_shape=[jax.ShapeDtypeStruct(shape, F32) for shape in outs],
        in_specs=[VMEM] * len(args),
        out_specs=[VMEM] * len(outs),
        scratch_shapes=[pltpu.VMEM(shape, F32) for shape in scratch],
    )(*args)


def sub_swaps(blocks, subs):
    flat = lambda b, s: b * subs + s
    first = [(flat(b, s), flat(b, s ^ 1)) for b in range(blocks) for s in range(subs)]
    second = []
    for b in range(blocks):
        for s in range(subs):
            other = s + 1 if s % 2 else s - 1
            inside = 0 <= other < subs
            second.append((flat(b, s), flat(b, other) if inside else flat(b ^ 1, s)))
    return first, second


def shards(source, trans_x, trans_y, trans_z, mortar_bot, mortar_top):
    count, rows, cells = source.shape[1:]
    width = mortar_bot.shape[3]
    subs = lax.axis_size("sub")
    blocks = lax.axis_size("block")
    assert subs % 2 == 0 and blocks % 2 == 0 and count > HALO
    names = ("block", "sub")
    pair_one, pair_two = sub_swaps(blocks, subs)

    def trade(a, b):
        return lax.ppermute(a, names, pair_one), lax.ppermute(b, names, pair_two)

    coeffs = (source, trans_x, trans_y, trans_z)
    faces = (mortar_bot, mortar_top)
    face = (rows, cells)
    edges = call(edge_kernel, [(EDGE,) + face] * 2, coeffs)
    got = trade(*edges)
    moved = call(
        rest_kernel,
        [(REST,) + face] * 2 + [(2 * HALO, rows, width)] * 2,
        coeffs + faces,
    )
    more = trade(*moved[:2])
    more_rows = trade(*moved[2:])
    third, halo_a, halo_b, share_a, share_b = call(
        first_kernel,
        [(count,) + face] + [(HALO + 1,) + face] * 2 + [(1, width)] * 2,
        coeffs + faces + got,
        [(EDGE,) + face] * 2,
    )

    block_one = [(b, b ^ 1) for b in range(blocks)]
    block_two = [(b, (b + 1 if b % 2 else b - 1) % blocks) for b in range(blocks)]

    def everyone(value):
        if subs <= 4:
            swaps = range(subs - 1, 0, -1)
            return [value] + [
                lax.ppermute(value, "sub", [(i, i ^ k) for i in range(subs)]) for k in swaps
            ]
        return [lax.psum(value, "sub")]

    near_a = lax.ppermute(share_a, "block", block_one)
    near_b = lax.ppermute(share_b, "block", block_two)
    halos = trade(halo_a, halo_b)
    jumps = jnp.concatenate([share_a + near_a, share_b + near_b], axis=0)
    parts = everyone(jumps)
    pressure, cbot, ctop, mortar = call(
        second_kernel,
        [source.shape] + [(1, width)] * 3,
        coeffs + faces + got + tuple(more) + tuple(more_rows) + (third,) + halos + tuple(parts),
        [(EDGE,) + face] * 2
        + [(REST,) + face] * 2
        + [(2 * HALO, rows, width)] * 2
        + [(HALO + 1,) + face] * 2,
    )
    upper = lax.ppermute(cbot, "block", [((b + 1) % blocks, b) for b in range(blocks)])
    total = mortar + MORTAR_STEP * sum(everyone(ctop + upper))
    share = width // subs
    final = lax.dynamic_slice_in_dim(total[0], lax.axis_index("sub") * share, share, 0)
    return pressure, final[None]


def solution(mesh):
    spec = P("block", "sub", None, None)
    return jax.shard_map(
        shards,
        mesh=mesh,
        in_specs=(spec,) * 6,
        out_specs=(spec, P("block", "sub")),
        check_vma=False,
    )
```

```python
import jax
import jax.numpy as jnp
from jax import lax
from jax.experimental import pallas as pl
from jax.experimental.pallas import tpu as pltpu
from jax.sharding import PartitionSpec as P

RELAX = 0.8
KEEP = 1.0 - RELAX
MORTAR_STEP = 0.05
F32 = jnp.float32
EDGE = 5
REST = 8
HALO = 2
VMEM = pl.BlockSpec(memory_space=pltpu.VMEM)


def prev(v, axis):
    return pltpu.roll(v, 1, axis)


def following(v, axis):
    return pltpu.roll(v, v.shape[axis] - 1, axis)


class Layer:
    def __init__(self, trans_y, trans_z, has_bot, has_top):
        rows = lax.broadcasted_iota(jnp.int32, trans_y.shape, 0)
        cols = lax.broadcasted_iota(jnp.int32, trans_y.shape, 1)
        self.first = cols == 0
        self.last = cols == trans_y.shape[1] - 1
        self.cy = jnp.where(rows > 0, trans_y, 0.0)
        self.cz = jnp.where(self.first, 0.0, trans_z)
        self.dbot = jnp.where(self.first, trans_z, 0.0) * has_bot
        self.dtop = jnp.where(self.last, trans_z, 0.0) * has_top
        self.diag = (
            self.cy
            + following(self.cy, 0)
            + self.cz
            + following(self.cz, 1)
            + self.dbot
            + self.dtop
        )

    def around(self, p):
        return (
            self.cy * prev(p, 0)
            + following(self.cy * p, 0)
            + self.cz * prev(p, 1)
            + following(self.cz * p, 1)
        )


def flags():
    block = lax.axis_index("block")
    sub = lax.axis_index("sub")
    has_bot = (block > 0).astype(F32)
    has_top = (block < lax.axis_size("block") - 1).astype(F32)
    has_below = (sub > 0).astype(F32)
    has_above = (sub < lax.axis_size("sub") - 1).astype(F32)
    return has_bot, has_top, has_below, has_above


def by_parity(axis, first, second, upward, downward):
    even = lax.rem(lax.axis_index(axis), 2) == 0

    @pl.when(even)
    def _():
        upward(first)
        downward(second)

    @pl.when(jnp.logical_not(even))
    def _():
        upward(second)
        downward(first)


def edge_kernel(src, tx, ty, tz, out_a, out_b):
    count = src.shape[1]
    has_bot, has_top, has_below, _ = flags()

    def layer(x):
        return Layer(ty[0, x], tz[0, x], has_bot, has_top)

    low = layer(0)
    w_low = RELAX / (low.diag + tx[0, 0] * has_below + tx[0, 1])
    p_low = w_low * src[0, 0]
    p_next = RELAX * src[0, 1] / (layer(1).diag + tx[0, 1] + tx[0, 2])
    q_low = KEEP * p_low + w_low * (src[0, 0] + tx[0, 1] * p_next + low.around(p_low))
    top = count - 1
    p_top = RELAX * src[0, top - 1] / (layer(top - 1).diag + tx[0, top - 1] + tx[0, top])

    def upward(ref):
        ref[0] = src[0, top]
        ref[1] = tx[0, top]
        ref[2] = ty[0, top]
        ref[3] = tz[0, top]
        ref[4] = p_top

    def downward(ref):
        ref[0] = tx[0, 0]
        ref[1] = p_low
        ref[2] = q_low
        ref[3] = w_low
        ref[4] = src[0, 0]

    by_parity("sub", out_a, out_b, upward, downward)


def rest_kernel(src, tx, ty, tz, bot, top, out_a, out_b, rows_a, rows_b):
    count = src.shape[1]

    def upward(ref):
        for i, part in enumerate((src, tx, ty, tz)):
            ref[i] = part[0, count - 2]
            ref[i + 4] = part[0, count - 2]

    def downward(ref):
        for i, part in enumerate((ty, tz)):
            ref[i] = part[0, 0]
        for i, part in enumerate((src, tx, ty, tz)):
            ref[i + 2] = part[0, 1]
        ref[6] = tx[0, 2]
        ref[7] = tx[0, 2]

    by_parity("sub", out_a, out_b, upward, downward)

    def rows_up(ref):
        ref[0:HALO] = bot[0, count - HALO : count]
        ref[HALO : 2 * HALO] = top[0, count - HALO : count]

    def rows_down(ref):
        ref[0:HALO] = bot[0, 0:HALO]
        ref[HALO : 2 * HALO] = top[0, 0:HALO]

    by_parity("sub", rows_a, rows_b, rows_up, rows_down)


def traces(flux, basis):
    return sum(
        jnp.sum(f * basis[0, x], axis=0, keepdims=True) for x, f in enumerate(flux)
    )


def place_shares(cbot, ctop, out_a, out_b):
    def upward(ref):
        ref[...] = ctop

    def downward(ref):
        ref[...] = cbot

    by_parity("block", out_a, out_b, upward, downward)


def first_kernel(src, tx, ty, tz, bot, top, got_a, got_b, p_out, halo_a, halo_b, sh_a, sh_b, above, below):
    count = src.shape[1]
    has_bot, has_top, has_below, has_above = flags()

    def take_above(ref):
        above[...] = ref[...]

    def take_below(ref):
        below[...] = ref[...]

    by_parity("sub", got_a, got_b, take_above, take_below)
    source = {x: src[0, x] for x in range(count)}
    source[-1] = below[0]
    cx = {x: tx[0, x] for x in range(1, count)}
    cx[-1] = below[1]
    cx[0] = tx[0, 0] * has_below
    cx[count] = above[0] * has_above
    layers = {x: Layer(ty[0, x], tz[0, x], has_bot, has_top) for x in range(count)}
    layers[-1] = Layer(below[2], below[3], has_bot, has_top)
    w = {x: RELAX / (layers[x].diag + cx[x] + cx[x + 1]) for x in range(-1, count)}
    p1 = {x: w[x] * source[x] for x in range(-1, count)}
    p1[-2] = below[4]
    p1[count] = above[1]

    def step(p, x):
        return KEEP * p[x] + w[x] * (
            source[x] + cx[x] * p[x - 1] + cx[x + 1] * p[x + 1] + layers[x].around(p[x])
        )

    p2 = {x: step(p1, x) for x in range(-1, count)}
    p2[count] = above[2] + above[3] * cx[count] * p1[count - 1]
    p3 = {x: step(p2, x) for x in range(count)}
    for x in range(count):
        p_out[x] = p3[x]
    width = halo_a.shape[0]

    def upward(ref):
        for i in range(width):
            ref[i] = p3[count - width + i]

    def downward(ref):
        for i in range(width):
            ref[i] = p3[i]

    by_parity("sub", halo_a, halo_b, upward, downward)
    end = src.shape[3] - 1
    flux_bot = [layers[x].dbot[:, 0:1] * p3[x][:, 0:1] for x in range(count)]
    flux_top = [layers[x].dtop[:, end:] * p3[x][:, end:] for x in range(count)]
    place_shares(traces(flux_bot, bot), traces(flux_top, top), sh_a, sh_b)


def second_kernel(
    src, tx, ty, tz, bot, top, got_a, got_b, rest_a, rest_b, rows_a, rows_b,
    p_in, halo_a, halo_b, *rest,
):
    parts = rest[:-12]
    p_out, cbot_out, ctop_out, mortar_out = rest[-12:-8]
    above, below, more_above, more_below, rows_above, rows_below, p_above, p_below = rest[-8:]
    count = src.shape[1]
    has_bot, has_top, has_below, has_above = flags()
    for pair, (up, down) in (
        ((got_a, got_b), (above, below)),
        ((rest_a, rest_b), (more_above, more_below)),
        ((rows_a, rows_b), (rows_above, rows_below)),
        ((halo_a, halo_b), (p_above, p_below)),
    ):
        def take_above(ref, to=up):
            to[...] = ref[...]

        def take_below(ref, to=down):
            to[...] = ref[...]

        by_parity("sub", *pair, take_above, take_below)

    jumps = MORTAR_STEP * sum(part[...] for part in parts)
    even = lax.rem(lax.axis_index("block"), 2) == 0
    own = jnp.where(even, jumps[0:1], jumps[1:2])
    under = jnp.where(even, jumps[1:2], jumps[0:1])
    mortar_out[...] = own

    source = {x: src[0, x] for x in range(count)}
    source[-1] = below[0]
    source[-2] = more_below[0]
    source[count] = above[4]
    source[count + 1] = more_above[2]
    cx = {x: tx[0, x] for x in range(1, count)}
    cx[-2] = more_below[1]
    cx[-1] = below[1]
    cx[0] = tx[0, 0] * has_below
    cx[count] = above[0] * has_above
    cx[count + 1] = more_above[3]
    cx[count + 2] = more_above[6]
    ty_of = {x: ty[0, x] for x in range(count)}
    tz_of = {x: tz[0, x] for x in range(count)}
    ty_of[-1], tz_of[-1] = below[2], below[3]
    ty_of[-2], tz_of[-2] = more_below[2], more_below[3]
    ty_of[count], tz_of[count] = more_above[0], more_above[1]
    ty_of[count + 1], tz_of[count + 1] = more_above[4], more_above[5]
    reach = range(-HALO, count + HALO)
    layers = {x: Layer(ty_of[x], tz_of[x], has_bot, has_top) for x in reach}
    w = {x: RELAX / (layers[x].diag + cx[x] + cx[x + 1]) for x in reach}

    def basis(ref, rows, face, x):
        if x < 0:
            return rows[1][face * HALO + x + HALO]
        if x >= count:
            return rows[0][face * HALO + x - count]
        return ref[0, x]

    halves = (rows_above, rows_below)
    gbot = {x: jnp.sum(basis(bot, halves, 0, x) * under, axis=1, keepdims=True) for x in reach}
    gtop = {x: jnp.sum(basis(top, halves, 1, x) * own, axis=1, keepdims=True) for x in reach}
    rhs = {
        x: source[x] + layers[x].dbot * gbot[x] + layers[x].dtop * gtop[x] for x in reach
    }
    width = p_above.shape[0]
    p = {x: p_in[x] for x in range(count)}
    for i in range(width):
        p[count + i] = p_above[i]
        p[i - width] = p_below[i]
    for margin in range(HALO, -1, -1):
        old = p
        p = {
            x: KEEP * old[x]
            + w[x] * (rhs[x] + cx[x] * old[x - 1] + cx[x + 1] * old[x + 1] + layers[x].around(old[x]))
            for x in range(-margin, count + margin)
        }
    for x in range(count):
        p_out[0, x] = p[x]
    end = src.shape[3] - 1
    flux_bot = [layers[x].dbot[:, 0:1] * (p[x][:, 0:1] - gbot[x]) for x in range(count)]
    flux_top = [layers[x].dtop[:, end:] * (p[x][:, end:] - gtop[x]) for x in range(count)]
    cbot_out[...] = traces(flux_bot, bot)
    ctop_out[...] = traces(flux_top, top)


def call(kernel, outs, args, scratch=()):
    args = [pltpu.with_memory_space_constraint(a, pltpu.VMEM) for a in args]
    return pl.pallas_call(
        kernel,
        out_shape=[pltpu.VMEM(shape, F32) for shape in outs],
        in_specs=[VMEM] * len(args),
        out_specs=[VMEM] * len(outs),
        scratch_shapes=[pltpu.VMEM(shape, F32) for shape in scratch],
        compiler_params=pltpu.CompilerParams(vmem_limit_bytes=16 << 20),
    )(*args)


def sub_swaps(blocks, subs):
    flat = lambda b, s: b * subs + s
    first = [(flat(b, s), flat(b, s ^ 1)) for b in range(blocks) for s in range(subs)]
    second = []
    for b in range(blocks):
        for s in range(subs):
            other = s + 1 if s % 2 else s - 1
            inside = 0 <= other < subs
            second.append((flat(b, s), flat(b, other) if inside else flat(b ^ 1, s)))
    return first, second


def shards(source, trans_x, trans_y, trans_z, mortar_bot, mortar_top):
    count, rows, cells = source.shape[1:]
    width = mortar_bot.shape[3]
    subs = lax.axis_size("sub")
    blocks = lax.axis_size("block")
    assert subs % 2 == 0 and blocks % 2 == 0 and count > HALO
    names = ("block", "sub")
    pair_one, pair_two = sub_swaps(blocks, subs)

    def trade(a, b):
        return lax.ppermute(a, names, pair_one), lax.ppermute(b, names, pair_two)

    coeffs = (source, trans_x, trans_y, trans_z)
    faces = (mortar_bot, mortar_top)
    face = (rows, cells)
    edges = call(edge_kernel, [(EDGE,) + face] * 2, coeffs)
    got = trade(*edges)
    moved = call(
        rest_kernel,
        [(REST,) + face] * 2 + [(2 * HALO, rows, width)] * 2,
        coeffs + faces,
    )
    more = trade(*moved[:2])
    more_rows = trade(*moved[2:])
    third, halo_a, halo_b, share_a, share_b = call(
        first_kernel,
        [(count,) + face] + [(HALO + 1,) + face] * 2 + [(1, width)] * 2,
        coeffs + faces + got,
        [(EDGE,) + face] * 2,
    )

    block_one = [(b, b ^ 1) for b in range(blocks)]
    block_two = [(b, (b + 1 if b % 2 else b - 1) % blocks) for b in range(blocks)]

    def everyone(value):
        if subs <= 4:
            swaps = range(subs - 1, 0, -1)
            return [value] + [
                lax.ppermute(value, "sub", [(i, i ^ k) for i in range(subs)]) for k in swaps
            ]
        return [lax.psum(value, "sub")]

    near_a = lax.ppermute(share_a, "block", block_one)
    near_b = lax.ppermute(share_b, "block", block_two)
    halos = trade(halo_a, halo_b)
    jumps = jnp.concatenate([share_a + near_a, share_b + near_b], axis=0)
    parts = everyone(jumps)
    pressure, cbot, ctop, mortar = call(
        second_kernel,
        [source.shape] + [(1, width)] * 3,
        coeffs + faces + got + tuple(more) + tuple(more_rows) + (third,) + halos + tuple(parts),
        [(EDGE,) + face] * 2
        + [(REST,) + face] * 2
        + [(2 * HALO, rows, width)] * 2
        + [(HALO + 1,) + face] * 2,
    )
    upper = lax.ppermute(cbot, "block", [((b + 1) % blocks, b) for b in range(blocks)])
    total = mortar + MORTAR_STEP * sum(everyone(ctop + upper))
    share = width // subs
    final = lax.dynamic_slice_in_dim(total[0], lax.axis_index("sub") * share, share, 0)
    return pressure, final[None]


def solution(mesh):
    spec = P("block", "sub", None, None)
    return jax.shard_map(
        shards,
        mesh=mesh,
        in_specs=(spec,) * 6,
        out_specs=(spec, P("block", "sub")),
        check_vma=False,
    )
```

```python
import jax
import jax.numpy as jnp
from jax import lax
from jax.experimental import pallas as pl
from jax.experimental.pallas import tpu as pltpu
from jax.sharding import PartitionSpec as P

PASSES = 3
RELAX = 0.8
KEEP = 1.0 - RELAX
MORTAR_STEP = 0.05
F32 = jnp.float32
EDGE = 6
MIDDLE = 3
HALO = 2
SLAB = 8
SPAN = 2 * SLAB
ITEMS = 5


def prev(v, axis):
    return pltpu.roll(v, 1, axis)


def following(v, axis):
    return pltpu.roll(v, v.shape[axis] - 1, axis)


class Layer:
    def __init__(self, trans_y, trans_z, has_bot, has_top):
        rows = lax.broadcasted_iota(jnp.int32, trans_y.shape, 0)
        self.cy = jnp.where(rows > 0, trans_y, 0.0)
        self.cz, self.zsum = along_z(trans_z, has_bot, has_top)
        self.diag = self.cy + following(self.cy, 0) + self.zsum

    def around(self, p):
        return (
            self.cy * prev(p, 0)
            + following(self.cy * p, 0)
            + self.cz * prev(p, 1)
            + following(self.cz * p, 1)
        )


def along_z(trans_z, has_bot, has_top):
    cols = lax.broadcasted_iota(jnp.int32, trans_z.shape, 1)
    first = cols == 0
    last = cols == trans_z.shape[1] - 1
    cz = jnp.where(first, 0.0, trans_z)
    ends = jnp.where(first, trans_z * has_bot, jnp.where(last, trans_z * has_top, 0.0))
    return cz, cz + following(cz, 1) + ends


class Thin:
    def __init__(self, trans_y, trans_z, zsum, has_bot, has_top):
        rows = lax.broadcasted_iota(jnp.int32, trans_y.shape, 0)
        cols = lax.broadcasted_iota(jnp.int32, trans_y.shape, 1)
        self.cy = jnp.where(cols > 0, trans_y, 0.0)
        self.cz = jnp.where(rows == SLAB, 0.0, trans_z)
        self.dbot = jnp.where(rows == SLAB, trans_z, 0.0) * has_bot
        self.dtop = jnp.where(rows == SLAB - 1, trans_z, 0.0) * has_top
        self.diag = self.cy + following(self.cy, 1) + zsum

    def around(self, p):
        return (
            self.cy * prev(p, 1)
            + following(self.cy * p, 1)
            + self.cz * prev(p, 0)
            + following(self.cz * p, 0)
        )


def flags():
    block = lax.axis_index("block")
    sub = lax.axis_index("sub")
    has_bot = (block > 0).astype(F32)
    has_top = (block < lax.axis_size("block") - 1).astype(F32)
    has_below = (sub > 0).astype(F32)
    has_above = (sub < lax.axis_size("sub") - 1).astype(F32)
    return has_bot, has_top, has_below, has_above


def by_parity(axis, first, second, upward, downward):
    even = lax.rem(lax.axis_index(axis), 2) == 0

    @pl.when(even)
    def _():
        upward(first)
        downward(second)

    @pl.when(jnp.logical_not(even))
    def _():
        upward(second)
        downward(first)


def sort_pair(pair, above, below):
    def take_above(ref):
        above[...] = ref[...]

    def take_below(ref):
        below[...] = ref[...]

    by_parity("sub", *pair, take_above, take_below)


def pack_kernel(src, tx, ty, tz, src_v, tx_v, ty_v, tz_v, slabs, out_a, out_b, sems):
    copies = [
        pltpu.make_async_copy(here, there, sems.at[i])
        for i, (here, there) in enumerate(
            ((tz, tz_v), (src, src_v), (tx, tx_v), (ty, ty_v))
        )
    ]
    for copy in copies:
        copy.start()
    for copy in copies:
        copy.wait()
    count, rows, cells = src_v.shape[1:]
    has_bot, has_top, _, _ = flags()
    items = []
    for x in range(count):
        zsum = along_z(tz_v[0, x], has_bot, has_top)[1]
        items += [tx_v[0, x], src_v[0, x], ty_v[0, x], tz_v[0, x], zsum]
    slot = lax.broadcasted_iota(jnp.int32, (rows, cells), 1) // SPAN
    each = cells // SPAN
    for start in range(0, len(items), each):
        packed = jnp.zeros((rows, cells), F32)
        for j, item in enumerate(items[start : start + each]):
            turned = pltpu.roll(item, (SPAN * j + SLAB) % cells, 1)
            packed = jnp.where(slot == j, turned, packed)
        slabs[start * SPAN : (start + each) * SPAN] = packed.T
    length = out_a.shape[0]
    last = count * ITEMS * SPAN

    def upward(ref):
        ref[0 : HALO * ITEMS * SPAN] = slabs[last - HALO * ITEMS * SPAN : last]
        ref[HALO * ITEMS * SPAN :] = slabs[0:SPAN]

    def downward(ref):
        ref[...] = slabs[0:length]

    by_parity("sub", out_a, out_b, upward, downward)


def rows_kernel(bot, top, bot_v, top_v, rows_a, rows_b, sems):
    count = bot.shape[1]
    whole = [
        pltpu.make_async_copy(bot, bot_v, sems.at[0]),
        pltpu.make_async_copy(top, top_v, sems.at[1]),
    ]
    for copy in whole:
        copy.start()
    for copy in whole:
        copy.wait()

    def rows_up(ref):
        ref[0:HALO] = bot_v[0, count - HALO : count]
        ref[HALO : 2 * HALO] = top_v[0, count - HALO : count]

    def rows_down(ref):
        ref[0:HALO] = bot_v[0, 0:HALO]
        ref[HALO : 2 * HALO] = top_v[0, 0:HALO]

    by_parity("sub", rows_a, rows_b, rows_up, rows_down)


def thin_round(slabs, above, below, reach, count):
    has_bot, has_top, has_below, has_above = flags()

    def item(x, which):
        if x < 0:
            start = ((x + HALO) * ITEMS + which) * SPAN
            return below[start : start + SPAN]
        if x >= count:
            start = ((x - count) * ITEMS + which) * SPAN
            return above[start : start + SPAN]
        start = (x * ITEMS + which) * SPAN
        return slabs[start : start + SPAN]

    cx = {x: item(x, 0) for x in range(-reach, count + reach + 1)}
    cx[0] = cx[0] * has_below
    cx[count] = cx[count] * has_above
    span = range(-reach, count + reach)
    source = {x: item(x, 1) for x in span}
    layers = {x: Thin(item(x, 2), item(x, 3), item(x, 4), has_bot, has_top) for x in span}
    weight = {x: RELAX / (layers[x].diag + cx[x] + cx[x + 1]) for x in span}
    return source, cx, layers, weight


def thin_pass(p, rhs, cx, layers, weight, low, high):
    return {
        x: KEEP * p[x]
        + weight[x] * (rhs[x] + cx[x] * p[x - 1] + cx[x + 1] * p[x + 1] + layers[x].around(p[x]))
        for x in range(low, high)
    }


def traces(flux_bot, flux_top, bot, top, rows):
    count = len(flux_bot)
    stacked = jnp.concatenate(flux_bot + flux_top, axis=0)
    fill = jnp.zeros((rows - stacked.shape[0], stacked.shape[1]), F32)
    columns = jnp.concatenate([stacked, fill], axis=0).T
    return [
        sum(
            jnp.sum(columns[:, face * count + x : face * count + x + 1] * basis[0, x], axis=0, keepdims=True)
            for x in range(count)
        )
        for face, basis in enumerate((bot, top))
    ]


def first_thin(slabs, bot, top, got_a, got_b, p_out, halo_a, halo_b, sh_a, sh_b, above, below):
    count, rows = bot.shape[1:3]
    sort_pair((got_a, got_b), above, below)
    source, cx, layers, weight = thin_round(slabs, above, below, HALO, count)
    p = {x: weight[x] * source[x] for x in range(-HALO, count + HALO)}
    for margin in range(HALO - 1, -1, -1):
        p = thin_pass(p, source, cx, layers, weight, -margin, count + margin)
    for x in range(count):
        p_out[x] = p[x]
    width = halo_a.shape[0]

    def upward(ref):
        for i in range(width):
            ref[i] = p[count - width + i]

    def downward(ref):
        for i in range(width):
            ref[i] = p[i]

    by_parity("sub", halo_a, halo_b, upward, downward)
    flux_bot = [(layers[x].dbot * p[x])[SLAB : SLAB + 1] for x in range(count)]
    flux_top = [(layers[x].dtop * p[x])[SLAB - 1 : SLAB] for x in range(count)]
    cbot, ctop = traces(flux_bot, flux_top, bot, top, rows)

    def to_above(ref):
        ref[...] = ctop

    def to_below(ref):
        ref[...] = cbot

    by_parity("block", sh_a, sh_b, to_above, to_below)


def second_thin(slabs, bot, top, got_a, got_b, rows_a, rows_b, p_in, halo_a, halo_b, *rest):
    parts = rest[:-10]
    p_out, cbot_out, ctop_out, mortar_out = rest[-10:-6]
    above, below, rows_above, rows_below, p_above, p_below = rest[-6:]
    count, rows = bot.shape[1:3]
    sort_pair((got_a, got_b), above, below)
    sort_pair((rows_a, rows_b), rows_above, rows_below)
    sort_pair((halo_a, halo_b), p_above, p_below)
    jumps = MORTAR_STEP * sum(part[...] for part in parts)
    even = lax.rem(lax.axis_index("block"), 2) == 0
    own = jnp.where(even, jumps[0:1], jumps[1:2])
    under = jnp.where(even, jumps[1:2], jumps[0:1])
    mortar_out[...] = own

    def basis(ref, face, x):
        if x < 0:
            return rows_below[face * HALO + x + HALO]
        if x >= count:
            return rows_above[face * HALO + x - count]
        return ref[0, x]

    span = range(-HALO, count + HALO)
    lanes = lax.broadcasted_iota(jnp.int32, (rows, rows), 1)
    columns = jnp.zeros((rows, rows), F32)
    for face, (ref, values) in enumerate(((bot, under), (top, own))):
        for i, x in enumerate(span):
            data = jnp.sum(basis(ref, face, x) * values, axis=1, keepdims=True)
            columns = jnp.where(lanes == face * len(span) + i, data, columns)
    data = columns.T
    gbot = {x: data[i : i + 1] for i, x in enumerate(span)}
    gtop = {x: data[len(span) + i : len(span) + i + 1] for i, x in enumerate(span)}

    source, cx, layers, weight = thin_round(slabs, above, below, HALO, count)
    rhs = {x: source[x] + layers[x].dbot * gbot[x] + layers[x].dtop * gtop[x] for x in span}
    width = p_above.shape[0]
    p = {x: p_in[x] for x in range(count)}
    for i in range(width):
        p[count + i] = p_above[i]
        p[i - width] = p_below[i]
    for margin in range(HALO, -1, -1):
        p = thin_pass(p, rhs, cx, layers, weight, -margin, count + margin)
    for x in range(count):
        p_out[x * SPAN : (x + 1) * SPAN] = p[x]
    flux_bot = [(layers[x].dbot * (p[x] - gbot[x]))[SLAB : SLAB + 1] for x in range(count)]
    flux_top = [(layers[x].dtop * (p[x] - gtop[x]))[SLAB - 1 : SLAB] for x in range(count)]
    cbot_out[...], ctop_out[...] = traces(flux_bot, flux_top, bot, top, rows)


def edge_kernel(src, tx, ty, tz, after, out_a, out_b):
    count = src.shape[1]
    has_bot, has_top, has_below, _ = flags()

    def layer(x):
        return Layer(ty[0, x], tz[0, x], has_bot, has_top)

    low = layer(0)
    w_low = RELAX / (low.diag + tx[0, 0] * has_below + tx[0, 1])
    p_low = w_low * src[0, 0]
    p_next = RELAX * src[0, 1] / (layer(1).diag + tx[0, 1] + tx[0, 2])
    q_low = KEEP * p_low + w_low * (src[0, 0] + tx[0, 1] * p_next + low.around(p_low))
    top = count - 1
    p_top = RELAX * src[0, top - 1] / (layer(top - 1).diag + tx[0, top - 1] + tx[0, top])

    def upward(ref):
        for i, v in enumerate((tx[0, top], p_top, src[0, top], src[0, top], ty[0, top], tz[0, top])):
            ref[i] = v

    def downward(ref):
        for i, v in enumerate((tx[0, 0], p_low, q_low, w_low, ty[0, 0], tz[0, 0])):
            ref[i] = v

    by_parity("sub", out_a, out_b, upward, downward)


def whole_setup(src, tx, ty, tz, above, below):
    count = src.shape[1]
    has_bot, has_top, has_below, has_above = flags()
    cx = {x: tx[0, x] for x in range(1, count)}
    cx[-1] = below[0]
    cx[0] = tx[0, 0] * has_below
    cx[count] = above[0] * has_above
    source = {x: src[0, x] for x in range(count)}
    source[-1] = below[2]
    layers = {x: Layer(ty[0, x], tz[0, x], has_bot, has_top) for x in range(count)}
    layers[-1] = Layer(below[4], below[5], has_bot, has_top)
    weight = {x: RELAX / (layers[x].diag + cx[x] + cx[x + 1]) for x in range(-1, count)}
    return source, cx, layers, weight


def first_whole(src, tx, ty, tz, got_a, got_b, after, p_out, mid_a, mid_b, above, below):
    count = src.shape[1]
    sort_pair((got_a, got_b), above, below)
    source, cx, layers, w = whole_setup(src, tx, ty, tz, above, below)
    p1 = {x: w[x] * source[x] for x in range(-1, count)}
    p1[-2] = below[1]
    p1[count] = above[1]
    p2 = thin_pass(p1, source, cx, layers, w, -1, count)
    p2[count] = above[2] + above[3] * cx[count] * p1[count - 1]
    p3 = thin_pass(p2, source, cx, layers, w, 0, count)
    for x in range(count):
        p_out[x] = p3[x]
    top = count - 1

    def send(ref, x, link, beyond):
        ref[0] = p3[x]
        ref[1] = KEEP * p3[x] + w[x] * (source[x] + link * p3[beyond] + layers[x].around(p3[x]))
        step = thin_pass(p3, source, cx, layers, w, beyond, beyond + 1)
        ref[2] = source[x] + link * step[beyond]

    by_parity(
        "sub",
        mid_a,
        mid_b,
        lambda ref: send(ref, top, cx[top], top - 1),
        lambda ref: send(ref, 0, cx[1], 1),
    )


def second_whole(src, tx, ty, tz, got_a, got_b, p_in, mid_a, mid_b, thin, p_out, above, below, p_above, p_below):
    count, rows, cells = src.shape[1:]
    sort_pair((got_a, got_b), above, below)
    sort_pair((mid_a, mid_b), p_above, p_below)
    source, cx, layers, w = whole_setup(src, tx, ty, tz, above, below)
    has_bot, has_top, _, _ = flags()
    layers[count] = Layer(above[4], above[5], has_bot, has_top)
    w[count] = above[3]
    p3 = {x: p_in[x] for x in range(count)}
    p3[count], p3[-1] = p_above[0], p_below[0]
    p4 = thin_pass(p3, source, cx, layers, w, 0, count)
    p4[count] = p_above[1] + w[count] * cx[count] * p3[count - 1]
    p4[-1] = p_below[1] + w[-1] * cx[0] * p3[0]
    p5 = thin_pass(p4, source, cx, layers, w, 0, count)
    for x, link, near, got in ((count, cx[count], count - 1, p_above), (-1, cx[0], 0, p_below)):
        p5[x] = KEEP * p4[x] + w[x] * (got[2] + link * p4[near] + layers[x].around(p4[x]))
    p6 = thin_pass(p5, source, cx, layers, w, 0, count)
    cols = lax.broadcasted_iota(jnp.int32, (rows, cells), 1)
    face = (cols < PASSES) | (cols >= cells - PASSES)
    each = cells // SPAN
    for start in range(0, count, each):
        here = thin[start * SPAN : (start + each) * SPAN]
        if here.shape[0] < cells:
            here = jnp.concatenate([here, jnp.zeros((cells - here.shape[0], rows), F32)], axis=0)
        back = here.T
        for x in range(start, min(start + each, count)):
            shift = (cells - (x - start) * SPAN - SLAB) % cells
            p_out[0, x] = jnp.where(face, pltpu.roll(back, shift, 1), p6[x])


def call(kernel, outs, args, scratch=(), copies=0):
    space = pltpu.HBM if copies else pltpu.VMEM
    args = [pltpu.with_memory_space_constraint(a, space) for a in args]
    return pl.pallas_call(
        kernel,
        out_shape=[pltpu.VMEM(shape, F32) for shape in outs],
        in_specs=[pl.BlockSpec(memory_space=space)] * len(args),
        out_specs=[pl.BlockSpec(memory_space=pltpu.VMEM)] * len(outs),
        scratch_shapes=[pltpu.VMEM(shape, F32) for shape in scratch]
        + ([pltpu.SemaphoreType.DMA((copies,))] if copies else []),
        compiler_params=pltpu.CompilerParams(vmem_limit_bytes=16 << 20),
    )(*args)


def sub_swaps(blocks, subs):
    flat = lambda b, s: b * subs + s
    first = [(flat(b, s), flat(b, s ^ 1)) for b in range(blocks) for s in range(subs)]
    second = []
    for b in range(blocks):
        for s in range(subs):
            other = s + 1 if s % 2 else s - 1
            inside = 0 <= other < subs
            second.append((flat(b, s), flat(b, other) if inside else flat(b ^ 1, s)))
    return first, second


def shards(source, trans_x, trans_y, trans_z, mortar_bot, mortar_top):
    count, rows, cells = source.shape[1:]
    width = mortar_bot.shape[3]
    subs = lax.axis_size("sub")
    blocks = lax.axis_size("block")
    assert subs % 2 == 0 and blocks % 2 == 0 and count > HALO
    names = ("block", "sub")
    pair_one, pair_two = sub_swaps(blocks, subs)

    def trade(a, b):
        return lax.ppermute(a, names, pair_one), lax.ppermute(b, names, pair_two)

    face = (rows, cells)
    each = cells // SPAN
    slab_rows = -(-count * ITEMS // each) * cells
    sent = (HALO * ITEMS + 1) * SPAN
    *coeffs, slabs, near_a, near_b = call(
        pack_kernel,
        [source.shape] * 4 + [(slab_rows, rows)] + [(sent, rows)] * 2,
        (source, trans_x, trans_y, trans_z),
        copies=4,
    )
    near = trade(near_a, near_b)
    bot, top, rows_a, rows_b = call(
        rows_kernel,
        [mortar_bot.shape] * 2 + [(2 * HALO, rows, width)] * 2,
        (mortar_bot, mortar_top),
        copies=2,
    )
    near_rows = trade(rows_a, rows_b)
    slab = (SPAN, rows)
    third, halo_a, halo_b, share_a, share_b = call(
        first_thin,
        [(count,) + slab] + [(HALO + 1,) + slab] * 2 + [(1, width)] * 2,
        (slabs, bot, top) + near,
        [(sent, rows)] * 2,
    )

    block_one = [(b, b ^ 1) for b in range(blocks)]
    block_two = [(b, (b + 1 if b % 2 else b - 1) % blocks) for b in range(blocks)]

    def everyone(value):
        if subs <= 4:
            swaps = range(subs - 1, 0, -1)
            return [value] + [
                lax.ppermute(value, "sub", [(i, i ^ k) for i in range(subs)]) for k in swaps
            ]
        return [lax.psum(value, "sub")]

    other_a = lax.ppermute(share_a, "block", block_one)
    other_b = lax.ppermute(share_b, "block", block_two)
    halos = trade(halo_a, halo_b)
    jumps = jnp.concatenate([share_a + other_a, share_b + other_b], axis=0)
    parts = everyone(jumps)
    edges = trade(*call(edge_kernel, [(EDGE,) + face] * 2, tuple(coeffs) + (jumps,)))
    slab_out, cbot, ctop, mortar = call(
        second_thin,
        [(each * SPAN, rows)] + [(1, width)] * 3,
        (slabs, bot, top) + near + near_rows + (third,) + halos + tuple(parts),
        [(sent, rows)] * 2 + [(2 * HALO, rows, width)] * 2 + [(HALO + 1,) + slab] * 2,
    )
    upper = lax.ppermute(cbot, "block", [((b + 1) % blocks, b) for b in range(blocks)])
    jump = ctop + upper
    total = mortar + MORTAR_STEP * sum(everyone(jump))
    share = width // subs
    final = lax.dynamic_slice_in_dim(total[0], lax.axis_index("sub") * share, share, 0)

    whole, mid_a, mid_b = call(
        first_whole,
        [(count,) + face] + [(MIDDLE,) + face] * 2,
        tuple(coeffs) + edges + (jump,),
        [(EDGE,) + face] * 2,
    )
    middle = trade(mid_a, mid_b)
    (pressure,) = call(
        second_whole,
        [source.shape],
        tuple(coeffs) + edges + (whole,) + middle + (slab_out,),
        [(EDGE,) + face] * 2 + [(MIDDLE,) + face] * 2,
    )
    return pressure, final[None]


def solution(mesh):
    spec = P("block", "sub", None, None)
    return jax.shard_map(
        shards,
        mesh=mesh,
        in_specs=(spec,) * 6,
        out_specs=(spec, P("block", "sub")),
        check_vma=False,
    )
```

```python
import jax
import jax.numpy as jnp
from jax import lax
from jax.experimental import pallas as pl
from jax.experimental.pallas import tpu as pltpu
from jax.sharding import PartitionSpec as P


PASSES = 3
RELAX = 0.8
KEEP = 1.0 - RELAX
MORTAR_STEP = 0.05
F32 = jnp.float32
EDGE = 6
MIDDLE = 3
HALO = 2
SLAB = 8
SPAN = 2 * SLAB
DIRECT = 4
ITEMS = 5


def prev(v, axis):
    return pltpu.roll(v, 1, axis)


def following(v, axis):
    return pltpu.roll(v, v.shape[axis] - 1, axis)


class Layer:
    def __init__(self, trans_y, trans_z, has_bot, has_top):
        rows = lax.broadcasted_iota(jnp.int32, trans_y.shape, 0)
        self.cy = jnp.where(rows > 0, trans_y, 0.0)
        self.cz, self.zsum = along_z(trans_z, has_bot, has_top)
        self.diag = self.cy + following(self.cy, 0) + self.zsum

    def around(self, p):
        return (
            self.cy * prev(p, 0)
            + following(self.cy * p, 0)
            + self.cz * prev(p, 1)
            + following(self.cz * p, 1)
        )


def along_z(trans_z, has_bot, has_top):
    cols = lax.broadcasted_iota(jnp.int32, trans_z.shape, 1)
    first = cols == 0
    last = cols == trans_z.shape[1] - 1
    cz = jnp.where(first, 0.0, trans_z)
    ends = jnp.where(first, trans_z * has_bot, jnp.where(last, trans_z * has_top, 0.0))
    return cz, cz + following(cz, 1) + ends


class Thin:
    def __init__(self, trans_y, trans_z, zsum, has_bot, has_top):
        rows = lax.broadcasted_iota(jnp.int32, trans_y.shape, 0)
        cols = lax.broadcasted_iota(jnp.int32, trans_y.shape, 1)
        self.cy = jnp.where(cols > 0, trans_y, 0.0)
        self.cz = jnp.where(rows == SLAB, 0.0, trans_z)
        self.dbot = jnp.where(rows == SLAB, trans_z, 0.0) * has_bot
        self.dtop = jnp.where(rows == SLAB - 1, trans_z, 0.0) * has_top
        self.diag = self.cy + following(self.cy, 1) + zsum

    def around(self, p):
        return (
            self.cy * prev(p, 1)
            + following(self.cy * p, 1)
            + self.cz * prev(p, 0)
            + following(self.cz * p, 0)
        )


def flags():
    block = lax.axis_index("block")
    sub = lax.axis_index("sub")
    has_bot = (block > 0).astype(F32)
    has_top = (block < lax.axis_size("block") - 1).astype(F32)
    has_below = (sub > 0).astype(F32)
    has_above = (sub < lax.axis_size("sub") - 1).astype(F32)
    return has_bot, has_top, has_below, has_above


def by_parity(axis, first, second, upward, downward):
    even = lax.rem(lax.axis_index(axis), 2) == 0

    @pl.when(even)
    def _():
        upward(first)
        downward(second)

    @pl.when(jnp.logical_not(even))
    def _():
        upward(second)
        downward(first)


def sort_pair(pair, above, below):
    def take_above(ref):
        above[...] = ref[...]

    def take_below(ref):
        below[...] = ref[...]

    by_parity("sub", *pair, take_above, take_below)


def pack_kernel(src, tx, ty, tz, src_v, tx_v, ty_v, tz_v, slabs, out_a, out_b, sems):
    copies = [
        pltpu.make_async_copy(here, there, sems.at[i])
        for i, (here, there) in enumerate(
            ((tz, tz_v), (src, src_v), (tx, tx_v), (ty, ty_v))
        )
    ]
    for copy in copies:
        copy.start()
    for copy in copies:
        copy.wait()
    count, rows, cells = src_v.shape[1:]
    has_bot, has_top, _, _ = flags()
    items = []
    for x in range(count):
        zsum = along_z(tz_v[0, x], has_bot, has_top)[1]
        items += [tx_v[0, x], src_v[0, x], ty_v[0, x], tz_v[0, x], zsum]
    slot = lax.broadcasted_iota(jnp.int32, (rows, cells), 1) // SPAN
    each = cells // SPAN
    for start in range(0, len(items), each):
        packed = jnp.zeros((rows, cells), F32)
        for j, item in enumerate(items[start : start + each]):
            turned = pltpu.roll(item, (SPAN * j + SLAB) % cells, 1)
            packed = jnp.where(slot == j, turned, packed)
        slabs[start * SPAN : (start + each) * SPAN] = packed.T
    length = out_a.shape[0]
    last = count * ITEMS * SPAN

    def upward(ref):
        ref[0 : HALO * ITEMS * SPAN] = slabs[last - HALO * ITEMS * SPAN : last]
        ref[HALO * ITEMS * SPAN :] = slabs[0:SPAN]

    def downward(ref):
        ref[...] = slabs[0:length]

    by_parity("sub", out_a, out_b, upward, downward)


def thin_round(slabs, above, below, reach, count):
    has_bot, has_top, has_below, has_above = flags()

    def item(x, which):
        if x < 0:
            start = ((x + HALO) * ITEMS + which) * SPAN
            return below[start : start + SPAN]
        if x >= count:
            start = ((x - count) * ITEMS + which) * SPAN
            return above[start : start + SPAN]
        start = (x * ITEMS + which) * SPAN
        return slabs[start : start + SPAN]

    cx = {x: item(x, 0) for x in range(-reach, count + reach + 1)}
    cx[0] = cx[0] * has_below
    cx[count] = cx[count] * has_above
    span = range(-reach, count + reach)
    source = {x: item(x, 1) for x in span}
    layers = {x: Thin(item(x, 2), item(x, 3), item(x, 4), has_bot, has_top) for x in span}
    weight = {x: RELAX / (layers[x].diag + cx[x] + cx[x + 1]) for x in span}
    return source, cx, layers, weight


def thin_pass(p, rhs, cx, layers, weight, low, high):
    return {
        x: KEEP * p[x]
        + weight[x] * (rhs[x] + cx[x] * p[x - 1] + cx[x + 1] * p[x + 1] + layers[x].around(p[x]))
        for x in range(low, high)
    }


def edge_data(ref, p, x, beyond, link, rhs, cx, layers, weight):
    ref[0] = p[x]
    ref[1] = KEEP * p[x] + weight[x] * (rhs[x] + link * p[beyond] + layers[x].around(p[x]))
    step = thin_pass(p, rhs, cx, layers, weight, beyond, beyond + 1)
    ref[2] = rhs[x] + link * step[beyond]


def three_passes(p, above, below, rhs, cx, layers, weight, count):
    sides = ((count, count - 1, cx[count], above), (-1, 0, cx[0], below))
    for x, _, _, got in sides:
        p[x] = got[0]
    after = thin_pass(p, rhs, cx, layers, weight, 0, count)
    for x, near, link, got in sides:
        after[x] = got[1] + weight[x] * link * p[near]
    last = thin_pass(after, rhs, cx, layers, weight, 0, count)
    for x, near, link, got in sides:
        last[x] = KEEP * after[x] + weight[x] * (
            got[2] + link * after[near] + layers[x].around(after[x])
        )
    return thin_pass(last, rhs, cx, layers, weight, 0, count)


def traces(flux_bot, flux_top, bot, top, rows):
    count = len(flux_bot)
    stacked = jnp.concatenate(flux_bot + flux_top, axis=0)
    fill = jnp.zeros((rows - stacked.shape[0], stacked.shape[1]), F32)
    columns = jnp.concatenate([stacked, fill], axis=0).T
    return [
        sum(
            jnp.sum(columns[:, face * count + x : face * count + x + 1] * basis[0, x], axis=0, keepdims=True)
            for x in range(count)
        )
        for face, basis in enumerate((bot, top))
    ]


def first_thin(slabs, bot, top, got_a, got_b, p_out, sh_a, sh_b, above, below):
    count, rows = bot.shape[1:3]
    sort_pair((got_a, got_b), above, below)
    source, cx, layers, weight = thin_round(slabs, above, below, HALO, count)
    p = {x: weight[x] * source[x] for x in range(-HALO, count + HALO)}
    for margin in range(HALO - 1, -1, -1):
        p = thin_pass(p, source, cx, layers, weight, -margin, count + margin)
    for x in range(count):
        p_out[x] = p[x]
    flux_bot = [(layers[x].dbot * p[x])[SLAB : SLAB + 1] for x in range(count)]
    flux_top = [(layers[x].dtop * p[x])[SLAB - 1 : SLAB] for x in range(count)]
    cbot, ctop = traces(flux_bot, flux_top, bot, top, rows)

    def to_above(ref):
        ref[...] = ctop

    def to_below(ref):
        ref[...] = cbot

    by_parity("block", sh_a, sh_b, to_above, to_below)


def with_faces(source, layers, data, count):
    gbot = {x: data[x : x + 1] for x in range(count)}
    gtop = {x: data[count + x : count + x + 1] for x in range(count)}
    rhs = {
        x: source[x] + layers[x].dbot * gbot[x] + layers[x].dtop * gtop[x]
        for x in range(count)
    }
    return gbot, gtop, rhs


def face_kernel(slabs, bot, top, got_a, got_b, p_in, *rest):
    parts = rest[:-6]
    data_out, edge_a, edge_b, mortar_out, above, below = rest[-6:]
    count, rows = bot.shape[1:3]
    sort_pair((got_a, got_b), above, below)
    jumps = MORTAR_STEP * sum(part[...] for part in parts)
    even = lax.rem(lax.axis_index("block"), 2) == 0
    own = jnp.where(even, jumps[0:1], jumps[1:2])
    under = jnp.where(even, jumps[1:2], jumps[0:1])
    mortar_out[...] = own
    lanes = lax.broadcasted_iota(jnp.int32, (rows, rows), 1)
    columns = jnp.zeros((rows, rows), F32)
    for face, (ref, values) in enumerate(((bot, under), (top, own))):
        for x in range(count):
            data = jnp.sum(ref[0, x] * values, axis=1, keepdims=True)
            columns = jnp.where(lanes == face * count + x, data, columns)
    data = columns.T[0 : 2 * count]
    data_out[...] = data
    source, cx, layers, weight = thin_round(slabs, above, below, 0, count)
    rhs = with_faces(source, layers, data, count)[2]
    p = {x: p_in[x] for x in range(count)}
    last = count - 1
    by_parity(
        "sub",
        edge_a,
        edge_b,
        lambda ref: edge_data(ref, p, last, last - 1, cx[last], rhs, cx, layers, weight),
        lambda ref: edge_data(ref, p, 0, 1, cx[1], rhs, cx, layers, weight),
    )


def second_thin(
    slabs, bot, top, got_a, got_b, p_in, data, edge_a, edge_b,
    p_out, cbot_out, ctop_out, above, below, edge_above, edge_below,
):
    count, rows = bot.shape[1:3]
    sort_pair((got_a, got_b), above, below)
    sort_pair((edge_a, edge_b), edge_above, edge_below)
    source, cx, layers, weight = thin_round(slabs, above, below, 1, count)
    gbot, gtop, rhs = with_faces(source, layers, data, count)
    p = {x: p_in[x] for x in range(count)}
    p = three_passes(p, edge_above, edge_below, rhs, cx, layers, weight, count)
    for x in range(count):
        p_out[x * SPAN : (x + 1) * SPAN] = p[x]
    flux_bot = [(layers[x].dbot * (p[x] - gbot[x]))[SLAB : SLAB + 1] for x in range(count)]
    flux_top = [(layers[x].dtop * (p[x] - gtop[x]))[SLAB - 1 : SLAB] for x in range(count)]
    cbot_out[...], ctop_out[...] = traces(flux_bot, flux_top, bot, top, rows)


def edge_kernel(src, tx, ty, tz, out_a, out_b):
    count = src.shape[1]
    has_bot, has_top, has_below, _ = flags()

    def layer(x):
        return Layer(ty[0, x], tz[0, x], has_bot, has_top)

    low = layer(0)
    w_low = RELAX / (low.diag + tx[0, 0] * has_below + tx[0, 1])
    p_low = w_low * src[0, 0]
    p_next = RELAX * src[0, 1] / (layer(1).diag + tx[0, 1] + tx[0, 2])
    q_low = KEEP * p_low + w_low * (src[0, 0] + tx[0, 1] * p_next + low.around(p_low))
    top = count - 1
    p_top = RELAX * src[0, top - 1] / (layer(top - 1).diag + tx[0, top - 1] + tx[0, top])

    def upward(ref):
        for i, v in enumerate((tx[0, top], p_top, src[0, top], src[0, top], ty[0, top], tz[0, top])):
            ref[i] = v

    def downward(ref):
        for i, v in enumerate((tx[0, 0], p_low, q_low, w_low, ty[0, 0], tz[0, 0])):
            ref[i] = v

    by_parity("sub", out_a, out_b, upward, downward)


def whole_setup(src, tx, ty, tz, above, below):
    count = src.shape[1]
    has_bot, has_top, has_below, has_above = flags()
    cx = {x: tx[0, x] for x in range(1, count)}
    cx[-1] = below[0]
    cx[0] = tx[0, 0] * has_below
    cx[count] = above[0] * has_above
    source = {x: src[0, x] for x in range(count)}
    source[-1] = below[2]
    layers = {x: Layer(ty[0, x], tz[0, x], has_bot, has_top) for x in range(count)}
    layers[-1] = Layer(below[4], below[5], has_bot, has_top)
    weight = {x: RELAX / (layers[x].diag + cx[x] + cx[x + 1]) for x in range(-1, count)}
    return source, cx, layers, weight


def first_whole(src, tx, ty, tz, got_a, got_b, after, p_out, mid_a, mid_b, above, below):
    count = src.shape[1]
    sort_pair((got_a, got_b), above, below)
    source, cx, layers, w = whole_setup(src, tx, ty, tz, above, below)
    p1 = {x: w[x] * source[x] for x in range(-1, count)}
    p1[-2] = below[1]
    p1[count] = above[1]
    p2 = thin_pass(p1, source, cx, layers, w, -1, count)
    p2[count] = above[2] + above[3] * cx[count] * p1[count - 1]
    p3 = thin_pass(p2, source, cx, layers, w, 0, count)
    for x in range(count):
        p_out[x] = p3[x]
    last = count - 1
    by_parity(
        "sub",
        mid_a,
        mid_b,
        lambda ref: edge_data(ref, p3, last, last - 1, cx[last], source, cx, layers, w),
        lambda ref: edge_data(ref, p3, 0, 1, cx[1], source, cx, layers, w),
    )


def second_whole(src, tx, ty, tz, got_a, got_b, p_in, mid_a, mid_b, thin, p_out, above, below, p_above, p_below):
    count, rows, cells = src.shape[1:]
    sort_pair((got_a, got_b), above, below)
    sort_pair((mid_a, mid_b), p_above, p_below)
    source, cx, layers, w = whole_setup(src, tx, ty, tz, above, below)
    has_bot, has_top, _, _ = flags()
    layers[count] = Layer(above[4], above[5], has_bot, has_top)
    w[count] = above[3]
    p3 = {x: p_in[x] for x in range(count)}
    p6 = three_passes(p3, p_above, p_below, source, cx, layers, w, count)
    cols = lax.broadcasted_iota(jnp.int32, (rows, cells), 1)
    face = (cols < PASSES) | (cols >= cells - PASSES)
    each = cells // SPAN
    for start in range(0, count, each):
        here = thin[start * SPAN : (start + each) * SPAN]
        if here.shape[0] < cells:
            here = jnp.concatenate([here, jnp.zeros((cells - here.shape[0], rows), F32)], axis=0)
        back = here.T
        for x in range(start, min(start + each, count)):
            shift = (cells - (x - start) * SPAN - SLAB) % cells
            p_out[0, x] = jnp.where(face, pltpu.roll(back, shift, 1), p6[x])


def call(kernel, outs, args, scratch=(), copies=0):
    space = pltpu.HBM if copies else pltpu.VMEM
    args = [pltpu.with_memory_space_constraint(a, space) for a in args]
    return pl.pallas_call(
        kernel,
        out_shape=[pltpu.VMEM(shape, F32) for shape in outs],
        in_specs=[pl.BlockSpec(memory_space=space)] * len(args),
        out_specs=[pl.BlockSpec(memory_space=pltpu.VMEM)] * len(outs),
        scratch_shapes=[pltpu.VMEM(shape, F32) for shape in scratch]
        + ([pltpu.SemaphoreType.DMA((copies,))] if copies else []),
        compiler_params=pltpu.CompilerParams(vmem_limit_bytes=16 << 20),
    )(*args)


def sub_swaps(blocks, subs):
    flat = lambda b, s: b * subs + s
    first = [(flat(b, s), flat(b, s ^ 1)) for b in range(blocks) for s in range(subs)]
    second = []
    for b in range(blocks):
        for s in range(subs):
            other = s + 1 if s % 2 else s - 1
            inside = 0 <= other < subs
            second.append((flat(b, s), flat(b, other) if inside else flat(b ^ 1, s)))
    return first, second


def work(source, trans_x, trans_y, trans_z, mortar_bot, mortar_top):
    count, rows, cells = source.shape[1:]
    width = mortar_bot.shape[3]
    subs = lax.axis_size("sub")
    blocks = lax.axis_size("block")
    assert subs % 2 == 0 and blocks % 2 == 0 and count > HALO
    names = ("block", "sub")
    pair_one, pair_two = sub_swaps(blocks, subs)

    def trade(a, b):
        first = lax.ppermute(a, names, pair_one)
        return first, lax.ppermute(b, names, pair_two)

    face = (rows, cells)
    each = cells // SPAN
    slab_rows = -(-count * ITEMS // each) * cells
    sent = (HALO * ITEMS + 1) * SPAN
    *coeffs, slabs, near_a, near_b = call(
        pack_kernel,
        [source.shape] * 4 + [(slab_rows, rows)] + [(sent, rows)] * 2,
        (source, trans_x, trans_y, trans_z),
        copies=4,
    )
    near = trade(near_a, near_b)
    edges = call(edge_kernel, [(EDGE,) + face] * 2, coeffs)
    edges = trade(*edges)
    slab = (SPAN, rows)
    third, share_a, share_b = call(
        first_thin,
        [(count,) + slab] + [(1, width)] * 2,
        (slabs, mortar_bot, mortar_top) + near,
        [(sent, rows)] * 2,
    )

    block_one = [(b, b ^ 1) for b in range(blocks)]
    block_two = [(b, (b + 1 if b % 2 else b - 1) % blocks) for b in range(blocks)]

    def everyone(value):
        if subs > DIRECT:
            return [lax.psum(value, "sub")]
        parts = [value]
        for k in range(subs - 1, 0, -1):
            parts.append(lax.ppermute(value, "sub", [(i, i ^ k) for i in range(subs)]))
        return parts

    other_a = lax.ppermute(share_a, "block", block_one)
    other_b = lax.ppermute(share_b, "block", block_two)
    jumps = jnp.concatenate([share_a + other_a, share_b + other_b], axis=0)
    parts = everyone(jumps)
    whole, mid_a, mid_b = call(
        first_whole,
        [(count,) + face] + [(MIDDLE,) + face] * 2,
        tuple(coeffs) + edges + (jumps,),
        [(EDGE,) + face] * 2,
    )
    middle = trade(mid_a, mid_b)
    data, edge_a, edge_b, mortar = call(
        face_kernel,
        [(2 * count, rows)] + [(MIDDLE,) + slab] * 2 + [(1, width)],
        (slabs, mortar_bot, mortar_top) + near + (third,) + tuple(parts),
        [(sent, rows)] * 2,
    )
    got = trade(edge_a, edge_b)
    slab_out, cbot, ctop = call(
        second_thin,
        [(each * SPAN, rows)] + [(1, width)] * 2,
        (slabs, mortar_bot, mortar_top) + near + (third, data) + got,
        [(sent, rows)] * 2 + [(MIDDLE,) + slab] * 2,
    )
    upper = lax.ppermute(cbot, "block", [((b + 1) % blocks, b) for b in range(blocks)])
    total = mortar + MORTAR_STEP * sum(everyone(ctop + upper))
    share = width // subs
    final = lax.dynamic_slice_in_dim(total[0], lax.axis_index("sub") * share, share, 0)
    (pressure,) = call(
        second_whole,
        [source.shape],
        tuple(coeffs) + edges + (whole,) + middle + (slab_out,),
        [(EDGE,) + face] * 2 + [(MIDDLE,) + face] * 2,
    )
    return pressure, final[None]


def solution(mesh):
    spec = P("block", "sub", None, None)
    return jax.shard_map(
        work,
        mesh=mesh,
        in_specs=(spec,) * 6,
        out_specs=(spec, P("block", "sub")),
        check_vma=False,
    )
```

```python
import jax
import jax.numpy as jnp
from jax import lax
from jax.experimental import pallas as pl
from jax.experimental.pallas import tpu as pltpu
from jax.sharding import PartitionSpec as P


PASSES = 3
RELAX = 0.8
KEEP = 1.0 - RELAX
MORTAR_STEP = 0.05
F32 = jnp.float32
EDGE = 6
MIDDLE = 3
HALO = 2
SLAB = 8
SPAN = 2 * SLAB
DIRECT = 4
ITEMS = 5


def prev(v, axis):
    return pltpu.roll(v, 1, axis)


def following(v, axis):
    return pltpu.roll(v, v.shape[axis] - 1, axis)


class Layer:
    def __init__(self, trans_y, trans_z, has_bot, has_top):
        rows = lax.broadcasted_iota(jnp.int32, trans_y.shape, 0)
        self.cy = jnp.where(rows > 0, trans_y, 0.0)
        self.cz, self.zsum = along_z(trans_z, has_bot, has_top)
        self.diag = self.cy + following(self.cy, 0) + self.zsum

    def around(self, p):
        return (
            self.cy * prev(p, 0)
            + following(self.cy * p, 0)
            + self.cz * prev(p, 1)
            + following(self.cz * p, 1)
        )


def along_z(trans_z, has_bot, has_top):
    cols = lax.broadcasted_iota(jnp.int32, trans_z.shape, 1)
    first = cols == 0
    last = cols == trans_z.shape[1] - 1
    cz = jnp.where(first, 0.0, trans_z)
    ends = jnp.where(first, trans_z * has_bot, jnp.where(last, trans_z * has_top, 0.0))
    return cz, cz + following(cz, 1) + ends


class Thin:
    def __init__(self, trans_y, trans_z, zsum, live):
        rows = lax.broadcasted_iota(jnp.int32, trans_y.shape, 0)
        cols = lax.broadcasted_iota(jnp.int32, trans_y.shape, 1)
        self.cy = jnp.where(cols > 0, trans_y, 0.0)
        self.cz = jnp.where(rows == SLAB, 0.0, trans_z)
        self.face = jnp.where((rows == SLAB) | (rows == SLAB - 1), trans_z, 0.0) * live
        self.diag = self.cy + following(self.cy, 1) + zsum

    def around(self, p):
        return (
            self.cy * prev(p, 1)
            + following(self.cy * p, 1)
            + self.cz * prev(p, 0)
            + following(self.cz * p, 0)
        )


def flags():
    block = lax.axis_index("block")
    sub = lax.axis_index("sub")
    has_bot = (block > 0).astype(F32)
    has_top = (block < lax.axis_size("block") - 1).astype(F32)
    has_below = (sub > 0).astype(F32)
    has_above = (sub < lax.axis_size("sub") - 1).astype(F32)
    return has_bot, has_top, has_below, has_above


def by_parity(axis, first, second, upward, downward):
    even = lax.rem(lax.axis_index(axis), 2) == 0

    @pl.when(even)
    def _():
        upward(first)
        downward(second)

    @pl.when(jnp.logical_not(even))
    def _():
        upward(second)
        downward(first)


def sort_pair(pair, above, below):
    def take_above(ref):
        above[...] = ref[...]

    def take_below(ref):
        below[...] = ref[...]

    by_parity("sub", *pair, take_above, take_below)


def pack_kernel(src, tx, ty, tz, src_v, tx_v, ty_v, tz_v, slabs, firsts, sems):
    copies = [
        pltpu.make_async_copy(here, there, sems.at[i])
        for i, (here, there) in enumerate(
            ((tz, tz_v), (src, src_v), (tx, tx_v), (ty, ty_v))
        )
    ]
    for copy in copies:
        copy.start()
    for copy in copies:
        copy.wait()
    count, rows, cells = src_v.shape[1:]
    has_bot, has_top, _, _ = flags()
    items = []
    for x in range(count):
        zsum = along_z(tz_v[0, x], has_bot, has_top)[1]
        items += [tx_v[0, x], src_v[0, x], ty_v[0, x], tz_v[0, x], zsum]
    slot = lax.broadcasted_iota(jnp.int32, (rows, cells), 1) // SPAN
    each = cells // SPAN
    for start in range(0, len(items), each):
        packed = jnp.zeros((rows, cells), F32)
        here = items[start : start + each]
        for j, item in enumerate(here):
            turned = pltpu.roll(item, (SPAN * j + SLAB) % cells, 1)
            packed = jnp.where(slot == j, turned, packed)
        turned = packed.T
        for j in range(len(here)):
            k = start + j
            slabs[k] = turned[j * SPAN : (j + 1) * SPAN]
            firsts[k] = turned[j * SPAN + SLAB : (j + 1) * SPAN]


def edge_parts(items, make, has_below):
    tx, src = (lambda x: items(0, x)), (lambda x: items(1, x))
    low = make(0)
    w_low = RELAX / (low.diag + tx(0) * has_below + tx(1))
    p_low = w_low * src(0)
    p_next = RELAX * src(1) / (make(1).diag + tx(1) + tx(2))
    q_low = KEEP * p_low + w_low * (src(0) + tx(1) * p_next + low.around(p_low))
    return p_low, q_low, w_low


def first_three(count, source, cx, layers, w, above, below):
    p1 = {x: w[x] * source[x] for x in range(-1, count)}
    p1[-2] = below[1]
    p1[count] = above[1]
    p2 = thin_pass(p1, source, cx, layers, w, -1, count)
    p2[count] = above[2] + above[3] * cx[count] * p1[count - 1]
    return thin_pass(p2, source, cx, layers, w, 0, count)


def join_kernel(slabs, firsts, joined, out_a, out_b):
    for k in range(firsts.shape[0]):
        joined[k, 0:SLAB] = slabs[k, 0:SLAB]
        joined[k, SLAB:SPAN] = firsts[k]
    count = firsts.shape[0] // ITEMS
    _, live, has_below, _ = flags()

    def item(which, x):
        return joined[x * ITEMS + which]

    def make(x):
        return Thin(item(2, x), item(3, x), item(4, x), live)

    p_low, q_low, w_low = edge_parts(item, make, has_below)
    top = count - 1
    p_top = RELAX * item(1, top - 1) / (make(top - 1).diag + item(0, top - 1) + item(0, top))

    def upward(ref):
        values = (item(0, top), p_top, item(1, top), item(4, top), item(2, top), item(3, top))
        for i, v in enumerate(values):
            ref[i] = v

    def downward(ref):
        values = (item(0, 0), p_low, q_low, w_low, item(2, 0), item(3, 0))
        for i, v in enumerate(values):
            ref[i] = v

    by_parity("sub", out_a, out_b, upward, downward)


def thin_setup(joined, above, below):
    count = joined.shape[0] // ITEMS
    _, live, has_below, has_above = flags()
    cx = {x: joined[x * ITEMS] for x in range(1, count)}
    cx[-1] = below[0]
    cx[0] = joined[0] * has_below
    cx[count] = above[0] * has_above
    source = {x: joined[x * ITEMS + 1] for x in range(count)}
    source[-1] = below[2]
    layers = {
        x: Thin(*(joined[x * ITEMS + i] for i in (2, 3, 4)), live) for x in range(count)
    }
    layers[-1] = Thin(below[4], below[5], below[3], live)
    layers[count] = Thin(above[4], above[5], above[3], live)
    w = {x: RELAX / (layers[x].diag + cx[x] + cx[x + 1]) for x in range(-1, count)}
    w[count] = above[3]
    return source, cx, layers, w


def thin_pass(p, rhs, cx, layers, weight, low, high):
    return {
        x: KEEP * p[x]
        + weight[x] * (rhs[x] + cx[x] * p[x - 1] + cx[x + 1] * p[x + 1] + layers[x].around(p[x]))
        for x in range(low, high)
    }


def edge_data(ref, p, x, beyond, link, rhs, cx, layers, weight):
    ref[0] = p[x]
    ref[1] = KEEP * p[x] + weight[x] * (rhs[x] + link * p[beyond] + layers[x].around(p[x]))
    step = thin_pass(p, rhs, cx, layers, weight, beyond, beyond + 1)
    ref[2] = rhs[x] + link * step[beyond]


def three_passes(p, above, below, rhs, cx, layers, weight, count):
    sides = ((count, count - 1, cx[count], above), (-1, 0, cx[0], below))
    for x, _, _, got in sides:
        p[x] = got[0]
    after = thin_pass(p, rhs, cx, layers, weight, 0, count)
    for x, near, link, got in sides:
        after[x] = got[1] + weight[x] * link * p[near]
    last = thin_pass(after, rhs, cx, layers, weight, 0, count)
    for x, near, link, got in sides:
        last[x] = KEEP * after[x] + weight[x] * (
            got[2] + link * after[near] + layers[x].around(after[x])
        )
    return thin_pass(last, rhs, cx, layers, weight, 0, count)


def traces(flux, bot, top, rows):
    count = len(flux)
    stacked = [f[SLAB : SLAB + 1] for f in flux] + [f[SLAB - 1 : SLAB] for f in flux]
    stacked.append(jnp.zeros((rows - len(stacked), flux[0].shape[1]), F32))
    columns = jnp.concatenate(stacked, axis=0).T
    total = sum(
        columns[:, face * count + x : face * count + x + 1] * basis[0, x]
        for face, basis in enumerate((bot, top))
        for x in range(count)
    )
    return jnp.sum(total, axis=0, keepdims=True)


def first_thin(joined, bot, top, got_a, got_b, p_out, share, above, below):
    count, rows = bot.shape[1:3]
    sort_pair((got_a, got_b), above, below)
    source, cx, layers, w = thin_setup(joined, above, below)
    p = first_three(count, source, cx, layers, w, above, below)
    for x in range(count):
        p_out[x] = p[x]
    flux = [layers[x].face * p[x] for x in range(count)]
    share[...] = traces(flux, bot, top, rows)


def with_faces(source, layers, data, count):
    known = {}
    for x in range(count):
        planes = lax.broadcasted_iota(jnp.int32, source[x].shape, 0)
        known[x] = jnp.where(planes == SLAB, data[x : x + 1], data[count + x : count + x + 1])
    return known, {x: source[x] + layers[x].face * known[x] for x in range(count)}


def face_kernel(joined, bot, top, got_a, got_b, p_in, *rest):
    parts = rest[:-6]
    data_out, edge_a, edge_b, mortar_out, above, below = rest[-6:]
    count, rows = bot.shape[1:3]
    sort_pair((got_a, got_b), above, below)
    mortar = MORTAR_STEP * sum(part[...] for part in parts)
    mortar_out[...] = mortar
    lanes = lax.broadcasted_iota(jnp.int32, (rows, rows), 1)
    columns = jnp.zeros((rows, rows), F32)
    for face, ref in enumerate((bot, top)):
        for x in range(count):
            data = jnp.sum(ref[0, x] * mortar, axis=1, keepdims=True)
            columns = jnp.where(lanes == face * count + x, data, columns)
    data = columns.T[0 : 2 * count]
    data_out[...] = data
    source, cx, layers, w = thin_setup(joined, above, below)
    rhs = with_faces(source, layers, data, count)[1]
    p = {x: p_in[x] for x in range(count)}
    last = count - 1
    by_parity(
        "sub",
        edge_a,
        edge_b,
        lambda ref: edge_data(ref, p, last, last - 1, cx[last], rhs, cx, layers, w),
        lambda ref: edge_data(ref, p, 0, 1, cx[1], rhs, cx, layers, w),
    )


def second_thin(
    joined, bot, top, got_a, got_b, p_in, data, edge_a, edge_b,
    lasts, firsts, share, above, below, edge_above, edge_below,
):
    count, rows = bot.shape[1:3]
    sort_pair((got_a, got_b), above, below)
    sort_pair((edge_a, edge_b), edge_above, edge_below)
    source, cx, layers, w = thin_setup(joined, above, below)
    known, rhs = with_faces(source, layers, data, count)
    p = {x: p_in[x] for x in range(count)}
    p = three_passes(p, edge_above, edge_below, rhs, cx, layers, w, count)
    for x in range(count):
        lasts[x] = p[x][0:SLAB]
        firsts[x] = p[x][SLAB:SPAN]
    flux = [layers[x].face * (p[x] - known[x]) for x in range(count)]
    share[...] = traces(flux, bot, top, rows)


def edge_kernel(src, tx, ty, tz, out_a, out_b):
    count = src.shape[1]
    has_bot, has_top, has_below, _ = flags()

    def make(x):
        return Layer(ty[0, x], tz[0, x], has_bot, has_top)

    p_low, q_low, w_low = edge_parts(lambda which, x: (tx, src)[which][0, x], make, has_below)
    top = count - 1
    p_top = RELAX * src[0, top - 1] / (make(top - 1).diag + tx[0, top - 1] + tx[0, top])

    def upward(ref):
        for i, v in enumerate((tx[0, top], p_top, src[0, top], src[0, top], ty[0, top], tz[0, top])):
            ref[i] = v

    def downward(ref):
        for i, v in enumerate((tx[0, 0], p_low, q_low, w_low, ty[0, 0], tz[0, 0])):
            ref[i] = v

    by_parity("sub", out_a, out_b, upward, downward)


def whole_setup(src, tx, ty, tz, above, below):
    count = src.shape[1]
    has_bot, has_top, has_below, has_above = flags()
    cx = {x: tx[0, x] for x in range(1, count)}
    cx[-1] = below[0]
    cx[0] = tx[0, 0] * has_below
    cx[count] = above[0] * has_above
    source = {x: src[0, x] for x in range(count)}
    source[-1] = below[2]
    layers = {x: Layer(ty[0, x], tz[0, x], has_bot, has_top) for x in range(count)}
    layers[-1] = Layer(below[4], below[5], has_bot, has_top)
    weight = {x: RELAX / (layers[x].diag + cx[x] + cx[x + 1]) for x in range(-1, count)}
    return source, cx, layers, weight


def first_whole(src, tx, ty, tz, got_a, got_b, after, p_out, mid_a, mid_b, above, below):
    count = src.shape[1]
    sort_pair((got_a, got_b), above, below)
    source, cx, layers, w = whole_setup(src, tx, ty, tz, above, below)
    p3 = first_three(count, source, cx, layers, w, above, below)
    for x in range(count):
        p_out[x] = p3[x]
    last = count - 1
    by_parity(
        "sub",
        mid_a,
        mid_b,
        lambda ref: edge_data(ref, p3, last, last - 1, cx[last], source, cx, layers, w),
        lambda ref: edge_data(ref, p3, 0, 1, cx[1], source, cx, layers, w),
    )


def second_whole(src, tx, ty, tz, got_a, got_b, p_in, mid_a, mid_b, p_out, above, below, p_above, p_below):
    count = src.shape[1]
    sort_pair((got_a, got_b), above, below)
    sort_pair((mid_a, mid_b), p_above, p_below)
    source, cx, layers, w = whole_setup(src, tx, ty, tz, above, below)
    has_bot, has_top, _, _ = flags()
    layers[count] = Layer(above[4], above[5], has_bot, has_top)
    w[count] = above[3]
    p3 = {x: p_in[x] for x in range(count)}
    p6 = three_passes(p3, p_above, p_below, source, cx, layers, w, count)
    for x in range(count):
        p_out[x] = p6[x]


def merge_kernel(whole, lasts, firsts, p_out):
    count, rows, cells = whole.shape
    cols = lax.broadcasted_iota(jnp.int32, (rows, cells), 1)
    face = (cols < PASSES) | (cols >= cells - PASSES)
    each = cells // SPAN
    for start in range(0, count, each):
        stop = min(start + each, count)
        here = [part[x] for x in range(start, stop) for part in (lasts, firsts)]
        if (stop - start) * SPAN < cells:
            here.append(jnp.zeros((cells - (stop - start) * SPAN, rows), F32))
        back = jnp.concatenate(here, axis=0).T
        for x in range(start, stop):
            shift = (cells - (x - start) * SPAN - SLAB) % cells
            p_out[0, x] = jnp.where(face, pltpu.roll(back, shift, 1), whole[x])


def call(kernel, outs, args, scratch=(), copies=0):
    space = pltpu.HBM if copies else pltpu.VMEM
    args = [pltpu.with_memory_space_constraint(a, space) for a in args]
    return pl.pallas_call(
        kernel,
        out_shape=[pltpu.VMEM(shape, F32) for shape in outs],
        in_specs=[pl.BlockSpec(memory_space=space)] * len(args),
        out_specs=[pl.BlockSpec(memory_space=pltpu.VMEM)] * len(outs),
        scratch_shapes=[pltpu.VMEM(shape, F32) for shape in scratch]
        + ([pltpu.SemaphoreType.DMA((copies,))] if copies else []),
        compiler_params=pltpu.CompilerParams(vmem_limit_bytes=16 << 20),
    )(*args)


def sub_swaps(blocks, subs):
    flat = lambda b, s: b * subs + s
    first = [(flat(b, s), flat(b, s ^ 1)) for b in range(blocks) for s in range(subs)]
    second = []
    for b in range(blocks):
        for s in range(subs):
            other = s + 1 if s % 2 else s - 1
            inside = 0 <= other < subs
            second.append((flat(b, s), flat(b, other) if inside else flat(b ^ 1, s)))
    return first, second


def work(source, trans_x, trans_y, trans_z, mortar_bot, mortar_top):
    count, rows, cells = source.shape[1:]
    width = mortar_bot.shape[3]
    subs = lax.axis_size("sub")
    blocks = lax.axis_size("block")
    assert subs % 2 == 0 and blocks % 2 == 0 and count > HALO
    names = ("block", "sub")
    pair_one, pair_two = sub_swaps(blocks, subs)

    def trade(a, b):
        first = lax.ppermute(a, names, pair_one)
        return first, lax.ppermute(b, names, pair_two)

    face = (rows, cells)
    kept = count * ITEMS
    slab = (SPAN, rows)
    half = (SLAB, rows)
    up = [(b, (b + 1) % blocks) for b in range(blocks)]
    down = [(b, a) for a, b in up]

    def everyone(value):
        if subs > DIRECT:
            return [lax.psum(value, "sub")]
        parts = [value]
        for k in range(subs - 1, 0, -1):
            parts.append(lax.ppermute(value, "sub", [(i, i ^ k) for i in range(subs)]))
        return parts

    *coeffs, slabs, firsts = call(
        pack_kernel,
        [source.shape] * 4 + [(kept,) + slab, (kept,) + half],
        (source, trans_x, trans_y, trans_z),
        copies=4,
    )
    firsts = lax.ppermute(firsts, "block", down)
    basis = lax.ppermute(mortar_bot, "block", down)
    joined, near_a, near_b = call(
        join_kernel, [(kept,) + slab] + [(EDGE,) + slab] * 2, (slabs, firsts)
    )
    near = trade(near_a, near_b)
    edges = call(edge_kernel, [(EDGE,) + face] * 2, coeffs)
    edges = trade(*edges)
    fixed = (joined, basis, mortar_top) + near
    sides = [(EDGE,) + slab] * 2
    third, share = call(first_thin, [(count,) + slab, (1, width)], fixed, sides)
    parts = everyone(share)
    whole, mid_a, mid_b = call(
        first_whole,
        [(count,) + face] + [(MIDDLE,) + face] * 2,
        tuple(coeffs) + edges + (share,),
        [(EDGE,) + face] * 2,
    )
    middle = trade(mid_a, mid_b)
    data, edge_a, edge_b, mortar = call(
        face_kernel,
        [(2 * count, rows)] + [(MIDDLE,) + slab] * 2 + [(1, width)],
        fixed + (third,) + tuple(parts),
        sides,
    )
    got = trade(edge_a, edge_b)
    lasts, firsts, share = call(
        second_thin,
        [(count,) + half] * 2 + [(1, width)],
        fixed + (third, data) + got,
        sides + [(MIDDLE,) + slab] * 2,
    )
    total = mortar + MORTAR_STEP * sum(everyone(share))
    columns = width // subs
    final = lax.dynamic_slice_in_dim(total[0], lax.axis_index("sub") * columns, columns, 0)
    firsts = lax.ppermute(firsts, "block", up)
    (whole,) = call(
        second_whole,
        [(count,) + face],
        tuple(coeffs) + edges + (whole,) + middle,
        [(EDGE,) + face] * 2 + [(MIDDLE,) + face] * 2,
    )
    (pressure,) = call(merge_kernel, [source.shape], (whole, lasts, firsts))
    return pressure, final[None]


def solution(mesh):
    spec = P("block", "sub", None, None)
    return jax.shard_map(
        work,
        mesh=mesh,
        in_specs=(spec,) * 6,
        out_specs=(spec, P("block", "sub")),
        check_vma=False,
    )
```

```python
import jax
import jax.numpy as jnp
from jax import lax
from jax.experimental import pallas as pl
from jax.experimental.pallas import tpu as pltpu
from jax.sharding import PartitionSpec as P


PASSES = 3
RELAX = 0.8
KEEP = 1.0 - RELAX
MORTAR_STEP = 0.05
F32 = jnp.float32
EDGE = 6
MIDDLE = 3
HALO = 2
SLAB = 8
SPAN = 2 * SLAB
DIRECT = 4
ITEMS = 5


def prev(v, axis):
    return pltpu.roll(v, 1, axis)


def following(v, axis):
    return pltpu.roll(v, v.shape[axis] - 1, axis)


class Layer:
    def __init__(self, trans_y, trans_z, has_bot, has_top):
        rows = lax.broadcasted_iota(jnp.int32, trans_y.shape, 0)
        self.cy = jnp.where(rows > 0, trans_y, 0.0)
        self.cz, self.zsum = along_z(trans_z, has_bot, has_top)
        self.diag = self.cy + following(self.cy, 0) + self.zsum

    def around(self, p):
        return (
            self.cy * prev(p, 0)
            + following(self.cy * p, 0)
            + self.cz * prev(p, 1)
            + following(self.cz * p, 1)
        )


def along_z(trans_z, has_bot, has_top):
    cols = lax.broadcasted_iota(jnp.int32, trans_z.shape, 1)
    first = cols == 0
    last = cols == trans_z.shape[1] - 1
    cz = jnp.where(first, 0.0, trans_z)
    ends = jnp.where(first, trans_z * has_bot, jnp.where(last, trans_z * has_top, 0.0))
    return cz, cz + following(cz, 1) + ends


class Thin:
    def __init__(self, trans_y, trans_z, zsum, has_bot, has_top):
        rows = lax.broadcasted_iota(jnp.int32, trans_y.shape, 0)
        cols = lax.broadcasted_iota(jnp.int32, trans_y.shape, 1)
        self.cy = jnp.where(cols > 0, trans_y, 0.0)
        self.cz = jnp.where(rows == SLAB, 0.0, trans_z)
        top = jnp.where(rows == SLAB - 1, trans_z * has_top, 0.0)
        self.face = jnp.where(rows == SLAB, trans_z * has_bot, top)
        self.diag = self.cy + following(self.cy, 1) + zsum

    def around(self, p):
        return (
            self.cy * prev(p, 1)
            + following(self.cy * p, 1)
            + self.cz * prev(p, 0)
            + following(self.cz * p, 0)
        )


def flags():
    block = lax.axis_index("block")
    sub = lax.axis_index("sub")
    has_bot = (block > 0).astype(F32)
    has_top = (block < lax.axis_size("block") - 1).astype(F32)
    has_below = (sub > 0).astype(F32)
    has_above = (sub < lax.axis_size("sub") - 1).astype(F32)
    return has_bot, has_top, has_below, has_above


def by_parity(axis, first, second, upward, downward):
    even = lax.rem(lax.axis_index(axis), 2) == 0

    @pl.when(even)
    def _():
        upward(first)
        downward(second)

    @pl.when(jnp.logical_not(even))
    def _():
        upward(second)
        downward(first)


def sort_pair(pair, above, below):
    def take_above(ref):
        above[...] = ref[...]

    def take_below(ref):
        below[...] = ref[...]

    by_parity("sub", *pair, take_above, take_below)


def pack_kernel(src, tx, ty, tz, src_v, tx_v, ty_v, tz_v, slabs, out_a, out_b, sems):
    count, rows, cells = src_v.shape[1:]
    copies = [
        pltpu.make_async_copy(here, there, sems.at[i])
        for i, (here, there) in enumerate(
            ((tz, tz_v), (tx, tx_v), (src, src_v), (ty, ty_v))
        )
    ]
    for copy in copies:
        copy.start()
    for copy in copies:
        copy.wait()
    has_bot, has_top, has_below, _ = flags()
    slot = lax.broadcasted_iota(jnp.int32, (rows, cells), 1) // SPAN
    each = cells // SPAN
    packed, done = jnp.zeros((rows, cells), F32), 0

    def flush(packed, done):
        turned = packed.T
        start = (done - 1) // each * each
        for k in range(start, done):
            slabs[k] = turned[(k - start) * SPAN : (k - start + 1) * SPAN]

    for x in range(count):
        zsum = along_z(tz_v[0, x], has_bot, has_top)[1]
        for item in (tx_v[0, x], src_v[0, x], ty_v[0, x], tz_v[0, x], zsum):
            j = done % each
            turned = pltpu.roll(item, (SPAN * j + SLAB) % cells, 1)
            packed = jnp.where(slot == j, turned, packed)
            done += 1
            if done % each == 0 or done == count * ITEMS:
                flush(packed, done)

    def item(which, x):
        return slabs[x * ITEMS + which]

    def make(x):
        return Thin(item(2, x), item(3, x), item(4, x), has_bot, has_top)

    p_low, q_low, w_low = edge_parts(item, make, has_below)
    top = count - 1
    p_top = RELAX * item(1, top - 1) / (make(top - 1).diag + item(0, top - 1) + item(0, top))

    def upward(ref):
        values = (item(0, top), p_top, item(1, top), item(4, top), item(2, top), item(3, top))
        for i, v in enumerate(values):
            ref[i] = v

    def downward(ref):
        values = (item(0, 0), p_low, q_low, w_low, item(2, 0), item(3, 0))
        for i, v in enumerate(values):
            ref[i] = v

    by_parity("sub", out_a, out_b, upward, downward)


def edge_parts(items, make, has_below):
    tx, src = (lambda x: items(0, x)), (lambda x: items(1, x))
    low = make(0)
    w_low = RELAX / (low.diag + tx(0) * has_below + tx(1))
    p_low = w_low * src(0)
    p_next = RELAX * src(1) / (make(1).diag + tx(1) + tx(2))
    q_low = KEEP * p_low + w_low * (src(0) + tx(1) * p_next + low.around(p_low))
    return p_low, q_low, w_low


def first_three(count, source, cx, layers, w, above, below):
    p1 = {x: w[x] * source[x] for x in range(-1, count)}
    p1[-2] = below[1]
    p1[count] = above[1]
    p2 = thin_pass(p1, source, cx, layers, w, -1, count)
    p2[count] = above[2] + above[3] * cx[count] * p1[count - 1]
    return thin_pass(p2, source, cx, layers, w, 0, count)


def thin_setup(slabs, above, below):
    count = slabs.shape[0] // ITEMS
    has_bot, has_top, has_below, has_above = flags()
    cx = {x: slabs[x * ITEMS] for x in range(1, count)}
    cx[-1] = below[0]
    cx[0] = slabs[0] * has_below
    cx[count] = above[0] * has_above
    source = {x: slabs[x * ITEMS + 1] for x in range(count)}
    source[-1] = below[2]
    layers = {
        x: Thin(*(slabs[x * ITEMS + i] for i in (2, 3, 4)), has_bot, has_top)
        for x in range(count)
    }
    layers[-1] = Thin(below[4], below[5], below[3], has_bot, has_top)
    layers[count] = Thin(above[4], above[5], above[3], has_bot, has_top)
    w = {x: RELAX / (layers[x].diag + cx[x] + cx[x + 1]) for x in range(-1, count)}
    w[count] = above[3]
    return source, cx, layers, w


def thin_pass(p, rhs, cx, layers, weight, low, high):
    return {
        x: KEEP * p[x]
        + weight[x] * (rhs[x] + cx[x] * p[x - 1] + cx[x + 1] * p[x + 1] + layers[x].around(p[x]))
        for x in range(low, high)
    }


def edge_data(ref, p, x, beyond, link, rhs, cx, layers, weight):
    ref[0] = p[x]
    ref[1] = KEEP * p[x] + weight[x] * (rhs[x] + link * p[beyond] + layers[x].around(p[x]))
    step = thin_pass(p, rhs, cx, layers, weight, beyond, beyond + 1)
    ref[2] = rhs[x] + link * step[beyond]


def three_passes(p, above, below, rhs, cx, layers, weight, count):
    sides = ((count, count - 1, cx[count], above), (-1, 0, cx[0], below))
    for x, _, _, got in sides:
        p[x] = got[0]
    after = thin_pass(p, rhs, cx, layers, weight, 0, count)
    for x, near, link, got in sides:
        after[x] = got[1] + weight[x] * link * p[near]
    last = thin_pass(after, rhs, cx, layers, weight, 0, count)
    for x, near, link, got in sides:
        last[x] = KEEP * after[x] + weight[x] * (
            got[2] + link * after[near] + layers[x].around(after[x])
        )
    return thin_pass(last, rhs, cx, layers, weight, 0, count)


def traces(flux, bot, top):
    count = len(flux)
    planes = (SLAB, SLAB - 1)
    columns = jnp.concatenate([f[at : at + 1] for at in planes for f in flux], axis=0).T
    sums = []
    for face, basis in enumerate((bot, top)):
        total = sum(
            columns[:, face * count + x : face * count + x + 1] * basis[0, x] for x in range(count)
        )
        sums.append(jnp.sum(total, axis=0, keepdims=True))
    return sums


def first_thin(slabs, bot, top, got_a, got_b, p_out, kept, sh_a, sh_b, above, below):
    count = bot.shape[1]
    sort_pair((got_a, got_b), above, below)
    source, cx, layers, w = thin_setup(slabs, above, below)
    p = first_three(count, source, cx, layers, w, above, below)
    for x in range(count):
        p_out[x] = p[x]
    cbot, ctop = traces([layers[x].face * p[x] for x in range(count)], bot, top)

    def to_above(ref):
        ref[...] = ctop

    def to_below(ref):
        ref[...] = cbot

    by_parity("block", sh_a, sh_b, to_above, to_below)
    for x in range(-1, count + 1):
        for i, v in enumerate((cx[x], w[x], layers[x].cy, layers[x].cz, layers[x].face)):
            kept[x + 1, i] = v


class Kept(Thin):
    def __init__(self, kept, x):
        self.cy, self.cz, self.face = (kept[x + 1, i] for i in (2, 3, 4))


def thin_again(slabs, kept):
    count = slabs.shape[0] // ITEMS
    span = range(-1, count + 1)
    cx = {x: kept[x + 1, 0] for x in span}
    w = {x: kept[x + 1, 1] for x in span}
    layers = {x: Kept(kept, x) for x in span}
    return {x: slabs[x * ITEMS + 1] for x in range(count)}, cx, layers, w


def with_faces(source, layers, data, count):
    known = {}
    for x in range(count):
        planes = lax.broadcasted_iota(jnp.int32, source[x].shape, 0)
        known[x] = jnp.where(planes == SLAB, data[x : x + 1], data[count + x : count + x + 1])
    return known, {x: source[x] + layers[x].face * known[x] for x in range(count)}


def face_kernel(slabs, bot, top, kept, p_in, *rest):
    parts = rest[:-4]
    data_out, edge_a, edge_b, mortar_out = rest[-4:]
    count = bot.shape[1]
    jumps = MORTAR_STEP * sum(part[...] for part in parts)
    even = lax.rem(lax.axis_index("block"), 2) == 0
    own = jnp.where(even, jumps[0:1], jumps[1:2])
    under = jnp.where(even, jumps[1:2], jumps[0:1])
    mortar_out[...] = own
    columns = [
        jnp.sum(ref[0, x] * values, axis=1, keepdims=True)
        for ref, values in ((bot, under), (top, own))
        for x in range(count)
    ]
    data = jnp.concatenate(columns, axis=1).T
    data_out[...] = data
    source, cx, layers, w = thin_again(slabs, kept)
    rhs = with_faces(source, layers, data, count)[1]
    p = {x: p_in[x] for x in range(count)}
    last = count - 1
    by_parity(
        "sub",
        edge_a,
        edge_b,
        lambda ref: edge_data(ref, p, last, last - 1, cx[last], rhs, cx, layers, w),
        lambda ref: edge_data(ref, p, 0, 1, cx[1], rhs, cx, layers, w),
    )


def second_thin(
    slabs, bot, top, kept, p_in, data, edge_a, edge_b,
    p_out, cbot_out, ctop_out, edge_above, edge_below,
):
    count = bot.shape[1]
    sort_pair((edge_a, edge_b), edge_above, edge_below)
    source, cx, layers, w = thin_again(slabs, kept)
    known, rhs = with_faces(source, layers, data, count)
    p = {x: p_in[x] for x in range(count)}
    p = three_passes(p, edge_above, edge_below, rhs, cx, layers, w, count)
    for x in range(count):
        p_out[x] = p[x]
    flux = [layers[x].face * (p[x] - known[x]) for x in range(count)]
    cbot_out[...], ctop_out[...] = traces(flux, bot, top)


def edge_kernel(src, tx, ty, tz, out_a, out_b):
    count = src.shape[1]
    has_bot, has_top, has_below, _ = flags()

    def make(x):
        return Layer(ty[0, x], tz[0, x], has_bot, has_top)

    p_low, q_low, w_low = edge_parts(lambda which, x: (tx, src)[which][0, x], make, has_below)
    top = count - 1
    p_top = RELAX * src[0, top - 1] / (make(top - 1).diag + tx[0, top - 1] + tx[0, top])

    def upward(ref):
        for i, v in enumerate((tx[0, top], p_top, src[0, top], src[0, top], ty[0, top], tz[0, top])):
            ref[i] = v

    def downward(ref):
        for i, v in enumerate((tx[0, 0], p_low, q_low, w_low, ty[0, 0], tz[0, 0])):
            ref[i] = v

    by_parity("sub", out_a, out_b, upward, downward)


def whole_setup(src, tx, ty, tz, above, below):
    count = src.shape[1]
    has_bot, has_top, has_below, has_above = flags()
    cx = {x: tx[0, x] for x in range(1, count)}
    cx[-1] = below[0]
    cx[0] = tx[0, 0] * has_below
    cx[count] = above[0] * has_above
    source = {x: src[0, x] for x in range(count)}
    source[-1] = below[2]
    layers = {x: Layer(ty[0, x], tz[0, x], has_bot, has_top) for x in range(count)}
    layers[-1] = Layer(below[4], below[5], has_bot, has_top)
    weight = {x: RELAX / (layers[x].diag + cx[x] + cx[x + 1]) for x in range(-1, count)}
    return source, cx, layers, weight


def first_whole(src, tx, ty, tz, got_a, got_b, p_out, mid_a, mid_b, above, below):
    count = src.shape[1]
    sort_pair((got_a, got_b), above, below)
    source, cx, layers, w = whole_setup(src, tx, ty, tz, above, below)
    p3 = first_three(count, source, cx, layers, w, above, below)
    for x in range(count):
        p_out[x] = p3[x]
    last = count - 1

    by_parity(
        "sub",
        mid_a,
        mid_b,
        lambda ref: edge_data(ref, p3, last, last - 1, cx[last], source, cx, layers, w),
        lambda ref: edge_data(ref, p3, 0, 1, cx[1], source, cx, layers, w),
    )


def second_whole(
    src, tx, ty, tz, got_a, got_b, p_in, mid_a, mid_b, p_out, above, below, p_above, p_below
):
    count = src.shape[1]
    sort_pair((got_a, got_b), above, below)
    sort_pair((mid_a, mid_b), p_above, p_below)
    source, cx, layers, w = whole_setup(src, tx, ty, tz, above, below)
    has_bot, has_top, _, _ = flags()
    layers[count] = Layer(above[4], above[5], has_bot, has_top)
    w[count] = above[3]
    p3 = {x: p_in[x] for x in range(count)}
    p6 = three_passes(p3, p_above, p_below, source, cx, layers, w, count)
    for x in range(count):
        p_out[x] = p6[x]


def finish_kernel(whole, thin, mortar, *rest):
    parts = rest[:-5]
    p_out, m_out, merged, piece, sems = rest[-5:]
    total = mortar[...] + MORTAR_STEP * sum(part[...] for part in parts)
    columns = piece.shape[1]
    shift = total.shape[1] - lax.axis_index("sub") * columns
    piece[...] = pltpu.roll(total, lax.rem(shift, total.shape[1]), 1)[:, 0:columns]
    copies = [pltpu.make_async_copy(piece, m_out, sems.at[0])]
    copies[0].start()
    count, rows, cells = whole.shape
    cols = lax.broadcasted_iota(jnp.int32, (rows, cells), 1)
    face = (cols < PASSES) | (cols >= cells - PASSES)
    each = cells // SPAN
    for start in range(0, count, each):
        stop = min(start + each, count)
        here = [thin[x] for x in range(start, stop)]
        if (stop - start) * SPAN < cells:
            here.append(jnp.zeros((cells - (stop - start) * SPAN, rows), F32))
        back = jnp.concatenate(here, axis=0).T
        for x in range(start, stop):
            shift = (cells - (x - start) * SPAN - SLAB) % cells
            merged[x] = jnp.where(face, pltpu.roll(back, shift, 1), whole[x])
            copies.append(pltpu.make_async_copy(merged.at[x], p_out.at[0, x], sems.at[x + 1]))
            copies[-1].start()
    for copy in copies:
        copy.wait()


def call(kernel, outs, args, scratch=(), copies=0, source=pltpu.VMEM, target=pltpu.VMEM):
    args = [pltpu.with_memory_space_constraint(a, source) for a in args]
    return pl.pallas_call(
        kernel,
        out_shape=[target(shape, F32) for shape in outs],
        in_specs=[pl.BlockSpec(memory_space=source)] * len(args),
        out_specs=[pl.BlockSpec(memory_space=target)] * len(outs),
        scratch_shapes=[pltpu.VMEM(shape, F32) for shape in scratch]
        + ([pltpu.SemaphoreType.DMA((copies,))] if copies else []),
        compiler_params=pltpu.CompilerParams(vmem_limit_bytes=16 << 20),
    )(*args)


def sub_swaps(blocks, subs):
    flat = lambda b, s: b * subs + s
    first = [(flat(b, s), flat(b, s ^ 1)) for b in range(blocks) for s in range(subs)]
    second = []
    for b in range(blocks):
        for s in range(subs):
            other = s + 1 if s % 2 else s - 1
            inside = 0 <= other < subs
            second.append((flat(b, s), flat(b, other) if inside else flat(b ^ 1, s)))
    return first, second


def work(source, trans_x, trans_y, trans_z, mortar_bot, mortar_top):
    count, rows, cells = source.shape[1:]
    width = mortar_bot.shape[3]
    subs = lax.axis_size("sub")
    blocks = lax.axis_size("block")
    assert subs % 2 == 0 and blocks % 2 == 0 and count > HALO
    names = ("block", "sub")
    pair_one, pair_two = sub_swaps(blocks, subs)

    def trade(a, b):
        first = lax.ppermute(a, names, pair_one)
        return first, lax.ppermute(b, names, pair_two)

    face = (rows, cells)
    kept = count * ITEMS
    slab = (SPAN, rows)

    def everyone(value):
        if subs > DIRECT:
            return [lax.psum(value, "sub")]
        parts = [value]
        for k in range(subs - 1, 0, -1):
            parts.append(lax.ppermute(value, "sub", [(i, i ^ k) for i in range(subs)]))
        return parts

    *coeffs, slabs, near_a, near_b = call(
        pack_kernel,
        [source.shape] * 4 + [(kept,) + slab] + [(EDGE,) + slab] * 2,
        (source, trans_x, trans_y, trans_z),
        copies=4,
        source=pltpu.HBM,
    )
    near = trade(near_a, near_b)
    edges = call(edge_kernel, [(EDGE,) + face] * 2, coeffs)
    edges = trade(*edges)
    fixed = (slabs, mortar_bot, mortar_top)
    third, known, share_a, share_b = call(
        first_thin,
        [(count,) + slab, (count + 2, 5) + slab] + [(1, width)] * 2,
        fixed + near,
        [(EDGE,) + slab] * 2,
    )
    block_one = [(b, b ^ 1) for b in range(blocks)]
    block_two = [(b, (b + 1 if b % 2 else b - 1) % blocks) for b in range(blocks)]
    other_a = lax.ppermute(share_a, "block", block_one)
    other_b = lax.ppermute(share_b, "block", block_two)
    jumps = jnp.concatenate([share_a + other_a, share_b + other_b], axis=0)
    parts = everyone(jumps)
    whole, mid_a, mid_b = call(
        first_whole,
        [(count,) + face] + [(MIDDLE,) + face] * 2,
        tuple(coeffs) + edges,
        [(EDGE,) + face] * 2,
    )
    middle = trade(mid_a, mid_b)
    data, edge_a, edge_b, mortar = call(
        face_kernel,
        [(2 * count, rows)] + [(MIDDLE,) + slab] * 2 + [(1, width)],
        fixed + (known, third) + tuple(parts),
    )
    got = trade(edge_a, edge_b)
    slab_out, cbot, ctop = call(
        second_thin,
        [(count,) + slab] + [(1, width)] * 2,
        fixed + (known, third, data) + got,
        [(MIDDLE,) + slab] * 2,
    )
    upper = lax.ppermute(cbot, "block", [((b + 1) % blocks, b) for b in range(blocks)])
    parts = everyone(ctop + upper)
    (whole,) = call(
        second_whole,
        [(count,) + face],
        tuple(coeffs) + edges + (whole,) + middle,
        [(EDGE,) + face] * 2 + [(MIDDLE,) + face] * 2,
    )
    columns = width // subs
    return call(
        finish_kernel,
        [source.shape, (1, columns)],
        (whole, slab_out, mortar) + tuple(parts),
        [(count,) + face, (1, columns)],
        copies=count + 1,
        target=pltpu.HBM,
    )


def solution(mesh):
    spec = P("block", "sub", None, None)
    return jax.shard_map(
        work,
        mesh=mesh,
        in_specs=(spec,) * 6,
        out_specs=(spec, P("block", "sub")),
        check_vma=False,
    )
```

```python
import jax
import jax.numpy as jnp
from jax import lax
from jax.experimental import pallas as pl
from jax.experimental.pallas import tpu as pltpu
from jax.sharding import PartitionSpec as P


PASSES = 3
RELAX = 0.8
KEEP = 1.0 - RELAX
MORTAR_STEP = 0.05
F32 = jnp.float32
EDGE = 6
MIDDLE = 3
HALO = 2
SLAB = 8
SPAN = 2 * SLAB
DIRECT = 4
ITEMS = 5


def prev(v, axis):
    return pltpu.roll(v, 1, axis)


def following(v, axis):
    return pltpu.roll(v, v.shape[axis] - 1, axis)


class Layer:
    def __init__(self, trans_y, trans_z, has_bot, has_top):
        rows = lax.broadcasted_iota(jnp.int32, trans_y.shape, 0)
        self.cy = jnp.where(rows > 0, trans_y, 0.0)
        self.cz, self.zsum = along_z(trans_z, has_bot, has_top)
        self.diag = self.cy + following(self.cy, 0) + self.zsum

    def around(self, p):
        return (
            self.cy * prev(p, 0)
            + following(self.cy * p, 0)
            + self.cz * prev(p, 1)
            + following(self.cz * p, 1)
        )


def along_z(trans_z, has_bot, has_top):
    cols = lax.broadcasted_iota(jnp.int32, trans_z.shape, 1)
    first = cols == 0
    last = cols == trans_z.shape[1] - 1
    cz = jnp.where(first, 0.0, trans_z)
    ends = jnp.where(first, trans_z * has_bot, jnp.where(last, trans_z * has_top, 0.0))
    return cz, cz + following(cz, 1) + ends


class Thin:
    def __init__(self, trans_y, trans_z, zsum, has_bot, has_top):
        rows = lax.broadcasted_iota(jnp.int32, trans_y.shape, 0)
        cols = lax.broadcasted_iota(jnp.int32, trans_y.shape, 1)
        self.cy = jnp.where(cols > 0, trans_y, 0.0)
        self.cz = jnp.where(rows == SLAB, 0.0, trans_z)
        top = jnp.where(rows == SLAB - 1, trans_z * has_top, 0.0)
        self.face = jnp.where(rows == SLAB, trans_z * has_bot, top)
        self.diag = self.cy + following(self.cy, 1) + zsum

    def around(self, p):
        return (
            self.cy * prev(p, 1)
            + following(self.cy * p, 1)
            + self.cz * prev(p, 0)
            + following(self.cz * p, 0)
        )


def flags():
    block = lax.axis_index("block")
    sub = lax.axis_index("sub")
    has_bot = (block > 0).astype(F32)
    has_top = (block < lax.axis_size("block") - 1).astype(F32)
    has_below = (sub > 0).astype(F32)
    has_above = (sub < lax.axis_size("sub") - 1).astype(F32)
    return has_bot, has_top, has_below, has_above


def by_parity(axis, first, second, upward, downward):
    even = lax.rem(lax.axis_index(axis), 2) == 0

    @pl.when(even)
    def _():
        upward(first)
        downward(second)

    @pl.when(jnp.logical_not(even))
    def _():
        upward(second)
        downward(first)


def sort_pair(pair, above, below):
    def take_above(ref):
        above[...] = ref[...]

    def take_below(ref):
        below[...] = ref[...]

    by_parity("sub", *pair, take_above, take_below)


def pack_kernel(src, tx, ty, tz, src_v, tx_v, ty_v, tz_v, slabs, out_a, out_b, sems):
    count, rows, cells = src_v.shape[1:]
    copies = [
        pltpu.make_async_copy(here, there, sems.at[i])
        for i, (here, there) in enumerate(
            ((tz, tz_v), (tx, tx_v), (src, src_v), (ty, ty_v))
        )
    ]
    for copy in copies:
        copy.start()
    for copy in copies:
        copy.wait()
    has_bot, has_top, has_below, _ = flags()
    slot = lax.broadcasted_iota(jnp.int32, (rows, cells), 1) // SPAN
    each = cells // SPAN
    packed, done = jnp.zeros((rows, cells), F32), 0

    def flush(packed, done):
        turned = packed.T
        start = (done - 1) // each * each
        for k in range(start, done):
            slabs[k] = turned[(k - start) * SPAN : (k - start + 1) * SPAN]

    for x in range(count):
        zsum = along_z(tz_v[0, x], has_bot, has_top)[1]
        for item in (tx_v[0, x], src_v[0, x], ty_v[0, x], tz_v[0, x], zsum):
            j = done % each
            turned = pltpu.roll(item, (SPAN * j + SLAB) % cells, 1)
            packed = jnp.where(slot == j, turned, packed)
            done += 1
            if done % each == 0 or done == count * ITEMS:
                flush(packed, done)

    def item(which, x):
        return slabs[x * ITEMS + which]

    def make(x):
        return Thin(item(2, x), item(3, x), item(4, x), has_bot, has_top)

    p_low, q_low, w_low = edge_parts(item, make, has_below)
    top = count - 1
    p_top = RELAX * item(1, top - 1) / (make(top - 1).diag + item(0, top - 1) + item(0, top))

    def upward(ref):
        values = (item(0, top), p_top, item(1, top), item(4, top), item(2, top), item(3, top))
        for i, v in enumerate(values):
            ref[i] = v

    def downward(ref):
        values = (item(0, 0), p_low, q_low, w_low, item(2, 0), item(3, 0))
        for i, v in enumerate(values):
            ref[i] = v

    by_parity("sub", out_a, out_b, upward, downward)


def edge_parts(items, make, has_below):
    tx, src = (lambda x: items(0, x)), (lambda x: items(1, x))
    low = make(0)
    w_low = RELAX / (low.diag + tx(0) * has_below + tx(1))
    p_low = w_low * src(0)
    p_next = RELAX * src(1) / (make(1).diag + tx(1) + tx(2))
    q_low = KEEP * p_low + w_low * (src(0) + tx(1) * p_next + low.around(p_low))
    return p_low, q_low, w_low


def first_three(count, source, cx, layers, w, above, below):
    p1 = {x: w[x] * source[x] for x in range(-1, count)}
    p1[-2] = below[1]
    p1[count] = above[1]
    p2 = thin_pass(p1, source, cx, layers, w, -1, count)
    p2[count] = above[2] + above[3] * cx[count] * p1[count - 1]
    return thin_pass(p2, source, cx, layers, w, 0, count)


def thin_setup(slabs, above, below):
    count = slabs.shape[0] // ITEMS
    has_bot, has_top, has_below, has_above = flags()
    cx = {x: slabs[x * ITEMS] for x in range(1, count)}
    cx[-1] = below[0]
    cx[0] = slabs[0] * has_below
    cx[count] = above[0] * has_above
    source = {x: slabs[x * ITEMS + 1] for x in range(count)}
    source[-1] = below[2]
    layers = {
        x: Thin(*(slabs[x * ITEMS + i] for i in (2, 3, 4)), has_bot, has_top)
        for x in range(count)
    }
    layers[-1] = Thin(below[4], below[5], below[3], has_bot, has_top)
    layers[count] = Thin(above[4], above[5], above[3], has_bot, has_top)
    w = {x: RELAX / (layers[x].diag + cx[x] + cx[x + 1]) for x in range(-1, count)}
    w[count] = above[3]
    return source, cx, layers, w


def thin_pass(p, rhs, cx, layers, weight, low, high):
    return {
        x: KEEP * p[x]
        + weight[x] * (rhs[x] + cx[x] * p[x - 1] + cx[x + 1] * p[x + 1] + layers[x].around(p[x]))
        for x in range(low, high)
    }


def edge_data(ref, p, x, beyond, link, rhs, cx, layers, weight):
    ref[0] = p[x]
    ref[1] = KEEP * p[x] + weight[x] * (rhs[x] + link * p[beyond] + layers[x].around(p[x]))
    step = thin_pass(p, rhs, cx, layers, weight, beyond, beyond + 1)
    ref[2] = rhs[x] + link * step[beyond]


def three_passes(p, above, below, rhs, cx, layers, weight, count):
    sides = ((count, count - 1, cx[count], above), (-1, 0, cx[0], below))
    for x, _, _, got in sides:
        p[x] = got[0]
    after = thin_pass(p, rhs, cx, layers, weight, 0, count)
    for x, near, link, got in sides:
        after[x] = got[1] + weight[x] * link * p[near]
    last = thin_pass(after, rhs, cx, layers, weight, 0, count)
    for x, near, link, got in sides:
        last[x] = KEEP * after[x] + weight[x] * (
            got[2] + link * after[near] + layers[x].around(after[x])
        )
    return thin_pass(last, rhs, cx, layers, weight, 0, count)


def trace(flux, plane, basis):
    columns = jnp.concatenate([f[plane : plane + 1] for f in flux], axis=0)
    fill = jnp.zeros((SLAB - len(flux), flux[0].shape[1]), F32)
    columns = jnp.concatenate([columns, fill], axis=0).T
    total = sum(columns[:, x : x + 1] * basis[0, x] for x in range(len(flux)))
    return jnp.sum(total, axis=0, keepdims=True)


def share_of(flux, bot, top, first, second):
    def to_above(ref):
        if ref is not None:
            ref[...] = trace(flux, SLAB - 1, top)

    def to_below(ref):
        if ref is not None:
            ref[...] = trace(flux, SLAB, bot)

    by_parity("block", first, second, to_above, to_below)


def first_thin(slabs, bot, top, got_a, got_b, p_out, kept, share, above, below):
    count = bot.shape[1]
    sort_pair((got_a, got_b), above, below)
    source, cx, layers, w = thin_setup(slabs, above, below)
    p = first_three(count, source, cx, layers, w, above, below)
    for x in range(count):
        p_out[x] = p[x]
    share_of([layers[x].face * p[x] for x in range(count)], bot, top, None, share)
    for x in range(-1, count + 1):
        for i, v in enumerate((cx[x], w[x], layers[x].cy, layers[x].cz, layers[x].face)):
            kept[x + 1, i] = v


def other_share(bot, top, kept, p_in, share):
    flux = [kept[x + 1, 4] * p_in[x] for x in range(bot.shape[1])]
    share_of(flux, bot, top, share, None)


class Kept(Thin):
    def __init__(self, kept, x):
        self.cy, self.cz, self.face = (kept[x + 1, i] for i in (2, 3, 4))


def thin_again(slabs, kept):
    count = slabs.shape[0] // ITEMS
    span = range(-1, count + 1)
    cx = {x: kept[x + 1, 0] for x in span}
    w = {x: kept[x + 1, 1] for x in span}
    layers = {x: Kept(kept, x) for x in span}
    return {x: slabs[x * ITEMS + 1] for x in range(count)}, cx, layers, w


def with_faces(source, layers, data, count):
    known = {}
    for x in range(count):
        planes = lax.broadcasted_iota(jnp.int32, source[x].shape, 0)
        known[x] = jnp.where(planes == SLAB, data[x : x + 1], data[count + x : count + x + 1])
    return known, {x: source[x] + layers[x].face * known[x] for x in range(count)}


def face_kernel(slabs, bot, top, kept, p_in, *rest):
    parts = rest[:-4]
    data_out, edge_a, edge_b, mortar_out = rest[-4:]
    count = bot.shape[1]
    jumps = MORTAR_STEP * sum(part[...] for part in parts)
    even = lax.rem(lax.axis_index("block"), 2) == 0
    own = jnp.where(even, jumps[0:1], jumps[1:2])
    under = jnp.where(even, jumps[1:2], jumps[0:1])
    mortar_out[...] = own
    columns = [
        jnp.sum(ref[0, x] * values, axis=1, keepdims=True)
        for ref, values in ((bot, under), (top, own))
        for x in range(count)
    ]
    data = jnp.concatenate(columns, axis=1).T
    data_out[...] = data
    source, cx, layers, w = thin_again(slabs, kept)
    rhs = with_faces(source, layers, data, count)[1]
    p = {x: p_in[x] for x in range(count)}
    last = count - 1
    by_parity(
        "sub",
        edge_a,
        edge_b,
        lambda ref: edge_data(ref, p, last, last - 1, cx[last], rhs, cx, layers, w),
        lambda ref: edge_data(ref, p, 0, 1, cx[1], rhs, cx, layers, w),
    )


def second_thin(
    slabs, bot, kept, p_in, data, edge_a, edge_b,
    p_out, flux_out, cbot_out, edge_above, edge_below,
):
    count = bot.shape[1]
    sort_pair((edge_a, edge_b), edge_above, edge_below)
    source, cx, layers, w = thin_again(slabs, kept)
    known, rhs = with_faces(source, layers, data, count)
    p = {x: p_in[x] for x in range(count)}
    p = three_passes(p, edge_above, edge_below, rhs, cx, layers, w, count)
    for x in range(count):
        p_out[x] = p[x]
    flux = [layers[x].face * (p[x] - known[x]) for x in range(count)]
    cbot_out[...] = trace(flux, SLAB, bot)
    for x in range(count):
        flux_out[x] = flux[x]


def top_share(top, flux, ctop_out):
    ctop_out[...] = trace([flux[x] for x in range(top.shape[1])], SLAB - 1, top)


def edge_kernel(src, tx, ty, tz, out_a, out_b):
    count = src.shape[1]
    has_bot, has_top, has_below, _ = flags()

    def make(x):
        return Layer(ty[0, x], tz[0, x], has_bot, has_top)

    p_low, q_low, w_low = edge_parts(lambda which, x: (tx, src)[which][0, x], make, has_below)
    top = count - 1
    p_top = RELAX * src[0, top - 1] / (make(top - 1).diag + tx[0, top - 1] + tx[0, top])

    def upward(ref):
        for i, v in enumerate((tx[0, top], p_top, src[0, top], src[0, top], ty[0, top], tz[0, top])):
            ref[i] = v

    def downward(ref):
        for i, v in enumerate((tx[0, 0], p_low, q_low, w_low, ty[0, 0], tz[0, 0])):
            ref[i] = v

    by_parity("sub", out_a, out_b, upward, downward)


def whole_setup(src, tx, ty, tz, above, below):
    count = src.shape[1]
    has_bot, has_top, has_below, has_above = flags()
    cx = {x: tx[0, x] for x in range(1, count)}
    cx[-1] = below[0]
    cx[0] = tx[0, 0] * has_below
    cx[count] = above[0] * has_above
    source = {x: src[0, x] for x in range(count)}
    source[-1] = below[2]
    layers = {x: Layer(ty[0, x], tz[0, x], has_bot, has_top) for x in range(count)}
    layers[-1] = Layer(below[4], below[5], has_bot, has_top)
    weight = {x: RELAX / (layers[x].diag + cx[x] + cx[x + 1]) for x in range(-1, count)}
    return source, cx, layers, weight


def first_whole(src, tx, ty, tz, got_a, got_b, p_out, mid_a, mid_b, above, below):
    count = src.shape[1]
    sort_pair((got_a, got_b), above, below)
    source, cx, layers, w = whole_setup(src, tx, ty, tz, above, below)
    p3 = first_three(count, source, cx, layers, w, above, below)
    for x in range(count):
        p_out[x] = p3[x]
    last = count - 1

    by_parity(
        "sub",
        mid_a,
        mid_b,
        lambda ref: edge_data(ref, p3, last, last - 1, cx[last], source, cx, layers, w),
        lambda ref: edge_data(ref, p3, 0, 1, cx[1], source, cx, layers, w),
    )


def second_whole(
    src, tx, ty, tz, got_a, got_b, p_in, mid_a, mid_b, thin,
    p_out, above, below, p_above, p_below,
):
    count, rows, cells = src.shape[1:]
    sort_pair((got_a, got_b), above, below)
    sort_pair((mid_a, mid_b), p_above, p_below)
    source, cx, layers, w = whole_setup(src, tx, ty, tz, above, below)
    has_bot, has_top, _, _ = flags()
    layers[count] = Layer(above[4], above[5], has_bot, has_top)
    w[count] = above[3]
    p3 = {x: p_in[x] for x in range(count)}
    p6 = three_passes(p3, p_above, p_below, source, cx, layers, w, count)
    cols = lax.broadcasted_iota(jnp.int32, (rows, cells), 1)
    face = (cols < PASSES) | (cols >= cells - PASSES)
    each = cells // SPAN
    for start in range(0, count, each):
        stop = min(start + each, count)
        here = [thin[x] for x in range(start, stop)]
        if (stop - start) * SPAN < cells:
            here.append(jnp.zeros((cells - (stop - start) * SPAN, rows), F32))
        back = jnp.concatenate(here, axis=0).T
        for x in range(start, stop):
            shift = (cells - (x - start) * SPAN - SLAB) % cells
            p_out[0, x] = jnp.where(face, pltpu.roll(back, shift, 1), p6[x])


def finish_kernel(merged, mortar, *rest):
    parts = rest[:-4]
    p_out, m_out, piece, sems = rest[-4:]
    whole = pltpu.make_async_copy(merged, p_out, sems.at[0])
    whole.start()
    total = mortar[...] + MORTAR_STEP * sum(part[...] for part in parts)
    columns = piece.shape[1]
    shift = total.shape[1] - lax.axis_index("sub") * columns
    piece[...] = pltpu.roll(total, lax.rem(shift, total.shape[1]), 1)[:, 0:columns]
    copy = pltpu.make_async_copy(piece, m_out, sems.at[1])
    copy.start()
    whole.wait()
    copy.wait()


def call(kernel, outs, args, scratch=(), copies=0, source=pltpu.VMEM, target=pltpu.VMEM):
    args = [pltpu.with_memory_space_constraint(a, source) for a in args]
    return pl.pallas_call(
        kernel,
        out_shape=[target(shape, F32) for shape in outs],
        in_specs=[pl.BlockSpec(memory_space=source)] * len(args),
        out_specs=[pl.BlockSpec(memory_space=target)] * len(outs),
        scratch_shapes=[pltpu.VMEM(shape, F32) for shape in scratch]
        + ([pltpu.SemaphoreType.DMA((copies,))] if copies else []),
        compiler_params=pltpu.CompilerParams(vmem_limit_bytes=16 << 20),
    )(*args)


def sub_swaps(blocks, subs):
    flat = lambda b, s: b * subs + s
    first = [(flat(b, s), flat(b, s ^ 1)) for b in range(blocks) for s in range(subs)]
    second = []
    for b in range(blocks):
        for s in range(subs):
            other = s + 1 if s % 2 else s - 1
            inside = 0 <= other < subs
            second.append((flat(b, s), flat(b, other) if inside else flat(b ^ 1, s)))
    return first, second


def work(source, trans_x, trans_y, trans_z, mortar_bot, mortar_top):
    count, rows, cells = source.shape[1:]
    width = mortar_bot.shape[3]
    subs = lax.axis_size("sub")
    blocks = lax.axis_size("block")
    assert subs % 2 == 0 and blocks % 2 == 0 and count > HALO
    names = ("block", "sub")
    pair_one, pair_two = sub_swaps(blocks, subs)

    def trade(a, b):
        first = lax.ppermute(a, names, pair_one)
        return first, lax.ppermute(b, names, pair_two)

    face = (rows, cells)
    kept = count * ITEMS
    slab = (SPAN, rows)

    def everyone(value):
        if subs > DIRECT:
            return [lax.psum(value, "sub")]
        parts = [value]
        for k in range(subs - 1, 0, -1):
            parts.append(lax.ppermute(value, "sub", [(i, i ^ k) for i in range(subs)]))
        return parts

    *coeffs, slabs, near_a, near_b = call(
        pack_kernel,
        [source.shape] * 4 + [(kept,) + slab] + [(EDGE,) + slab] * 2,
        (source, trans_x, trans_y, trans_z),
        copies=4,
        source=pltpu.HBM,
    )
    near = trade(near_a, near_b)
    edges = call(edge_kernel, [(EDGE,) + face] * 2, coeffs)
    edges = trade(*edges)
    fixed = (slabs, mortar_bot, mortar_top)
    third, known, share_b = call(
        first_thin,
        [(count,) + slab, (count + 2, 5) + slab, (1, width)],
        fixed + near,
        [(EDGE,) + slab] * 2,
    )
    block_one = [(b, b ^ 1) for b in range(blocks)]
    block_two = [(b, (b + 1 if b % 2 else b - 1) % blocks) for b in range(blocks)]
    other_b = lax.ppermute(share_b, "block", block_two)
    (share_a,) = call(other_share, [(1, width)], fixed[1:] + (known, third))
    other_a = lax.ppermute(share_a, "block", block_one)
    jumps = jnp.concatenate([share_a + other_a, share_b + other_b], axis=0)
    parts = everyone(jumps)
    whole, mid_a, mid_b = call(
        first_whole,
        [(count,) + face] + [(MIDDLE,) + face] * 2,
        tuple(coeffs) + edges,
        [(EDGE,) + face] * 2,
    )
    middle = trade(mid_a, mid_b)
    data, edge_a, edge_b, mortar = call(
        face_kernel,
        [(2 * count, rows)] + [(MIDDLE,) + slab] * 2 + [(1, width)],
        fixed + (known, third) + tuple(parts),
    )
    got = trade(edge_a, edge_b)
    slab_out, flux, cbot = call(
        second_thin,
        [(count,) + slab] * 2 + [(1, width)],
        fixed[:2] + (known, third, data) + got,
        [(MIDDLE,) + slab] * 2,
    )
    (ctop,) = call(top_share, [(1, width)], (mortar_top, flux))
    upper = lax.ppermute(cbot, "block", [((b + 1) % blocks, b) for b in range(blocks)])
    parts = everyone(ctop + upper)
    (whole,) = call(
        second_whole,
        [source.shape],
        tuple(coeffs) + edges + (whole,) + middle + (slab_out,),
        [(EDGE,) + face] * 2 + [(MIDDLE,) + face] * 2,
    )
    columns = width // subs
    return call(
        finish_kernel,
        [source.shape, (1, columns)],
        (whole, mortar) + tuple(parts),
        [(1, columns)],
        copies=2,
        target=pltpu.HBM,
    )


def solution(mesh):
    spec = P("block", "sub", None, None)
    return jax.shard_map(
        work,
        mesh=mesh,
        in_specs=(spec,) * 6,
        out_specs=(spec, P("block", "sub")),
        check_vma=False,
    )
```

```python
import jax
import jax.numpy as jnp
from jax import lax
from jax.experimental import pallas as pl
from jax.experimental.pallas import tpu as pltpu
from jax.sharding import PartitionSpec as P


PASSES = 3
RELAX = 0.8
KEEP = 1.0 - RELAX
MORTAR_STEP = 0.05
F32 = jnp.float32
EDGE = 6
MIDDLE = 3
HALO = 2
SLAB = 8
SPAN = 2 * SLAB
DIRECT = 4
ITEMS = 5


def prev(v, axis):
    return pltpu.roll(v, 1, axis)


def following(v, axis):
    return pltpu.roll(v, v.shape[axis] - 1, axis)


class Layer:
    def __init__(self, trans_y, trans_z, has_bot, has_top):
        rows = lax.broadcasted_iota(jnp.int32, trans_y.shape, 0)
        self.cy = jnp.where(rows > 0, trans_y, 0.0)
        self.cz, self.zsum = along_z(trans_z, has_bot, has_top)
        self.diag = self.cy + following(self.cy, 0) + self.zsum

    def around(self, p):
        return (
            self.cy * prev(p, 0)
            + following(self.cy * p, 0)
            + self.cz * prev(p, 1)
            + following(self.cz * p, 1)
        )


def along_z(trans_z, has_bot, has_top):
    cols = lax.broadcasted_iota(jnp.int32, trans_z.shape, 1)
    first = cols == 0
    last = cols == trans_z.shape[1] - 1
    cz = jnp.where(first, 0.0, trans_z)
    ends = jnp.where(first, trans_z * has_bot, jnp.where(last, trans_z * has_top, 0.0))
    return cz, cz + following(cz, 1) + ends


class Thin:
    def __init__(self, trans_y, trans_z, z_next, has_bot, has_top):
        rows = lax.broadcasted_iota(jnp.int32, trans_y.shape, 0)
        cols = lax.broadcasted_iota(jnp.int32, trans_y.shape, 1)
        self.cy = jnp.where(cols > 0, trans_y, 0.0)
        self.cz = jnp.where(rows == SLAB, 0.0, trans_z)
        top = jnp.where(rows == SLAB - 1, trans_z * has_top, 0.0)
        self.face = jnp.where(rows == SLAB, trans_z * has_bot, top)
        after = jnp.where(rows == SLAB - 1, 0.0, z_next)
        self.diag = self.cy + following(self.cy, 1) + self.cz + after + self.face

    def around(self, p):
        return (
            self.cy * prev(p, 1)
            + following(self.cy * p, 1)
            + self.cz * prev(p, 0)
            + following(self.cz * p, 0)
        )


def flags():
    block = lax.axis_index("block")
    sub = lax.axis_index("sub")
    has_bot = (block > 0).astype(F32)
    has_top = (block < lax.axis_size("block") - 1).astype(F32)
    has_below = (sub > 0).astype(F32)
    has_above = (sub < lax.axis_size("sub") - 1).astype(F32)
    return has_bot, has_top, has_below, has_above


def by_parity(axis, first, second, upward, downward):
    even = lax.rem(lax.axis_index(axis), 2) == 0

    @pl.when(even)
    def _():
        upward(first)
        downward(second)

    @pl.when(jnp.logical_not(even))
    def _():
        upward(second)
        downward(first)


def sort_pair(pair, above, below):
    def take_above(ref):
        above[...] = ref[...]

    def take_below(ref):
        below[...] = ref[...]

    by_parity("sub", *pair, take_above, take_below)


def pack_kernel(src, tx, ty, tz, src_v, tx_v, ty_v, tz_v, slabs, out_a, out_b, sems):
    count, rows, cells = src_v.shape[1:]
    copies = [
        pltpu.make_async_copy(here, there, sems.at[i])
        for i, (here, there) in enumerate(
            ((tz, tz_v), (tx, tx_v), (src, src_v), (ty, ty_v))
        )
    ]
    for copy in copies:
        copy.start()
    for copy in copies:
        copy.wait()
    has_bot, has_top, has_below, _ = flags()
    slot = lax.broadcasted_iota(jnp.int32, (rows, cells), 1) // SPAN
    each = cells // SPAN
    packed, done = jnp.zeros((rows, cells), F32), 0

    def flush(packed, done):
        turned = packed.T
        start = (done - 1) // each * each
        for k in range(start, done):
            slabs[k] = turned[(k - start) * SPAN : (k - start + 1) * SPAN]

    for x in range(count):
        for which, ref in enumerate((tx_v, src_v, ty_v, tz_v, tz_v)):
            j = done % each
            ahead = which // 4
            turned = pltpu.roll(ref[0, x], (SPAN * j + SLAB - ahead) % cells, 1)
            packed = jnp.where(slot == j, turned, packed)
            done += 1
            if done % each == 0 or done == count * ITEMS:
                flush(packed, done)

    def item(which, x):
        return slabs[x * ITEMS + which]

    def make(x):
        return Thin(item(2, x), item(3, x), item(4, x), has_bot, has_top)

    p_low, q_low, w_low = edge_parts(item, make, has_below)
    top = count - 1
    p_top = RELAX * item(1, top - 1) / (make(top - 1).diag + item(0, top - 1) + item(0, top))

    def upward(ref):
        values = (item(0, top), p_top, item(1, top), make(top).diag, item(2, top), item(3, top))
        for i, v in enumerate(values):
            ref[i] = v

    def downward(ref):
        values = (item(0, 0), p_low, q_low, w_low, item(2, 0), item(3, 0))
        for i, v in enumerate(values):
            ref[i] = v

    by_parity("sub", out_a, out_b, upward, downward)


def edge_parts(items, make, has_below):
    tx, src = (lambda x: items(0, x)), (lambda x: items(1, x))
    low = make(0)
    w_low = RELAX / (low.diag + tx(0) * has_below + tx(1))
    p_low = w_low * src(0)
    p_next = RELAX * src(1) / (make(1).diag + tx(1) + tx(2))
    q_low = KEEP * p_low + w_low * (src(0) + tx(1) * p_next + low.around(p_low))
    return p_low, q_low, w_low


def first_three(count, source, cx, layers, w, above, below):
    p1 = {x: w[x] * source[x] for x in range(-1, count)}
    p1[-2] = below[1]
    p1[count] = above[1]
    p2 = thin_pass(p1, source, cx, layers, w, -1, count)
    p2[count] = above[2] + above[3] * cx[count] * p1[count - 1]
    return thin_pass(p2, source, cx, layers, w, 0, count)


def thin_setup(slabs, above, below):
    count = slabs.shape[0] // ITEMS
    has_bot, has_top, has_below, has_above = flags()
    cx = {x: slabs[x * ITEMS] for x in range(1, count)}
    cx[-1] = below[0]
    cx[0] = slabs[0] * has_below
    cx[count] = above[0] * has_above
    source = {x: slabs[x * ITEMS + 1] for x in range(count)}
    source[-1] = below[2]
    layers = {
        x: Thin(*(slabs[x * ITEMS + i] for i in (2, 3, 4)), has_bot, has_top)
        for x in range(count)
    }
    layers[-1] = Thin(below[4], below[5], below[3], has_bot, has_top)
    layers[-1].diag = below[3]
    layers[count] = Thin(above[4], above[5], above[3], has_bot, has_top)
    w = {x: RELAX / (layers[x].diag + cx[x] + cx[x + 1]) for x in range(-1, count)}
    w[count] = above[3]
    return source, cx, layers, w


def thin_pass(p, rhs, cx, layers, weight, low, high):
    return {
        x: KEEP * p[x]
        + weight[x] * (rhs[x] + cx[x] * p[x - 1] + cx[x + 1] * p[x + 1] + layers[x].around(p[x]))
        for x in range(low, high)
    }


def edge_data(ref, p, x, beyond, link, rhs, cx, layers, weight):
    ref[0] = p[x]
    ref[1] = KEEP * p[x] + weight[x] * (rhs[x] + link * p[beyond] + layers[x].around(p[x]))
    step = thin_pass(p, rhs, cx, layers, weight, beyond, beyond + 1)
    ref[2] = rhs[x] + link * step[beyond]


def three_passes(p, above, below, rhs, cx, layers, weight, count):
    sides = ((count, count - 1, cx[count], above), (-1, 0, cx[0], below))
    for x, _, _, got in sides:
        p[x] = got[0]
    after = thin_pass(p, rhs, cx, layers, weight, 0, count)
    for x, near, link, got in sides:
        after[x] = got[1] + weight[x] * link * p[near]
    last = thin_pass(after, rhs, cx, layers, weight, 0, count)
    for x, near, link, got in sides:
        last[x] = KEEP * after[x] + weight[x] * (
            got[2] + link * after[near] + layers[x].around(after[x])
        )
    return thin_pass(last, rhs, cx, layers, weight, 0, count)


def trace(flux, plane, basis):
    rows, width = basis.shape[2:]
    total = 0.0
    for x, f in enumerate(flux):
        turned = jnp.broadcast_to(f[plane : plane + 1], (rows, rows)).T
        total += jnp.concatenate([turned] * (width // rows), axis=1) * basis[0, x]
    return jnp.sum(total, axis=0, keepdims=True)


def share_of(flux, bot, top, first, second):
    def to_above(ref):
        if ref is not None:
            ref[...] = trace(flux, SLAB - 1, top)

    def to_below(ref):
        if ref is not None:
            ref[...] = trace(flux, SLAB, bot)

    by_parity("block", first, second, to_above, to_below)


def first_thin(slabs, bot, top, got_a, got_b, p_out, kept, share, above, below):
    count = bot.shape[1]
    sort_pair((got_a, got_b), above, below)
    source, cx, layers, w = thin_setup(slabs, above, below)
    p = first_three(count, source, cx, layers, w, above, below)
    for x in range(count):
        p_out[x] = p[x]
    share_of([layers[x].face * p[x] for x in range(count)], bot, top, None, share)
    for x in range(-1, count + 1):
        for i, v in enumerate((cx[x], w[x], layers[x].cy, layers[x].cz, layers[x].face)):
            kept[x + 1, i] = v


def other_share(bot, top, kept, p_in, share):
    flux = [kept[x + 1, 4] * p_in[x] for x in range(bot.shape[1])]
    share_of(flux, bot, top, share, None)


class Kept(Thin):
    def __init__(self, kept, x):
        self.cy, self.cz, self.face = (kept[x + 1, i] for i in (2, 3, 4))


def thin_again(slabs, kept):
    count = slabs.shape[0] // ITEMS
    span = range(-1, count + 1)
    cx = {x: kept[x + 1, 0] for x in span}
    w = {x: kept[x + 1, 1] for x in span}
    layers = {x: Kept(kept, x) for x in span}
    return {x: slabs[x * ITEMS + 1] for x in range(count)}, cx, layers, w


def with_faces(source, layers, data, count):
    known = {}
    for x in range(count):
        planes = lax.broadcasted_iota(jnp.int32, source[x].shape, 0)
        known[x] = jnp.where(planes == SLAB, data[x : x + 1], data[count + x : count + x + 1])
    return known, {x: source[x] + layers[x].face * known[x] for x in range(count)}


def face_kernel(slabs, bot, top, kept, p_in, *rest):
    parts = rest[:-4]
    data_out, edge_a, edge_b, mortar_out = rest[-4:]
    count = bot.shape[1]
    jumps = MORTAR_STEP * sum(part[...] for part in parts)
    even = lax.rem(lax.axis_index("block"), 2) == 0
    own = jnp.where(even, jumps[0:1], jumps[1:2])
    under = jnp.where(even, jumps[1:2], jumps[0:1])
    mortar_out[...] = own
    rows, width = bot.shape[2:]
    data = []
    for ref, values in ((bot, under), (top, own)):
        for x in range(count):
            product = ref[0, x] * values
            folded = sum(product[:, i : i + rows] for i in range(0, width, rows))
            data.append(jnp.sum(folded.T, axis=0, keepdims=True))
    data = jnp.concatenate(data, axis=0)
    data_out[...] = data
    source, cx, layers, w = thin_again(slabs, kept)
    rhs = with_faces(source, layers, data, count)[1]
    p = {x: p_in[x] for x in range(count)}
    last = count - 1
    by_parity(
        "sub",
        edge_a,
        edge_b,
        lambda ref: edge_data(ref, p, last, last - 1, cx[last], rhs, cx, layers, w),
        lambda ref: edge_data(ref, p, 0, 1, cx[1], rhs, cx, layers, w),
    )


def second_thin(
    slabs, bot, kept, p_in, data, edge_a, edge_b,
    p_out, flux_out, cbot_out, edge_above, edge_below,
):
    count = bot.shape[1]
    sort_pair((edge_a, edge_b), edge_above, edge_below)
    source, cx, layers, w = thin_again(slabs, kept)
    known, rhs = with_faces(source, layers, data, count)
    p = {x: p_in[x] for x in range(count)}
    p = three_passes(p, edge_above, edge_below, rhs, cx, layers, w, count)
    for x in range(count):
        p_out[x] = p[x]
    flux = [layers[x].face * (p[x] - known[x]) for x in range(count)]
    cbot_out[...] = trace(flux, SLAB, bot)
    for x in range(count):
        flux_out[x] = flux[x]


def top_share(top, flux, ctop_out):
    ctop_out[...] = trace([flux[x] for x in range(top.shape[1])], SLAB - 1, top)


def edge_kernel(src, tx, ty, tz, out_a, out_b):
    count = src.shape[1]
    has_bot, has_top, has_below, _ = flags()

    def make(x):
        return Layer(ty[0, x], tz[0, x], has_bot, has_top)

    p_low, q_low, w_low = edge_parts(lambda which, x: (tx, src)[which][0, x], make, has_below)
    top = count - 1
    p_top = RELAX * src[0, top - 1] / (make(top - 1).diag + tx[0, top - 1] + tx[0, top])

    def upward(ref):
        for i, v in enumerate((tx[0, top], p_top, src[0, top], src[0, top], ty[0, top], tz[0, top])):
            ref[i] = v

    def downward(ref):
        for i, v in enumerate((tx[0, 0], p_low, q_low, w_low, ty[0, 0], tz[0, 0])):
            ref[i] = v

    by_parity("sub", out_a, out_b, upward, downward)


def whole_setup(src, tx, ty, tz, above, below):
    count = src.shape[1]
    has_bot, has_top, has_below, has_above = flags()
    cx = {x: tx[0, x] for x in range(1, count)}
    cx[-1] = below[0]
    cx[0] = tx[0, 0] * has_below
    cx[count] = above[0] * has_above
    source = {x: src[0, x] for x in range(count)}
    source[-1] = below[2]
    layers = {x: Layer(ty[0, x], tz[0, x], has_bot, has_top) for x in range(count)}
    layers[-1] = Layer(below[4], below[5], has_bot, has_top)
    weight = {x: RELAX / (layers[x].diag + cx[x] + cx[x + 1]) for x in range(-1, count)}
    return source, cx, layers, weight


def first_whole(src, tx, ty, tz, got_a, got_b, p_out, mid_a, mid_b, above, below):
    count = src.shape[1]
    sort_pair((got_a, got_b), above, below)
    source, cx, layers, w = whole_setup(src, tx, ty, tz, above, below)
    p3 = first_three(count, source, cx, layers, w, above, below)
    for x in range(count):
        p_out[x] = p3[x]
    last = count - 1

    by_parity(
        "sub",
        mid_a,
        mid_b,
        lambda ref: edge_data(ref, p3, last, last - 1, cx[last], source, cx, layers, w),
        lambda ref: edge_data(ref, p3, 0, 1, cx[1], source, cx, layers, w),
    )


def second_whole(
    src, tx, ty, tz, got_a, got_b, p_in, mid_a, mid_b, thin,
    p_out, above, below, p_above, p_below,
):
    count, rows, cells = src.shape[1:]
    sort_pair((got_a, got_b), above, below)
    sort_pair((mid_a, mid_b), p_above, p_below)
    source, cx, layers, w = whole_setup(src, tx, ty, tz, above, below)
    has_bot, has_top, _, _ = flags()
    layers[count] = Layer(above[4], above[5], has_bot, has_top)
    w[count] = above[3]
    p3 = {x: p_in[x] for x in range(count)}
    p6 = three_passes(p3, p_above, p_below, source, cx, layers, w, count)
    cols = lax.broadcasted_iota(jnp.int32, (rows, cells), 1)
    face = (cols < PASSES) | (cols >= cells - PASSES)
    each = cells // SPAN
    for start in range(0, count, each):
        stop = min(start + each, count)
        here = [thin[x] for x in range(start, stop)]
        if (stop - start) * SPAN < cells:
            here.append(jnp.zeros((cells - (stop - start) * SPAN, rows), F32))
        back = jnp.concatenate(here, axis=0).T
        for x in range(start, stop):
            shift = (cells - (x - start) * SPAN - SLAB) % cells
            p_out[0, x] = jnp.where(face, pltpu.roll(back, shift, 1), p6[x])


def finish_kernel(merged, mortar, *rest):
    parts = rest[:-4]
    p_out, m_out, piece, sems = rest[-4:]
    whole = pltpu.make_async_copy(merged, p_out, sems.at[0])
    whole.start()
    total = mortar[...] + MORTAR_STEP * sum(part[...] for part in parts)
    columns = piece.shape[1]
    shift = total.shape[1] - lax.axis_index("sub") * columns
    piece[...] = pltpu.roll(total, lax.rem(shift, total.shape[1]), 1)[:, 0:columns]
    copy = pltpu.make_async_copy(piece, m_out, sems.at[1])
    copy.start()
    whole.wait()
    copy.wait()


def call(kernel, outs, args, scratch=(), copies=0, source=pltpu.VMEM, target=pltpu.VMEM):
    args = [pltpu.with_memory_space_constraint(a, source) for a in args]
    return pl.pallas_call(
        kernel,
        out_shape=[target(shape, F32) for shape in outs],
        in_specs=[pl.BlockSpec(memory_space=source)] * len(args),
        out_specs=[pl.BlockSpec(memory_space=target)] * len(outs),
        scratch_shapes=[pltpu.VMEM(shape, F32) for shape in scratch]
        + ([pltpu.SemaphoreType.DMA((copies,))] if copies else []),
        compiler_params=pltpu.CompilerParams(vmem_limit_bytes=16 << 20),
    )(*args)


def sub_swaps(blocks, subs):
    flat = lambda b, s: b * subs + s
    first = [(flat(b, s), flat(b, s ^ 1)) for b in range(blocks) for s in range(subs)]
    second = []
    for b in range(blocks):
        for s in range(subs):
            other = s + 1 if s % 2 else s - 1
            inside = 0 <= other < subs
            second.append((flat(b, s), flat(b, other) if inside else flat(b ^ 1, s)))
    return first, second


def work(source, trans_x, trans_y, trans_z, mortar_bot, mortar_top):
    count, rows, cells = source.shape[1:]
    width = mortar_bot.shape[3]
    subs = lax.axis_size("sub")
    blocks = lax.axis_size("block")
    assert subs % 2 == 0 and blocks % 2 == 0 and count > HALO
    names = ("block", "sub")
    pair_one, pair_two = sub_swaps(blocks, subs)

    def trade(a, b):
        first = lax.ppermute(a, names, pair_one)
        return first, lax.ppermute(b, names, pair_two)

    face = (rows, cells)
    kept = count * ITEMS
    slab = (SPAN, rows)

    def everyone(value):
        if subs > DIRECT:
            return [lax.psum(value, "sub")]
        parts = [value]
        for k in range(subs - 1, 0, -1):
            parts.append(lax.ppermute(value, "sub", [(i, i ^ k) for i in range(subs)]))
        return parts

    *coeffs, slabs, near_a, near_b = call(
        pack_kernel,
        [source.shape] * 4 + [(kept,) + slab] + [(EDGE,) + slab] * 2,
        (source, trans_x, trans_y, trans_z),
        copies=4,
        source=pltpu.HBM,
    )
    near = trade(near_a, near_b)
    edges = call(edge_kernel, [(EDGE,) + face] * 2, coeffs)
    edges = trade(*edges)
    fixed = (slabs, mortar_bot, mortar_top)
    third, known, share_b = call(
        first_thin,
        [(count,) + slab, (count + 2, 5) + slab, (1, width)],
        fixed + near,
        [(EDGE,) + slab] * 2,
    )
    block_one = [(b, b ^ 1) for b in range(blocks)]
    block_two = [(b, (b + 1 if b % 2 else b - 1) % blocks) for b in range(blocks)]
    other_b = lax.ppermute(share_b, "block", block_two)
    (share_a,) = call(other_share, [(1, width)], fixed[1:] + (known, third))
    other_a = lax.ppermute(share_a, "block", block_one)
    jumps = jnp.concatenate([share_a + other_a, share_b + other_b], axis=0)
    parts = everyone(jumps)
    whole, mid_a, mid_b = call(
        first_whole,
        [(count,) + face] + [(MIDDLE,) + face] * 2,
        tuple(coeffs) + edges,
        [(EDGE,) + face] * 2,
    )
    middle = trade(mid_a, mid_b)
    data, edge_a, edge_b, mortar = call(
        face_kernel,
        [(2 * count, rows)] + [(MIDDLE,) + slab] * 2 + [(1, width)],
        fixed + (known, third) + tuple(parts),
    )
    got = trade(edge_a, edge_b)
    slab_out, flux, cbot = call(
        second_thin,
        [(count,) + slab] * 2 + [(1, width)],
        fixed[:2] + (known, third, data) + got,
        [(MIDDLE,) + slab] * 2,
    )
    (ctop,) = call(top_share, [(1, width)], (mortar_top, flux))
    upper = lax.ppermute(cbot, "block", [((b + 1) % blocks, b) for b in range(blocks)])
    parts = everyone(ctop + upper)
    (whole,) = call(
        second_whole,
        [source.shape],
        tuple(coeffs) + edges + (whole,) + middle + (slab_out,),
        [(EDGE,) + face] * 2 + [(MIDDLE,) + face] * 2,
    )
    columns = width // subs
    return call(
        finish_kernel,
        [source.shape, (1, columns)],
        (whole, mortar) + tuple(parts),
        [(1, columns)],
        copies=2,
        target=pltpu.HBM,
    )


def solution(mesh):
    spec = P("block", "sub", None, None)
    return jax.shard_map(
        work,
        mesh=mesh,
        in_specs=(spec,) * 6,
        out_specs=(spec, P("block", "sub")),
        check_vma=False,
    )
```

```python
import jax
import jax.numpy as jnp
from jax import lax
from jax.experimental import pallas as pl
from jax.experimental.pallas import tpu as pltpu
from jax.sharding import PartitionSpec as P


PASSES = 3
RELAX = 0.8
KEEP = 1.0 - RELAX
MORTAR_STEP = 0.05
F32 = jnp.float32
EDGE = 6
MIDDLE = 3
WHOLE = 5
HALO = 2
SLAB = 8
SPAN = 2 * SLAB
DIRECT = 4
ITEMS = 5


def prev(v, axis):
    return pltpu.roll(v, 1, axis)


def following(v, axis):
    return pltpu.roll(v, v.shape[axis] - 1, axis)


class Layer:
    def __init__(self, trans_y, trans_z, has_bot, has_top):
        rows = lax.broadcasted_iota(jnp.int32, trans_y.shape, 0)
        self.cy = jnp.where(rows > 0, trans_y, 0.0)
        self.cz, self.zsum = along_z(trans_z, has_bot, has_top)
        self.diag = self.cy + following(self.cy, 0) + self.zsum

    def around(self, p):
        return (
            self.cy * prev(p, 0)
            + following(self.cy * p, 0)
            + self.cz * prev(p, 1)
            + following(self.cz * p, 1)
        )


def along_z(trans_z, has_bot, has_top):
    cols = lax.broadcasted_iota(jnp.int32, trans_z.shape, 1)
    first = cols == 0
    last = cols == trans_z.shape[1] - 1
    cz = jnp.where(first, 0.0, trans_z)
    ends = jnp.where(first, trans_z * has_bot, jnp.where(last, trans_z * has_top, 0.0))
    return cz, cz + following(cz, 1) + ends


class Thin:
    def __init__(self, trans_y, trans_z, z_next, has_bot, has_top):
        rows = lax.broadcasted_iota(jnp.int32, trans_y.shape, 0)
        cols = lax.broadcasted_iota(jnp.int32, trans_y.shape, 1)
        self.cy = jnp.where(cols > 0, trans_y, 0.0)
        self.cz = jnp.where(rows == SLAB, 0.0, trans_z)
        top = jnp.where(rows == SLAB - 1, trans_z * has_top, 0.0)
        self.face = jnp.where(rows == SLAB, trans_z * has_bot, top)
        after = jnp.where(rows == SLAB - 1, 0.0, z_next)
        self.diag = self.cy + following(self.cy, 1) + self.cz + after + self.face

    def around(self, p):
        return (
            self.cy * prev(p, 1)
            + following(self.cy * p, 1)
            + self.cz * prev(p, 0)
            + following(self.cz * p, 0)
        )


def flags():
    block = lax.axis_index("block")
    sub = lax.axis_index("sub")
    has_bot = (block > 0).astype(F32)
    has_top = (block < lax.axis_size("block") - 1).astype(F32)
    has_below = (sub > 0).astype(F32)
    has_above = (sub < lax.axis_size("sub") - 1).astype(F32)
    return has_bot, has_top, has_below, has_above


def by_parity(axis, first, second, upward, downward):
    even = lax.rem(lax.axis_index(axis), 2) == 0

    @pl.when(even)
    def _():
        upward(first)
        downward(second)

    @pl.when(jnp.logical_not(even))
    def _():
        upward(second)
        downward(first)


def sort_pair(pair, above, below):
    def take_above(ref):
        above[...] = ref[...]

    def take_below(ref):
        below[...] = ref[...]

    by_parity("sub", *pair, take_above, take_below)


def pack_kernel(src, tx, ty, tz, src_v, tx_v, ty_v, tz_v, slabs, out_a, out_b, sems):
    count, rows, cells = src_v.shape[1:]
    copies = [
        pltpu.make_async_copy(here, there, sems.at[i])
        for i, (here, there) in enumerate(
            ((tz, tz_v), (tx, tx_v), (src, src_v), (ty, ty_v))
        )
    ]
    for copy in copies:
        copy.start()
    for copy in copies:
        copy.wait()
    has_bot, has_top, has_below, _ = flags()
    slot = lax.broadcasted_iota(jnp.int32, (rows, cells), 1) // SPAN
    each = cells // SPAN
    packed, done = jnp.zeros((rows, cells), F32), 0

    def flush(packed, done):
        turned = packed.T
        start = (done - 1) // each * each
        for k in range(start, done):
            slabs[k] = turned[(k - start) * SPAN : (k - start + 1) * SPAN]

    for x in range(count):
        for which, ref in enumerate((tx_v, src_v, ty_v, tz_v, tz_v)):
            j = done % each
            ahead = which // 4
            turned = pltpu.roll(ref[0, x], (SPAN * j + SLAB - ahead) % cells, 1)
            packed = jnp.where(slot == j, turned, packed)
            done += 1
            if done % each == 0 or done == count * ITEMS:
                flush(packed, done)

    def item(which, x):
        return slabs[x * ITEMS + which]

    def make(x):
        return Thin(item(2, x), item(3, x), item(4, x), has_bot, has_top)

    p_low, q_low, w_low = edge_parts(item, make, has_below)
    top = count - 1
    p_top = RELAX * item(1, top - 1) / (make(top - 1).diag + item(0, top - 1) + item(0, top))

    def upward(ref):
        values = (item(0, top), p_top, item(1, top), make(top).diag, item(2, top), item(3, top))
        for i, v in enumerate(values):
            ref[i] = v

    def downward(ref):
        values = (item(0, 0), p_low, q_low, w_low, item(2, 0), item(3, 0))
        for i, v in enumerate(values):
            ref[i] = v

    by_parity("sub", out_a, out_b, upward, downward)


def edge_parts(items, make, has_below):
    tx, src = (lambda x: items(0, x)), (lambda x: items(1, x))
    low = make(0)
    w_low = RELAX / (low.diag + tx(0) * has_below + tx(1))
    p_low = w_low * src(0)
    p_next = RELAX * src(1) / (make(1).diag + tx(1) + tx(2))
    q_low = KEEP * p_low + w_low * (src(0) + tx(1) * p_next + low.around(p_low))
    return p_low, q_low, w_low


def first_three(count, source, cx, layers, w, above, below):
    p1 = {x: w[x] * source[x] for x in range(-1, count)}
    p1[-2] = below[1]
    p1[count] = above[1]
    p2 = thin_pass(p1, source, cx, layers, w, -1, count)
    p2[count] = above[2] + above[3] * cx[count] * p1[count - 1]
    return thin_pass(p2, source, cx, layers, w, 0, count)


def thin_setup(slabs, above, below):
    count = slabs.shape[0] // ITEMS
    has_bot, has_top, has_below, has_above = flags()
    cx = {x: slabs[x * ITEMS] for x in range(1, count)}
    cx[-1] = below[0]
    cx[0] = slabs[0] * has_below
    cx[count] = above[0] * has_above
    source = {x: slabs[x * ITEMS + 1] for x in range(count)}
    source[-1] = below[2]
    layers = {
        x: Thin(*(slabs[x * ITEMS + i] for i in (2, 3, 4)), has_bot, has_top)
        for x in range(count)
    }
    layers[-1] = Thin(below[4], below[5], below[3], has_bot, has_top)
    layers[-1].diag = below[3]
    layers[count] = Thin(above[4], above[5], above[3], has_bot, has_top)
    w = {x: RELAX / (layers[x].diag + cx[x] + cx[x + 1]) for x in range(-1, count)}
    w[count] = above[3]
    return source, cx, layers, w


def thin_pass(p, rhs, cx, layers, weight, low, high):
    return {
        x: KEEP * p[x]
        + weight[x] * (rhs[x] + cx[x] * p[x - 1] + cx[x + 1] * p[x + 1] + layers[x].around(p[x]))
        for x in range(low, high)
    }


def edge_data(ref, p, x, beyond, link, rhs, cx, layers, weight):
    ref[0] = p[x]
    ref[1] = KEEP * p[x] + weight[x] * (rhs[x] + link * p[beyond] + layers[x].around(p[x]))
    step = thin_pass(p, rhs, cx, layers, weight, beyond, beyond + 1)
    ref[2] = rhs[x] + link * step[beyond]


def three_passes(p, above, below, rhs, cx, layers, weight, count):
    sides = ((count, count - 1, cx[count], above), (-1, 0, cx[0], below))
    for x, _, _, got in sides:
        p[x] = got[0]
    after = thin_pass(p, rhs, cx, layers, weight, 0, count)
    for x, near, link, got in sides:
        after[x] = got[1] + weight[x] * link * p[near]
    last = thin_pass(after, rhs, cx, layers, weight, 0, count)
    for x, near, link, got in sides:
        last[x] = KEEP * after[x] + weight[x] * (
            got[2] + link * after[near] + layers[x].around(after[x])
        )
    return thin_pass(last, rhs, cx, layers, weight, 0, count)


def trace(flux, plane, basis):
    rows, width = basis.shape[2:]
    total = 0.0
    for x, f in enumerate(flux):
        turned = jnp.broadcast_to(f[plane : plane + 1], (rows, rows)).T
        total += jnp.concatenate([turned] * (width // rows), axis=1) * basis[0, x]
    return jnp.sum(total, axis=0, keepdims=True)


def share_of(flux, bot, top, first, second):
    def to_above(ref):
        if ref is not None:
            ref[...] = trace(flux, SLAB - 1, top)

    def to_below(ref):
        if ref is not None:
            ref[...] = trace(flux, SLAB, bot)

    by_parity("block", first, second, to_above, to_below)


def first_thin(slabs, bot, top, got_a, got_b, p_out, kept, share, above, below):
    count = bot.shape[1]
    sort_pair((got_a, got_b), above, below)
    source, cx, layers, w = thin_setup(slabs, above, below)
    p = first_three(count, source, cx, layers, w, above, below)
    for x in range(count):
        p_out[x] = p[x]
    share_of([layers[x].face * p[x] for x in range(count)], bot, top, None, share)
    for x in range(-1, count + 1):
        for i, v in enumerate((cx[x], w[x], layers[x].cy, layers[x].cz, layers[x].face)):
            kept[x + 1, i] = v


def other_share(bot, top, kept, p_in, share):
    flux = [kept[x + 1, 4] * p_in[x] for x in range(bot.shape[1])]
    share_of(flux, bot, top, share, None)


class Kept(Thin):
    def __init__(self, kept, x):
        self.cy, self.cz, self.face = (kept[x + 1, i] for i in (2, 3, 4))


def thin_again(slabs, kept):
    count = slabs.shape[0] // ITEMS
    span = range(-1, count + 1)
    cx = {x: kept[x + 1, 0] for x in span}
    w = {x: kept[x + 1, 1] for x in span}
    layers = {x: Kept(kept, x) for x in span}
    return {x: slabs[x * ITEMS + 1] for x in range(count)}, cx, layers, w


def with_faces(source, layers, data, count):
    known = {}
    for x in range(count):
        planes = lax.broadcasted_iota(jnp.int32, source[x].shape, 0)
        known[x] = jnp.where(planes == SLAB, data[x : x + 1], data[count + x : count + x + 1])
    return known, {x: source[x] + layers[x].face * known[x] for x in range(count)}


def face_kernel(slabs, bot, top, kept, p_in, *rest):
    parts = rest[:-4]
    data_out, edge_a, edge_b, mortar_out = rest[-4:]
    count = bot.shape[1]
    jumps = MORTAR_STEP * sum(part[...] for part in parts)
    even = lax.rem(lax.axis_index("block"), 2) == 0
    own = jnp.where(even, jumps[0:1], jumps[1:2])
    under = jnp.where(even, jumps[1:2], jumps[0:1])
    mortar_out[...] = own
    rows, width = bot.shape[2:]
    data = []
    for ref, values in ((bot, under), (top, own)):
        for x in range(count):
            product = ref[0, x] * values
            folded = sum(product[:, i : i + rows] for i in range(0, width, rows))
            data.append(jnp.sum(folded.T, axis=0, keepdims=True))
    data = jnp.concatenate(data, axis=0)
    data_out[...] = data
    source, cx, layers, w = thin_again(slabs, kept)
    rhs = with_faces(source, layers, data, count)[1]
    p = {x: p_in[x] for x in range(count)}
    last = count - 1
    by_parity(
        "sub",
        edge_a,
        edge_b,
        lambda ref: edge_data(ref, p, last, last - 1, cx[last], rhs, cx, layers, w),
        lambda ref: edge_data(ref, p, 0, 1, cx[1], rhs, cx, layers, w),
    )


def second_thin(
    slabs, bot, kept, p_in, data, edge_a, edge_b,
    p_out, flux_out, cbot_out, edge_above, edge_below,
):
    count = bot.shape[1]
    sort_pair((edge_a, edge_b), edge_above, edge_below)
    source, cx, layers, w = thin_again(slabs, kept)
    known, rhs = with_faces(source, layers, data, count)
    p = {x: p_in[x] for x in range(count)}
    p = three_passes(p, edge_above, edge_below, rhs, cx, layers, w, count)
    for x in range(count):
        p_out[x] = p[x]
    flux = [layers[x].face * (p[x] - known[x]) for x in range(count)]
    cbot_out[...] = trace(flux, SLAB, bot)
    for x in range(count):
        flux_out[x] = flux[x]


def top_share(top, flux, ctop_out):
    ctop_out[...] = trace([flux[x] for x in range(top.shape[1])], SLAB - 1, top)


def edge_kernel(src, tx, ty, tz, out_a, out_b):
    count = src.shape[1]
    has_bot, has_top, has_below, _ = flags()

    def make(x):
        return Layer(ty[0, x], tz[0, x], has_bot, has_top)

    p_low, q_low, w_low = edge_parts(lambda which, x: (tx, src)[which][0, x], make, has_below)
    top = count - 1
    p_top = RELAX * src[0, top - 1] / (make(top - 1).diag + tx[0, top - 1] + tx[0, top])

    def upward(ref):
        for i, v in enumerate((tx[0, top], p_top, src[0, top], ty[0, top], tz[0, top])):
            ref[i] = v

    def downward(ref):
        for i, v in enumerate((tx[0, 0], p_low, q_low, w_low)):
            ref[i] = v

    by_parity("sub", out_a, out_b, upward, downward)


def whole_setup(src, tx, ty, tz, above, below):
    count = src.shape[1]
    has_bot, has_top, has_below, has_above = flags()
    cx = {x: tx[0, x] for x in range(1, count)}
    cx[-1] = below[0]
    cx[0] = tx[0, 0] * has_below
    cx[count] = above[0] * has_above
    source = {x: src[0, x] for x in range(count)}
    source[-1] = below[2]
    layers = {x: Layer(ty[0, x], tz[0, x], has_bot, has_top) for x in range(count)}
    layers[-1] = Layer(below[3], below[4], has_bot, has_top)
    weight = {x: RELAX / (layers[x].diag + cx[x] + cx[x + 1]) for x in range(-1, count)}
    return source, cx, layers, weight


def first_whole(src, tx, ty, tz, got_a, got_b, p_out, mid_a, mid_b, above, below):
    count = src.shape[1]
    sort_pair((got_a, got_b), above, below)
    source, cx, layers, w = whole_setup(src, tx, ty, tz, above, below)
    p3 = first_three(count, source, cx, layers, w, above, below)
    for x in range(count):
        p_out[x] = p3[x]
    last = count - 1

    def downward(ref):
        edge_data(ref, p3, 0, 1, cx[1], source, cx, layers, w)
        ref[3] = ty[0, 0]
        ref[4] = tz[0, 0]

    by_parity(
        "sub",
        mid_a,
        mid_b,
        lambda ref: edge_data(ref, p3, last, last - 1, cx[last], source, cx, layers, w),
        downward,
    )


def second_whole(
    src, tx, ty, tz, got_a, got_b, p_in, mid_a, mid_b, thin,
    p_out, above, below, p_above, p_below,
):
    count, rows, cells = src.shape[1:]
    sort_pair((got_a, got_b), above, below)
    sort_pair((mid_a, mid_b), p_above, p_below)
    source, cx, layers, w = whole_setup(src, tx, ty, tz, above, below)
    has_bot, has_top, _, _ = flags()
    layers[count] = Layer(p_above[3], p_above[4], has_bot, has_top)
    w[count] = above[3]
    p3 = {x: p_in[x] for x in range(count)}
    p6 = three_passes(p3, p_above, p_below, source, cx, layers, w, count)
    cols = lax.broadcasted_iota(jnp.int32, (rows, cells), 1)
    face = (cols < PASSES) | (cols >= cells - PASSES)
    each = cells // SPAN
    for start in range(0, count, each):
        stop = min(start + each, count)
        here = [thin[x] for x in range(start, stop)]
        if (stop - start) * SPAN < cells:
            here.append(jnp.zeros((cells - (stop - start) * SPAN, rows), F32))
        back = jnp.concatenate(here, axis=0).T
        for x in range(start, stop):
            shift = (cells - (x - start) * SPAN - SLAB) % cells
            p_out[0, x] = jnp.where(face, pltpu.roll(back, shift, 1), p6[x])


def finish_kernel(merged, mortar, *rest):
    parts = rest[:-4]
    p_out, m_out, piece, sems = rest[-4:]
    whole = pltpu.make_async_copy(merged, p_out, sems.at[0])
    whole.start()
    total = mortar[...] + MORTAR_STEP * sum(part[...] for part in parts)
    columns = piece.shape[1]
    shift = total.shape[1] - lax.axis_index("sub") * columns
    piece[...] = pltpu.roll(total, lax.rem(shift, total.shape[1]), 1)[:, 0:columns]
    copy = pltpu.make_async_copy(piece, m_out, sems.at[1])
    copy.start()
    whole.wait()
    copy.wait()


def call(kernel, outs, args, scratch=(), copies=0, source=pltpu.VMEM, target=pltpu.VMEM):
    args = [pltpu.with_memory_space_constraint(a, source) for a in args]
    return pl.pallas_call(
        kernel,
        out_shape=[target(shape, F32) for shape in outs],
        in_specs=[pl.BlockSpec(memory_space=source)] * len(args),
        out_specs=[pl.BlockSpec(memory_space=target)] * len(outs),
        scratch_shapes=[pltpu.VMEM(shape, F32) for shape in scratch]
        + ([pltpu.SemaphoreType.DMA((copies,))] if copies else []),
        compiler_params=pltpu.CompilerParams(vmem_limit_bytes=16 << 20),
    )(*args)


def sub_swaps(blocks, subs):
    flat = lambda b, s: b * subs + s
    first = [(flat(b, s), flat(b, s ^ 1)) for b in range(blocks) for s in range(subs)]
    second = []
    for b in range(blocks):
        for s in range(subs):
            other = s + 1 if s % 2 else s - 1
            inside = 0 <= other < subs
            second.append((flat(b, s), flat(b, other) if inside else flat(b ^ 1, s)))
    return first, second


def work(source, trans_x, trans_y, trans_z, mortar_bot, mortar_top):
    count, rows, cells = source.shape[1:]
    width = mortar_bot.shape[3]
    subs = lax.axis_size("sub")
    blocks = lax.axis_size("block")
    assert subs % 2 == 0 and blocks % 2 == 0 and count > HALO
    names = ("block", "sub")
    pair_one, pair_two = sub_swaps(blocks, subs)

    def trade(a, b):
        first = lax.ppermute(a, names, pair_one)
        return first, lax.ppermute(b, names, pair_two)

    face = (rows, cells)
    kept = count * ITEMS
    slab = (SPAN, rows)

    def everyone(value):
        if subs > DIRECT:
            return [lax.psum(value, "sub")]
        parts = [value]
        for k in range(subs - 1, 0, -1):
            parts.append(lax.ppermute(value, "sub", [(i, i ^ k) for i in range(subs)]))
        return parts

    *coeffs, slabs, near_a, near_b = call(
        pack_kernel,
        [source.shape] * 4 + [(kept,) + slab] + [(EDGE,) + slab] * 2,
        (source, trans_x, trans_y, trans_z),
        copies=4,
        source=pltpu.HBM,
    )
    near = trade(near_a, near_b)
    edges = call(edge_kernel, [(WHOLE,) + face] * 2, coeffs)
    edges = trade(*edges)
    fixed = (slabs, mortar_bot, mortar_top)
    third, known, share_b = call(
        first_thin,
        [(count,) + slab, (count + 2, 5) + slab, (1, width)],
        fixed + near,
        [(EDGE,) + slab] * 2,
    )
    block_one = [(b, b ^ 1) for b in range(blocks)]
    block_two = [(b, (b + 1 if b % 2 else b - 1) % blocks) for b in range(blocks)]
    other_b = lax.ppermute(share_b, "block", block_two)
    (share_a,) = call(other_share, [(1, width)], fixed[1:] + (known, third))
    other_a = lax.ppermute(share_a, "block", block_one)
    jumps = jnp.concatenate([share_a + other_a, share_b + other_b], axis=0)
    parts = everyone(jumps)
    whole, mid_a, mid_b = call(
        first_whole,
        [(count,) + face] + [(WHOLE,) + face] * 2,
        tuple(coeffs) + edges,
        [(WHOLE,) + face] * 2,
    )
    middle = trade(mid_a, mid_b)
    data, edge_a, edge_b, mortar = call(
        face_kernel,
        [(2 * count, rows)] + [(MIDDLE,) + slab] * 2 + [(1, width)],
        fixed + (known, third) + tuple(parts),
    )
    got = trade(edge_a, edge_b)
    slab_out, flux, cbot = call(
        second_thin,
        [(count,) + slab] * 2 + [(1, width)],
        fixed[:2] + (known, third, data) + got,
        [(MIDDLE,) + slab] * 2,
    )
    (ctop,) = call(top_share, [(1, width)], (mortar_top, flux))
    upper = lax.ppermute(cbot, "block", [((b + 1) % blocks, b) for b in range(blocks)])
    parts = everyone(ctop + upper)
    (whole,) = call(
        second_whole,
        [source.shape],
        tuple(coeffs) + edges + (whole,) + middle + (slab_out,),
        [(WHOLE,) + face] * 4,
    )
    columns = width // subs
    return call(
        finish_kernel,
        [source.shape, (1, columns)],
        (whole, mortar) + tuple(parts),
        [(1, columns)],
        copies=2,
        target=pltpu.HBM,
    )


def solution(mesh):
    spec = P("block", "sub", None, None)
    return jax.shard_map(
        work,
        mesh=mesh,
        in_specs=(spec,) * 6,
        out_specs=(spec, P("block", "sub")),
        check_vma=False,
    )
```

```python
import jax
import jax.numpy as jnp
from jax import lax
from jax.experimental import pallas as pl
from jax.experimental.pallas import tpu as pltpu
from jax.sharding import PartitionSpec as P


PASSES = 3
RELAX = 0.8
KEEP = 1.0 - RELAX
MORTAR_STEP = 0.05
F32 = jnp.float32
EDGE = 6
MIDDLE = 3
WHOLE = 5
HALO = 2
SLAB = 8
SPAN = 2 * SLAB
DIRECT = 4
ITEMS = 5


def prev(v, axis):
    return pltpu.roll(v, 1, axis)


def following(v, axis):
    return pltpu.roll(v, v.shape[axis] - 1, axis)


class Layer:
    def __init__(self, trans_y, trans_z, has_bot, has_top):
        rows = lax.broadcasted_iota(jnp.int32, trans_y.shape, 0)
        self.cy = jnp.where(rows > 0, trans_y, 0.0)
        self.cz, self.zsum = along_z(trans_z, has_bot, has_top)
        self.diag = self.cy + following(self.cy, 0) + self.zsum

    def around(self, p):
        return (
            self.cy * prev(p, 0)
            + following(self.cy * p, 0)
            + self.cz * prev(p, 1)
            + following(self.cz * p, 1)
        )


def along_z(trans_z, has_bot, has_top):
    cols = lax.broadcasted_iota(jnp.int32, trans_z.shape, 1)
    first = cols == 0
    last = cols == trans_z.shape[1] - 1
    cz = jnp.where(first, 0.0, trans_z)
    ends = jnp.where(first, trans_z * has_bot, jnp.where(last, trans_z * has_top, 0.0))
    return cz, cz + following(cz, 1) + ends


class Thin:
    def __init__(self, trans_y, trans_z, z_next, has_bot, has_top):
        rows = lax.broadcasted_iota(jnp.int32, trans_y.shape, 0)
        cols = lax.broadcasted_iota(jnp.int32, trans_y.shape, 1)
        self.cy = jnp.where(cols > 0, trans_y, 0.0)
        self.cz = jnp.where(rows == SLAB, 0.0, trans_z)
        top = jnp.where(rows == SLAB - 1, trans_z * has_top, 0.0)
        self.face = jnp.where(rows == SLAB, trans_z * has_bot, top)
        after = jnp.where(rows == SLAB - 1, 0.0, z_next)
        self.diag = self.cy + following(self.cy, 1) + self.cz + after + self.face

    def around(self, p):
        return (
            self.cy * prev(p, 1)
            + following(self.cy * p, 1)
            + self.cz * prev(p, 0)
            + following(self.cz * p, 0)
        )


def flags():
    block = lax.axis_index("block")
    sub = lax.axis_index("sub")
    has_bot = (block > 0).astype(F32)
    has_top = (block < lax.axis_size("block") - 1).astype(F32)
    has_below = (sub > 0).astype(F32)
    has_above = (sub < lax.axis_size("sub") - 1).astype(F32)
    return has_bot, has_top, has_below, has_above


def by_parity(axis, first, second, upward, downward):
    even = lax.rem(lax.axis_index(axis), 2) == 0

    @pl.when(even)
    def _():
        upward(first)
        downward(second)

    @pl.when(jnp.logical_not(even))
    def _():
        upward(second)
        downward(first)


def sort_pair(pair, above, below):
    def take_above(ref):
        above[...] = ref[...]

    def take_below(ref):
        below[...] = ref[...]

    by_parity("sub", *pair, take_above, take_below)


def pack_kernel(src, tx, ty, tz, src_v, tx_v, ty_v, tz_v, slabs, out_a, out_b, sems):
    count, rows, cells = src_v.shape[1:]
    copies = [
        pltpu.make_async_copy(here, there, sems.at[i])
        for i, (here, there) in enumerate(
            ((tx, tx_v), (src, src_v), (ty, ty_v), (tz, tz_v))
        )
    ]
    for copy in copies:
        copy.start()
    has_bot, has_top, has_below, _ = flags()
    slot = lax.broadcasted_iota(jnp.int32, (rows, cells), 1) // SPAN
    each = cells // SPAN
    packed, done = jnp.zeros((rows, cells), F32), 0

    def flush(packed, done):
        turned = packed.T
        start = (done - 1) // each * each
        for k in range(start, done):
            slabs[k] = turned[(k - start) * SPAN : (k - start + 1) * SPAN]

    for which, ref in enumerate((tx_v, src_v, ty_v, tz_v, tz_v)):
        ahead = which // 4
        if not ahead:
            copies[which].wait()
        for x in range(count):
            j = done % each
            turned = pltpu.roll(ref[0, x], (SPAN * j + SLAB - ahead) % cells, 1)
            packed = jnp.where(slot == j, turned, packed)
            done += 1
            if done % each == 0 or done == count * ITEMS:
                flush(packed, done)

    def item(which, x):
        return slabs[which * count + x]

    def make(x):
        return Thin(item(2, x), item(3, x), item(4, x), has_bot, has_top)

    p_low, q_low, w_low = edge_parts(item, make, has_below)
    top = count - 1
    p_top = RELAX * item(1, top - 1) / (make(top - 1).diag + item(0, top - 1) + item(0, top))

    def upward(ref):
        values = (item(0, top), p_top, item(1, top), make(top).diag, item(2, top), item(3, top))
        for i, v in enumerate(values):
            ref[i] = v

    def downward(ref):
        values = (item(0, 0), p_low, q_low, w_low, item(2, 0), item(3, 0))
        for i, v in enumerate(values):
            ref[i] = v

    by_parity("sub", out_a, out_b, upward, downward)


def edge_parts(items, make, has_below):
    tx, src = (lambda x: items(0, x)), (lambda x: items(1, x))
    low = make(0)
    w_low = RELAX / (low.diag + tx(0) * has_below + tx(1))
    p_low = w_low * src(0)
    p_next = RELAX * src(1) / (make(1).diag + tx(1) + tx(2))
    q_low = KEEP * p_low + w_low * (src(0) + tx(1) * p_next + low.around(p_low))
    return p_low, q_low, w_low


def first_three(count, source, cx, layers, w, above, below):
    p1 = {x: w[x] * source[x] for x in range(-1, count)}
    p1[-2] = below[1]
    p1[count] = above[1]
    p2 = thin_pass(p1, source, cx, layers, w, -1, count)
    p2[count] = above[2] + above[3] * cx[count] * p1[count - 1]
    return thin_pass(p2, source, cx, layers, w, 0, count)


def thin_setup(slabs, above, below):
    count = slabs.shape[0] // ITEMS
    has_bot, has_top, has_below, has_above = flags()
    cx = {x: slabs[x] for x in range(1, count)}
    cx[-1] = below[0]
    cx[0] = slabs[0] * has_below
    cx[count] = above[0] * has_above
    source = {x: slabs[count + x] for x in range(count)}
    source[-1] = below[2]
    layers = {
        x: Thin(*(slabs[i * count + x] for i in (2, 3, 4)), has_bot, has_top)
        for x in range(count)
    }
    layers[-1] = Thin(below[4], below[5], below[3], has_bot, has_top)
    layers[-1].diag = below[3]
    layers[count] = Thin(above[4], above[5], above[3], has_bot, has_top)
    w = {x: RELAX / (layers[x].diag + cx[x] + cx[x + 1]) for x in range(-1, count)}
    w[count] = above[3]
    return source, cx, layers, w


def thin_pass(p, rhs, cx, layers, weight, low, high):
    return {
        x: KEEP * p[x]
        + weight[x] * (rhs[x] + cx[x] * p[x - 1] + cx[x + 1] * p[x + 1] + layers[x].around(p[x]))
        for x in range(low, high)
    }


def edge_data(ref, p, x, beyond, link, rhs, cx, layers, weight):
    ref[0] = p[x]
    ref[1] = KEEP * p[x] + weight[x] * (rhs[x] + link * p[beyond] + layers[x].around(p[x]))
    step = thin_pass(p, rhs, cx, layers, weight, beyond, beyond + 1)
    ref[2] = rhs[x] + link * step[beyond]


def three_passes(p, above, below, rhs, cx, layers, weight, count):
    sides = ((count, count - 1, cx[count], above), (-1, 0, cx[0], below))
    for x, _, _, got in sides:
        p[x] = got[0]
    after = thin_pass(p, rhs, cx, layers, weight, 0, count)
    for x, near, link, got in sides:
        after[x] = got[1] + weight[x] * link * p[near]
    last = thin_pass(after, rhs, cx, layers, weight, 0, count)
    for x, near, link, got in sides:
        last[x] = KEEP * after[x] + weight[x] * (
            got[2] + link * after[near] + layers[x].around(after[x])
        )
    return thin_pass(last, rhs, cx, layers, weight, 0, count)


def trace(flux, plane, basis):
    rows, width = basis.shape[2:]
    total = 0.0
    for x, f in enumerate(flux):
        turned = jnp.broadcast_to(f[plane : plane + 1], (rows, rows)).T
        total += jnp.concatenate([turned] * (width // rows), axis=1) * basis[0, x]
    return jnp.sum(total, axis=0, keepdims=True)


def share_of(flux, bot, top, first, second):
    def to_above(ref):
        if ref is not None:
            ref[...] = trace(flux, SLAB - 1, top)

    def to_below(ref):
        if ref is not None:
            ref[...] = trace(flux, SLAB, bot)

    by_parity("block", first, second, to_above, to_below)


def first_thin(slabs, bot, top, got_a, got_b, p_out, kept, share, above, below):
    count = bot.shape[1]
    sort_pair((got_a, got_b), above, below)
    source, cx, layers, w = thin_setup(slabs, above, below)
    p = first_three(count, source, cx, layers, w, above, below)
    for x in range(count):
        p_out[x] = p[x]
    share_of([layers[x].face * p[x] for x in range(count)], bot, top, None, share)
    for x in range(-1, count + 1):
        for i, v in enumerate((cx[x], w[x], layers[x].cy, layers[x].cz, layers[x].face)):
            kept[x + 1, i] = v


def other_share(bot, top, kept, p_in, share):
    flux = [kept[x + 1, 4] * p_in[x] for x in range(bot.shape[1])]
    share_of(flux, bot, top, share, None)


class Kept(Thin):
    def __init__(self, kept, x):
        self.cy, self.cz, self.face = (kept[x + 1, i] for i in (2, 3, 4))


def thin_again(slabs, kept):
    count = slabs.shape[0] // ITEMS
    span = range(-1, count + 1)
    cx = {x: kept[x + 1, 0] for x in span}
    w = {x: kept[x + 1, 1] for x in span}
    layers = {x: Kept(kept, x) for x in span}
    return {x: slabs[count + x] for x in range(count)}, cx, layers, w


def with_faces(source, layers, data, count):
    known = {}
    for x in range(count):
        planes = lax.broadcasted_iota(jnp.int32, source[x].shape, 0)
        known[x] = jnp.where(planes == SLAB, data[x : x + 1], data[count + x : count + x + 1])
    return known, {x: source[x] + layers[x].face * known[x] for x in range(count)}


def face_kernel(slabs, bot, top, kept, p_in, *rest):
    parts = rest[:-4]
    data_out, edge_a, edge_b, mortar_out = rest[-4:]
    count = bot.shape[1]
    jumps = MORTAR_STEP * sum(part[...] for part in parts)
    even = lax.rem(lax.axis_index("block"), 2) == 0
    own = jnp.where(even, jumps[0:1], jumps[1:2])
    under = jnp.where(even, jumps[1:2], jumps[0:1])
    mortar_out[...] = own
    rows, width = bot.shape[2:]
    data = []
    for ref, values in ((bot, under), (top, own)):
        for x in range(count):
            product = ref[0, x] * values
            folded = sum(product[:, i : i + rows] for i in range(0, width, rows))
            data.append(jnp.sum(folded.T, axis=0, keepdims=True))
    data = jnp.concatenate(data, axis=0)
    data_out[...] = data
    source, cx, layers, w = thin_again(slabs, kept)
    rhs = with_faces(source, layers, data, count)[1]
    p = {x: p_in[x] for x in range(count)}
    last = count - 1
    by_parity(
        "sub",
        edge_a,
        edge_b,
        lambda ref: edge_data(ref, p, last, last - 1, cx[last], rhs, cx, layers, w),
        lambda ref: edge_data(ref, p, 0, 1, cx[1], rhs, cx, layers, w),
    )


def second_thin(
    slabs, bot, kept, p_in, data, edge_a, edge_b,
    p_out, flux_out, cbot_out, edge_above, edge_below,
):
    count = bot.shape[1]
    sort_pair((edge_a, edge_b), edge_above, edge_below)
    source, cx, layers, w = thin_again(slabs, kept)
    known, rhs = with_faces(source, layers, data, count)
    p = {x: p_in[x] for x in range(count)}
    p = three_passes(p, edge_above, edge_below, rhs, cx, layers, w, count)
    for x in range(count):
        p_out[x] = p[x]
    flux = [layers[x].face * (p[x] - known[x]) for x in range(count)]
    cbot_out[...] = trace(flux, SLAB, bot)
    for x in range(count):
        flux_out[x] = flux[x]


def top_share(top, flux, ctop_out):
    ctop_out[...] = trace([flux[x] for x in range(top.shape[1])], SLAB - 1, top)


def edge_kernel(src, tx, ty, tz, out_a, out_b):
    count = src.shape[1]
    has_bot, has_top, has_below, _ = flags()

    def make(x):
        return Layer(ty[0, x], tz[0, x], has_bot, has_top)

    p_low, q_low, w_low = edge_parts(lambda which, x: (tx, src)[which][0, x], make, has_below)
    top = count - 1
    p_top = RELAX * src[0, top - 1] / (make(top - 1).diag + tx[0, top - 1] + tx[0, top])

    def upward(ref):
        for i, v in enumerate((tx[0, top], p_top, src[0, top], ty[0, top], tz[0, top])):
            ref[i] = v

    def downward(ref):
        for i, v in enumerate((tx[0, 0], p_low, q_low, w_low)):
            ref[i] = v

    by_parity("sub", out_a, out_b, upward, downward)


def whole_setup(src, tx, ty, tz, above, below):
    count = src.shape[1]
    has_bot, has_top, has_below, has_above = flags()
    cx = {x: tx[0, x] for x in range(1, count)}
    cx[-1] = below[0]
    cx[0] = tx[0, 0] * has_below
    cx[count] = above[0] * has_above
    source = {x: src[0, x] for x in range(count)}
    source[-1] = below[2]
    layers = {x: Layer(ty[0, x], tz[0, x], has_bot, has_top) for x in range(count)}
    layers[-1] = Layer(below[3], below[4], has_bot, has_top)
    weight = {x: RELAX / (layers[x].diag + cx[x] + cx[x + 1]) for x in range(-1, count)}
    return source, cx, layers, weight


def first_whole(src, tx, ty, tz, got_a, got_b, p_out, mid_a, mid_b, above, below):
    count = src.shape[1]
    sort_pair((got_a, got_b), above, below)
    source, cx, layers, w = whole_setup(src, tx, ty, tz, above, below)
    p3 = first_three(count, source, cx, layers, w, above, below)
    for x in range(count):
        p_out[x] = p3[x]
    last = count - 1

    def downward(ref):
        edge_data(ref, p3, 0, 1, cx[1], source, cx, layers, w)
        ref[3] = ty[0, 0]
        ref[4] = tz[0, 0]

    by_parity(
        "sub",
        mid_a,
        mid_b,
        lambda ref: edge_data(ref, p3, last, last - 1, cx[last], source, cx, layers, w),
        downward,
    )


def second_whole(
    src, tx, ty, tz, got_a, got_b, p_in, mid_a, mid_b, thin,
    p_out, above, below, p_above, p_below,
):
    count, rows, cells = src.shape[1:]
    sort_pair((got_a, got_b), above, below)
    sort_pair((mid_a, mid_b), p_above, p_below)
    source, cx, layers, w = whole_setup(src, tx, ty, tz, above, below)
    has_bot, has_top, _, _ = flags()
    layers[count] = Layer(p_above[3], p_above[4], has_bot, has_top)
    w[count] = above[3]
    p3 = {x: p_in[x] for x in range(count)}
    p6 = three_passes(p3, p_above, p_below, source, cx, layers, w, count)
    cols = lax.broadcasted_iota(jnp.int32, (rows, cells), 1)
    face = (cols < PASSES) | (cols >= cells - PASSES)
    each = cells // SPAN
    for start in range(0, count, each):
        stop = min(start + each, count)
        here = [thin[x] for x in range(start, stop)]
        if (stop - start) * SPAN < cells:
            here.append(jnp.zeros((cells - (stop - start) * SPAN, rows), F32))
        back = jnp.concatenate(here, axis=0).T
        for x in range(start, stop):
            shift = (cells - (x - start) * SPAN - SLAB) % cells
            p_out[0, x] = jnp.where(face, pltpu.roll(back, shift, 1), p6[x])


def finish_kernel(merged, mortar, *rest):
    parts = rest[:-4]
    p_out, m_out, piece, sems = rest[-4:]
    whole = pltpu.make_async_copy(merged, p_out, sems.at[0])
    whole.start()
    total = mortar[...] + MORTAR_STEP * sum(part[...] for part in parts)
    columns = piece.shape[1]
    shift = total.shape[1] - lax.axis_index("sub") * columns
    piece[...] = pltpu.roll(total, lax.rem(shift, total.shape[1]), 1)[:, 0:columns]
    copy = pltpu.make_async_copy(piece, m_out, sems.at[1])
    copy.start()
    whole.wait()
    copy.wait()


def call(kernel, outs, args, scratch=(), copies=0, source=pltpu.VMEM, target=pltpu.VMEM):
    args = [pltpu.with_memory_space_constraint(a, source) for a in args]
    return pl.pallas_call(
        kernel,
        out_shape=[target(shape, F32) for shape in outs],
        in_specs=[pl.BlockSpec(memory_space=source)] * len(args),
        out_specs=[pl.BlockSpec(memory_space=target)] * len(outs),
        scratch_shapes=[pltpu.VMEM(shape, F32) for shape in scratch]
        + ([pltpu.SemaphoreType.DMA((copies,))] if copies else []),
        compiler_params=pltpu.CompilerParams(vmem_limit_bytes=16 << 20),
    )(*args)


def sub_swaps(blocks, subs):
    flat = lambda b, s: b * subs + s
    first = [(flat(b, s), flat(b, s ^ 1)) for b in range(blocks) for s in range(subs)]
    second = []
    for b in range(blocks):
        for s in range(subs):
            other = s + 1 if s % 2 else s - 1
            inside = 0 <= other < subs
            second.append((flat(b, s), flat(b, other) if inside else flat(b ^ 1, s)))
    return first, second


def work(source, trans_x, trans_y, trans_z, mortar_bot, mortar_top):
    count, rows, cells = source.shape[1:]
    width = mortar_bot.shape[3]
    subs = lax.axis_size("sub")
    blocks = lax.axis_size("block")
    assert subs % 2 == 0 and blocks % 2 == 0 and count > HALO
    names = ("block", "sub")
    pair_one, pair_two = sub_swaps(blocks, subs)

    def trade(a, b):
        first = lax.ppermute(a, names, pair_one)
        return first, lax.ppermute(b, names, pair_two)

    face = (rows, cells)
    kept = count * ITEMS
    slab = (SPAN, rows)

    def everyone(value):
        if subs > DIRECT:
            return [lax.psum(value, "sub")]
        parts = [value]
        for k in range(subs - 1, 0, -1):
            parts.append(lax.ppermute(value, "sub", [(i, i ^ k) for i in range(subs)]))
        return parts

    *coeffs, slabs, near_a, near_b = call(
        pack_kernel,
        [source.shape] * 4 + [(kept,) + slab] + [(EDGE,) + slab] * 2,
        (source, trans_x, trans_y, trans_z),
        copies=4,
        source=pltpu.HBM,
    )
    near = trade(near_a, near_b)
    edges = call(edge_kernel, [(WHOLE,) + face] * 2, coeffs)
    edges = trade(*edges)
    fixed = (slabs, mortar_bot, mortar_top)
    third, known, share_b = call(
        first_thin,
        [(count,) + slab, (count + 2, 5) + slab, (1, width)],
        fixed + near,
        [(EDGE,) + slab] * 2,
    )
    block_one = [(b, b ^ 1) for b in range(blocks)]
    block_two = [(b, (b + 1 if b % 2 else b - 1) % blocks) for b in range(blocks)]
    other_b = lax.ppermute(share_b, "block", block_two)
    (share_a,) = call(other_share, [(1, width)], fixed[1:] + (known, third))
    other_a = lax.ppermute(share_a, "block", block_one)
    jumps = jnp.concatenate([share_a + other_a, share_b + other_b], axis=0)
    parts = everyone(jumps)
    whole, mid_a, mid_b = call(
        first_whole,
        [(count,) + face] + [(WHOLE,) + face] * 2,
        tuple(coeffs) + edges,
        [(WHOLE,) + face] * 2,
    )
    middle = trade(mid_a, mid_b)
    data, edge_a, edge_b, mortar = call(
        face_kernel,
        [(2 * count, rows)] + [(MIDDLE,) + slab] * 2 + [(1, width)],
        fixed + (known, third) + tuple(parts),
    )
    got = trade(edge_a, edge_b)
    slab_out, flux, cbot = call(
        second_thin,
        [(count,) + slab] * 2 + [(1, width)],
        fixed[:2] + (known, third, data) + got,
        [(MIDDLE,) + slab] * 2,
    )
    (ctop,) = call(top_share, [(1, width)], (mortar_top, flux))
    upper = lax.ppermute(cbot, "block", [((b + 1) % blocks, b) for b in range(blocks)])
    parts = everyone(ctop + upper)
    (whole,) = call(
        second_whole,
        [source.shape],
        tuple(coeffs) + edges + (whole,) + middle + (slab_out,),
        [(WHOLE,) + face] * 4,
    )
    columns = width // subs
    return call(
        finish_kernel,
        [source.shape, (1, columns)],
        (whole, mortar) + tuple(parts),
        [(1, columns)],
        copies=2,
        target=pltpu.HBM,
    )


def solution(mesh):
    spec = P("block", "sub", None, None)
    return jax.shard_map(
        work,
        mesh=mesh,
        in_specs=(spec,) * 6,
        out_specs=(spec, P("block", "sub")),
        check_vma=False,
    )
```
